32 devices in a mesh: dp: 8 (over y, x, core), tensor: 4 (over z).
Axes of the slice: x: 2, y: 2, z: 4, core: 2. Of those that a mesh axis runs over, the one named last changes fastest.
Arguments:
- tokens: bfloat16 [2, 8192, 768], P(None, ('dp', 'tensor')), may hold values from -6 to 6
- cotangent: bfloat16 [2, 8192, 768], P(None, ('dp', 'tensor')), may hold values from -6 to 6
- lengths: int32 [2, 8, 4], P(None, 'dp'), may hold values from 1 to 900, 1024 in all within a row
- padding: int32 [2, 8192], P(None, 'dp'), may hold values 0 or 1
- ln_gain: bfloat16 [1, 2, 768], P(None, None, 'dp'), may hold values from 0.5 to 1.5
- w_qkv: bfloat16 [1, 768, 3, 768], P(None, 'dp', None, 'tensor'), may hold values from -0.3125 to 0.3125
- w_out: bfloat16 [1, 768, 768], P(None, 'tensor', 'dp'), may hold values from -0.875 to 0.875
- w_up: bfloat16 [1, 768, 3072], P(None, 'dp', 'tensor'), may hold values from -0.21875 to 0.21875
- w_down: bfloat16 [1, 3072, 768], P(None, 'tensor', 'dp'), may hold values from -0.109375 to 0.109375
Outputs:
- layer_out: float32 [2, 8192, 768], P(None, ('dp', 'tensor'))
- input_grad: float32 [2, 8192, 768], P(None, ('dp', 'tensor'))
- gain_grad: float32 [1536], P(('dp', 'tensor'))
- qkv_grad: float32 [1, 768, 3, 768], P(None, 'dp', None, 'tensor')
- out_grad: float32 [1, 768, 768], P(None, 'tensor', 'dp')
- up_grad: float32 [1, 768, 3072], P(None, 'dp', 'tensor')
- down_grad: float32 [1, 3072, 768], P(None, 'tensor', 'dp')
The draws below stay inside these ranges and needn't reach their ends.
Inputs may be any that keep to these rules, and one draw needn't show every extreme that they name: In every block the 4 image lengths sum to 1024, and one image has exactly 900 tokens.
All inputs are finite; a program needn't handle non-finite values. No bound on the sum of `padding` on one device may be relied on, other than what follows from the above.
Results may differ from the reference program's by a relative error of at most 0.012.
The reference program's roundings to bfloat16 on the way count: a program that leaves them out, or rounds other values in their place, can miss the bound.
Values may be sent and summed in bfloat16 or wider, within the bound.
A program may use at most 128 MiB of HBM per device.

```python
import math
import jax
import jax.numpy as jnp
import numpy as np
from jax import lax

D = 768
HEADS = 12
HD = 64
FF = 3072
LAYERS = 1
MB = 2
BLK = 1024
MOST = 900
NIMG = 4
MB_TOKENS = 8192
N_DP = 8


def set_ends(values, stream_key, smallest, top_value):
    extent = values.shape
    place = [jax.random.randint(jax.random.fold_in(stream_key, axis), (), 0, extent[axis]) for axis in range(len(extent))]
    values = values.at[tuple(place)].set(smallest)
    longest = extent.index(max(extent))
    place[longest] = (place[longest] + 1) % extent[longest]
    return values.at[tuple(place)].set(top_value)


def steps_of(key, shape, pieces, low, top_value):
    loudness = 1.0
    for position, blocks in pieces:
        draws = jax.random.uniform(jax.random.fold_in(jax.random.fold_in(key, 6), position), (blocks,), jnp.float32, low / len(pieces), top_value / len(pieces))
        loudness = loudness * jnp.repeat(jnp.exp(draws), shape[position] // blocks).reshape((-1,) + (1,) * (len(shape) - 1 - position))
    return loudness


def profile(amount, total, bound, slope):
    weights = [(1 << 20) // math.isqrt(rank ** slope) + 1 for rank in range(2, amount + 1)]
    spare, holding = total - bound - (amount - 1), [1] * (amount - 1)
    while spare > 0:
        candidates = [i for i in range(amount - 1) if holding[i] < bound]
        whole, budget = sum([weights[i] for i in candidates]), spare
        for i in candidates:
            addition = min(bound - holding[i], max(1, budget * weights[i] // whole), spare)
            holding[i] = holding[i] + addition
            spare = spare - addition
    return np.array([bound] + holding)


def uneven_parts(rng, amount, total, limit, slope):
    if amount == 2:
        one = jax.random.randint(rng, (), max(1, total - limit), min(limit, total - 1) + 1)
        return jnp.stack([one, total - one])
    sizes = jnp.asarray(profile(amount, total, limit, slope), jnp.int32)
    couples = (amount - 1) // 2
    donor, receiver = sizes[1:1 + 2 * couples:2], sizes[2:2 + 2 * couples:2]
    margin = jnp.minimum(donor - 1, limit - receiver)
    moved = jax.random.randint(jax.random.fold_in(rng, 1), (couples,), 0, 1 << 20) % (margin + 1)
    sizes = sizes.at[1:1 + 2 * couples:2].set(donor - moved).at[2:2 + 2 * couples:2].set(receiver + moved)
    return sizes[jax.random.permutation(jax.random.fold_in(rng, 2), amount)]


def scatter_about(rng, dims, deviation, most, cuts=(), dtype=jnp.bfloat16):
    level = steps_of(rng, dims, cuts, -0.22, 0.18) if cuts else 1.0
    drawn = jax.random.normal(rng, dims, jnp.float32) * deviation * level
    return jnp.minimum(jnp.maximum(drawn, -most), most).astype(dtype)


def setup_inputs(seed: int = 0) -> dict:
    key_list = jax.random.split(jax.random.key(seed), 10)
    tokens = scatter_about(key_list[0], (MB, MB_TOKENS, D), 1.0, 6.0, ((1, 32),))
    cotangent = scatter_about(key_list[1], (MB, MB_TOKENS, D), 1.0, 6.0, ((1, 32),))
    lengths = jax.vmap(lambda own: uneven_parts(own, NIMG, BLK, MOST, 1))(jax.random.split(key_list[2], MB * N_DP)).reshape((MB, N_DP, NIMG)).astype(jnp.int32)
    padding = set_ends((jax.random.randint(key_list[3], (MB, MB_TOKENS), 0, 8) < 7).astype(jnp.int32), jax.random.fold_in(key_list[3], 1), 0, 1)
    ln_gain = jnp.clip(1.0 + 0.1 * jax.random.normal(key_list[4], (LAYERS, 2, D), jnp.float32), 0.5, 1.5).astype(jnp.bfloat16)
    w_qkv = scatter_about(key_list[5], (LAYERS, D, 3, D), (D // 2) ** -0.5, 0.3125, ((1, 8), (3, 4)))
    w_out = scatter_about(key_list[6], (LAYERS, D, D), (D // 16) ** -0.5, 0.875, ((1, 4), (2, 8)))
    w_up = scatter_about(key_list[7], (LAYERS, D, FF), D ** -0.5, 0.21875, ((1, 8), (2, 4)))
    w_down = scatter_about(key_list[8], (LAYERS, FF, D), FF ** -0.5, 0.109375, ((1, 4), (2, 8)))
    return dict(tokens=tokens, cotangent=cotangent, lengths=lengths, padding=padding, ln_gain=ln_gain, w_qkv=w_qkv, w_out=w_out, w_up=w_up, w_down=w_down)


HIGHEST = lax.Precision.HIGHEST
NEGATIVE = -1e+30
EPSILON = 1e-06

@jax.custom_vjp
def low(v):
    return lax.optimization_barrier(v.astype(jnp.bfloat16)).astype(jnp.float32)

@jax.custom_vjp
def low_back(v):
    return v

def low_keep(v):
    return (low(v), None)

def low_pass(kept, grad):
    return (grad,)

def back_keep(v):
    return (v, None)

def back_low(kept, grad):
    return (low(grad),)
low.defvjp(low_keep, low_pass)
low_back.defvjp(back_keep, back_low)

def normalize(row_block):
    average = lax.optimization_barrier(jnp.mean(row_block, axis=-1, keepdims=True))
    centred = row_block - average
    variance = lax.optimization_barrier(jnp.mean(centred * centred, axis=-1, keepdims=True))
    return centred * lax.rsqrt(variance + EPSILON)

def visible(lengths_row, padding_row):
    places = lax.iota(jnp.int32, padding_row.shape[0])
    bounds = jnp.cumsum(lengths_row.astype(jnp.int32))
    picture = lax.optimization_barrier(jnp.sum((places[:, None] >= bounds[None, :]).astype(jnp.int32), axis=1))
    same_image = picture[:, None] == picture[None, :]
    return same_image & ((padding_row[None, :] == 1) | (places[:, None] == places[None, :]))

def attend_block(items):
    block_rows, lengths_row, padding_row = items
    allowed = visible(lengths_row, padding_row)
    scaling = HD ** (-0.5)
    scores = low_back(jnp.einsum('qhd,khd->hqk', block_rows[:, 0], block_rows[:, 1], precision=HIGHEST) * scaling)
    scores = jnp.where(allowed[None], scores, NEGATIVE)
    probability = low(jax.nn.softmax(scores, axis=-1))
    return jnp.einsum('hqk,khd->qhd', probability, block_rows[:, 2], precision=HIGHEST)

def forward(state, gains, qkv_weights, out_weights, up_weights, down_weights, lengths, padding):
    block_count = lengths.shape[0] * lengths.shape[1]
    length_rows = lengths.reshape(block_count, -1)
    padding_rows = padding.reshape(block_count, -1)
    for layer_index in range(LAYERS):
        entry = low(normalize(state) * gains[layer_index, 0])
        triple = low(low_back(jnp.einsum('rd,dcn->rcn', entry, qkv_weights[layer_index], precision=HIGHEST)))
        grouped = triple.reshape(block_count, BLK, 3, HEADS, HD)
        mixture = lax.map(jax.checkpoint(attend_block), (grouped, length_rows, padding_rows))
        mixture = low(low_back(mixture.reshape(-1, D)))
        state = state + low_back(jnp.dot(mixture, out_weights[layer_index], precision=HIGHEST))
        second_input = low(normalize(state) * gains[layer_index, 1])
        hidden_pre = low_back(jnp.dot(second_input, up_weights[layer_index], precision=HIGHEST))
        activated = low(jax.nn.gelu(hidden_pre, approximate=False))
        state = state + low_back(jnp.dot(activated, down_weights[layer_index], precision=HIGHEST))
    return state

def reference(tokens, cotangent, lengths, padding, ln_gain, w_qkv, w_out, w_up, w_down):
    state = tokens.astype(jnp.float32).reshape(-1, D)

    def wrapped(state_in, gains_in, qkv_in, out_in, up_in, down_in):
        return forward(state_in, gains_in, qkv_in, out_in, up_in, down_in, lengths, padding)
    result, pullback = jax.vjp(wrapped, state, ln_gain.astype(jnp.float32), w_qkv.astype(jnp.float32), w_out.astype(jnp.float32), w_up.astype(jnp.float32), w_down.astype(jnp.float32))
    gradients = pullback(cotangent.astype(jnp.float32).reshape(-1, D))
    return (result.reshape(tokens.shape), gradients[0].reshape(tokens.shape), gradients[1].reshape(-1), gradients[2], gradients[3], gradients[4], gradients[5])
```

```python
import functools

import jax
import jax.numpy as jnp
from jax import lax
from jax.experimental import pallas as pl
from jax.experimental.pallas import tpu as pltpu
from jax.sharding import PartitionSpec as P

D = 768
HD = 64
NEGATIVE = -1e30
EPSILON = 1e-06
MESH = pl.DeviceIdType.MESH
F32 = jnp.float32
BF16 = jnp.bfloat16
KINDS = 3


def flip(value, bit):
    size = 1 << bit
    return value + size * (1 - 2 * ((value // size) % 2))


def flip_mask(value, mask):
    bit = 0
    while mask >> bit:
        if (mask >> bit) & 1:
            value = flip(value, bit)
        bit += 1
    return value


def submasks(bits):
    masks = [0]
    for bit in bits:
        masks = masks + [mask | (1 << bit) for mask in masks]
    return masks


def color_order(color, bit_count):
    order = list(range(bit_count))
    return order if color == 0 else order[::-1]


class Place:
    def __init__(self, depth):
        dp = lax.axis_index("dp")
        self.z = lax.axis_index("tensor")
        self.c = dp % 2
        self.p = dp // 2
        self.depth = depth

    def same(self, p, c, z):
        return jnp.logical_and(c == self.c, z == self.z)


def device(p, c, z):
    return (2 * p + c, z)


def rows_of(p, color, shard):
    return pl.ds(pl.multiple_of((2 * p + color) * shard, 16), shard)


def send_or_copy(is_self, source, target, send_sem, recv_sem, dest):
    @pl.when(is_self)
    def _():
        pltpu.make_async_copy(source, target, recv_sem).start()

    @pl.when(jnp.logical_not(is_self))
    def _():
        pltpu.make_async_remote_copy(
            source, target, send_sem, recv_sem, device_id=dest, device_id_type=MESH
        ).start()


def wait_send_if(is_self, source, send_sem):
    @pl.when(jnp.logical_not(is_self))
    def _():
        pltpu.make_async_copy(source, source, send_sem).wait()


def wait_bytes(ref, sem):
    pltpu.make_async_copy(ref, ref, sem).wait()


def entry_barrier(here, depth, bit_count):
    barrier = pltpu.get_barrier_semaphore()
    count = 0
    for dz in range(depth):
        for dc in range(2):
            if dz == 0 and dc == 0:
                continue
            other_core = here.c if dc == 0 else 1 - here.c
            pl.semaphore_signal(
                barrier,
                inc=1,
                device_id=device(here.p, other_core, (here.z + dz) % depth),
                device_id_type=MESH,
            )
            count += 1
    for bit in range(bit_count):
        pl.semaphore_signal(
            barrier,
            inc=1,
            device_id=device(flip(here.p, bit), here.c, here.z),
            device_id_type=MESH,
        )
        count += 1
    pl.semaphore_wait(barrier, count)


def gather_kernel(depth, bit_count, shard, tok, cot, packed, x_out, dy_out, w_out, *sems):
    tok_s, tok_r, z_s, z_r, x_s, x_r = sems
    here = Place(depth)
    half = depth // 2
    entry_barrier(here, depth, bit_count)
    waits = []

    def send_rows(which, array, target):
        for m in range(2):
            to_z = 2 * m + here.c
            to_c = here.z // half
            is_self = here.same(here.p, to_c, to_z)
            slot = here.z % half
            send_or_copy(
                is_self,
                array.at[m],
                target.at[slot],
                tok_s.at[which, m],
                tok_r.at[which, slot],
                device(here.p, to_c, to_z),
            )
            waits.append(functools.partial(wait_send_if, is_self, array.at[m], tok_s.at[which, m]))

    def send_z(k):
        for dz in range(depth):
            to_z = (here.z + dz) % depth
            to_c = here.z // half
            is_self = here.same(here.p, to_c, to_z)
            slot = here.z % half
            send_or_copy(
                is_self,
                packed.at[k],
                w_out.at[k, slot, rows_of(here.p, here.c, shard)],
                z_s.at[k, dz],
                z_r.at[k, here.c, slot],
                device(here.p, to_c, to_z),
            )
            waits.append(functools.partial(wait_send_if, is_self, packed.at[k], z_s.at[k, dz]))

    def wait_z(k, color):
        for slot in range(half):
            wait_bytes(w_out.at[k, slot, rows_of(here.p, color, shard)], z_r.at[k, color, slot])

    def step(k, color, s):
        order = color_order(color, bit_count)
        for index, mask in enumerate(submasks(order[:s])):
            block = w_out.at[k, :, rows_of(flip_mask(here.p, mask), color, shard)]
            pltpu.make_async_remote_copy(
                block,
                block,
                x_s.at[k, color, s, index],
                x_r.at[k, color, s, index],
                device_id=device(flip(here.p, order[s]), here.c, here.z),
                device_id_type=MESH,
            ).start()
            waits.append(functools.partial(wait_bytes, block, x_s.at[k, color, s, index]))

    def wait_step(k, color, s):
        order = color_order(color, bit_count)
        for index, mask in enumerate(submasks(order[:s])):
            landed = flip(flip_mask(here.p, mask), order[s])
            wait_bytes(
                w_out.at[k, :, rows_of(landed, color, shard)], x_r.at[k, color, s, index]
            )

    send_z(0)
    send_rows(0, tok, x_out)
    send_z(1)
    send_z(2)
    send_rows(1, cot, dy_out)
    total = KINDS + bit_count
    for time in range(total + 1):
        for k in range(KINDS):
            s = time - k
            for color in range(2):
                if s == 0:
                    wait_z(k, color)
                elif 0 < s <= bit_count:
                    wait_step(k, color, s - 1)
                if 0 <= s < bit_count:
                    step(k, color, s)
    for which, target in ((0, x_out), (1, dy_out)):
        for slot in range(half):
            wait_bytes(target.at[slot], tok_r.at[which, slot])
    for wait in waits:
        wait()


def gather_all(mesh, tok, cot, packed):
    depth = mesh.shape["tensor"]
    bit_count = (mesh.shape["dp"] // 2).bit_length() - 1
    shard = packed.shape[1]
    half = depth // 2
    vmem = pl.BlockSpec(memory_space=pltpu.VMEM)
    sem = pltpu.SemaphoreType.DMA
    blocks = 1 << (bit_count - 1)
    return pl.pallas_call(
        functools.partial(gather_kernel, depth, bit_count, shard),
        out_shape=(
            jax.ShapeDtypeStruct((half,) + tok.shape[1:], BF16),
            jax.ShapeDtypeStruct((half,) + tok.shape[1:], BF16),
            jax.ShapeDtypeStruct((KINDS, half, D, packed.shape[2]), BF16),
        ),
        in_specs=[vmem] * 3,
        out_specs=(vmem,) * 3,
        scratch_shapes=[
            sem((2, 2)),
            sem((2, half)),
            sem((KINDS, depth)),
            sem((KINDS, 2, half)),
            sem((KINDS, 2, bit_count, blocks)),
            sem((KINDS, 2, bit_count, blocks)),
        ],
        compiler_params=pltpu.CompilerParams(
            collective_id=0, has_side_effects=True, vmem_limit_bytes=40 << 20
        ),
        name="gather_all",
    )(tok, cot, packed)


def scatter_kernel(
    depth, bit_count, shard, grads, y, dx, g_out, y_out, dx_out, held, rx, zrx, copy_sem, *sems
):
    row_s, row_r, z_s, z_r, x_s, x_r = sems
    here = Place(depth)
    half = depth // 2
    pltpu.make_async_copy(grads, held, copy_sem).start()
    entry_barrier(here, depth, bit_count)
    waits = []

    def send_rows(which, array, target):
        for slot in range(half):
            to_c = here.z % 2
            to_z = half * here.c + slot
            is_self = here.same(here.p, to_c, to_z)
            m = here.z // 2
            send_or_copy(
                is_self,
                array.at[slot],
                target.at[m],
                row_s.at[which, slot],
                row_r.at[which, m],
                device(here.p, to_c, to_z),
            )
            waits.append(
                functools.partial(wait_send_if, is_self, array.at[slot], row_s.at[which, slot])
            )

    def order_of(color):
        return color_order(color, bit_count)[::-1]

    def step(k, color, s):
        order = order_of(color)
        bit = order[s]
        for index, mask in enumerate(submasks(order[s + 1 :])):
            block = held.at[k, :, rows_of(flip_mask(flip(here.p, bit), mask), color, shard)]
            pltpu.make_async_remote_copy(
                block,
                rx.at[k, color, (1 << bit_count) - (1 << (bit_count - s)) + index],
                x_s.at[k, color, s, index],
                x_r.at[k, color, s, index],
                device_id=device(flip(here.p, bit), here.c, here.z),
                device_id_type=MESH,
            ).start()
            waits.append(functools.partial(wait_bytes, block, x_s.at[k, color, s, index]))

    def finish_step(k, color, s):
        order = order_of(color)
        for index, mask in enumerate(submasks(order[s + 1 :])):
            got = rx.at[k, color, (1 << bit_count) - (1 << (bit_count - s)) + index]
            wait_bytes(got, x_r.at[k, color, s, index])
            block = held.at[k, :, rows_of(flip_mask(here.p, mask), color, shard)]
            block[...] = (block[...].astype(F32) + got[...].astype(F32)).astype(BF16)

    def send_z(k, color):
        for slot in range(half):
            to_z = half * here.c + slot
            is_self = here.same(here.p, color, to_z)
            block = held.at[k, slot, rows_of(here.p, color, shard)]
            send_or_copy(
                is_self,
                block,
                zrx.at[k, here.z],
                z_s.at[k, color, slot],
                z_r.at[k, here.z],
                device(here.p, color, to_z),
            )
            waits.append(functools.partial(wait_send_if, is_self, block, z_s.at[k, color, slot]))

    def finish_z(k):
        for source in range(depth):
            wait_bytes(zrx.at[k, source], z_r.at[k, source])
        total = zrx[k, 0].astype(F32)
        for source in range(1, depth):
            total = total + zrx[k, source].astype(F32)
        g_out[k] = total

    send_rows(0, y, y_out)
    send_rows(1, dx, dx_out)
    pltpu.make_async_copy(grads, held, copy_sem).wait()
    for time in range(KINDS + bit_count + 1):
        for k in reversed(range(KINDS)):
            s = time - (KINDS - 1 - k)
            for color in range(2):
                if 0 < s <= bit_count:
                    finish_step(k, color, s - 1)
                if 0 <= s < bit_count:
                    step(k, color, s)
                elif s == bit_count:
                    send_z(k, color)
    for k in reversed(range(KINDS)):
        finish_z(k)
    for which, target in ((0, y_out), (1, dx_out)):
        for m in range(2):
            wait_bytes(target.at[m], row_r.at[which, m])
    for wait in waits:
        wait()


def scatter_all(mesh, grads, y, dx, shard):
    depth = mesh.shape["tensor"]
    bit_count = (mesh.shape["dp"] // 2).bit_length() - 1
    half = depth // 2
    vmem = pl.BlockSpec(memory_space=pltpu.VMEM)
    sem = pltpu.SemaphoreType.DMA
    blocks = 1 << (bit_count - 1)
    width = grads.shape[3]
    return pl.pallas_call(
        functools.partial(scatter_kernel, depth, bit_count, shard),
        out_shape=(
            jax.ShapeDtypeStruct((KINDS, shard, width), F32),
            jax.ShapeDtypeStruct(y.shape, BF16),
            jax.ShapeDtypeStruct(dx.shape, BF16),
        ),
        in_specs=[pl.BlockSpec(memory_space=pl.ANY), vmem, vmem],
        out_specs=(vmem,) * 3,
        scratch_shapes=[
            pltpu.VMEM(grads.shape, BF16),
            pltpu.VMEM((KINDS, 2, (1 << bit_count) - 1, half, shard, width), BF16),
            pltpu.VMEM((KINDS, depth, shard, width), BF16),
            sem(()),
            sem((2, half)),
            sem((2, 2)),
            sem((KINDS, 2, half)),
            sem((KINDS, depth)),
            sem((KINDS, 2, bit_count, blocks)),
            sem((KINDS, 2, bit_count, blocks)),
        ],
        compiler_params=pltpu.CompilerParams(
            collective_id=1, has_side_effects=True, vmem_limit_bytes=60 << 20
        ),
        name="scatter_all",
    )(grads, y, dx)


def normalize(row_block):
    average = jnp.mean(row_block, axis=-1, keepdims=True)
    centred = row_block - average
    variance = jnp.mean(centred * centred, axis=-1, keepdims=True)
    inverse = lax.rsqrt(variance + EPSILON)
    return (centred * inverse, inverse)


def norm_back(grad_out, gain_row, normed, inverse):
    scaled = grad_out * gain_row
    mean_grad = jnp.mean(scaled, axis=-1, keepdims=True)
    second = jnp.mean(scaled * normed, axis=-1, keepdims=True)
    return inverse * (scaled - mean_grad - normed * second)


def visible(lengths_row, padding_row):
    places = lax.iota(jnp.int32, padding_row.shape[0])
    bounds = jnp.cumsum(lengths_row)
    picture = jnp.sum((places[:, None] >= bounds[None, :]).astype(jnp.int32), axis=1)
    same_image = picture[:, None] == picture[None, :]
    return same_image & ((padding_row[None, :] == 1) | (places[:, None] == places[None, :]))


def gelu_exact(pre_values):
    return jax.nn.gelu(pre_values, approximate=False)


def masked_scores(queries, key_rows, allowed):
    scaling = queries.shape[-1] ** (-0.5)
    scores = (
        jnp.einsum("qhd,khd->hqk", queries, key_rows, preferred_element_type=jnp.float32) * scaling
    )
    return (jnp.where(allowed[None], scores, NEGATIVE), scaling)


def attend(stacked, allowed):
    scores, scaling = masked_scores(stacked[:, 0], stacked[:, 1], allowed)
    highest = jnp.max(scores, axis=-1, keepdims=True)
    exponent = jnp.exp(scores - highest)
    totals = jnp.sum(exponent, axis=-1, keepdims=True)
    rounded = (exponent / totals).astype(jnp.bfloat16)
    mixture = jnp.einsum("hqk,khd->qhd", rounded, stacked[:, 2], preferred_element_type=jnp.float32)
    return (mixture, highest, totals)


def attend_back(stacked, allowed, highest, totals, grad_mix):
    queries, key_rows, value_rows = (stacked[:, 0], stacked[:, 1], stacked[:, 2])
    scores, scaling = masked_scores(queries, key_rows, allowed)
    probability = jnp.exp(scores - highest) / totals
    rounded = probability.astype(jnp.bfloat16)
    grad_prob = jnp.einsum("qhd,khd->hqk", grad_mix, value_rows, preferred_element_type=jnp.float32)
    grad_values = jnp.einsum("hqk,qhd->khd", rounded, grad_mix, preferred_element_type=jnp.float32)
    inner_sum = jnp.sum(probability * grad_prob, axis=-1, keepdims=True)
    grad_scores = (probability * (grad_prob - inner_sum)).astype(jnp.bfloat16)
    grad_queries = (
        jnp.einsum("hqk,khd->qhd", grad_scores, key_rows, preferred_element_type=jnp.float32)
        * scaling
    )
    grad_keys = (
        jnp.einsum("hqk,qhd->khd", grad_scores, queries, preferred_element_type=jnp.float32)
        * scaling
    )
    return jnp.stack([grad_queries, grad_keys, grad_values], axis=1).astype(jnp.bfloat16)


def block_body(mesh, tokens, cotangent, lengths, padding, ln_gain, w_qkv, w_out, w_up, w_down):
    dp_size, depth = mesh.shape["dp"], mesh.shape["tensor"]
    half = depth // 2
    core = lax.axis_index("dp") % 2
    z = lax.axis_index("tensor")
    swap = [(i, i ^ 1) for i in range(dp_size)]

    def partner(value):
        return lax.ppermute(value, "dp", swap)

    def pair_gather(own):
        other = partner(own)
        return jnp.concatenate(
            [jnp.where(core == 0, own, other), jnp.where(core == 0, other, own)], axis=0
        )

    def pair_scatter(partial):
        rows = partial.shape[0] // 2
        parts = partial.reshape(2, rows, -1)
        own = lax.dynamic_index_in_dim(parts, core, 0, keepdims=False)
        other = lax.dynamic_index_in_dim(parts, 1 - core, 0, keepdims=False)
        return own + partner(other.astype(BF16)).astype(F32)

    shard = w_up.shape[1]
    hid = w_up.shape[2]
    heads_width = w_qkv.shape[3]
    packed = jnp.stack(
        [
            jnp.concatenate([w_qkv[0].reshape(shard, 3 * heads_width), w_out[0].T], axis=1),
            w_up[0],
            w_down[0].T,
        ]
    )
    gains = lax.all_gather(ln_gain[0], "dp", axis=1, tiled=True).astype(F32)
    gain_first, gain_second = gains[0], gains[1]
    other_lengths = partner(lengths)
    other_padding = partner(padding)
    micro = z // 2
    mine = (z % 2) == core
    use_lengths = jnp.where(mine, lengths, other_lengths)[:, 0]
    use_padding = jnp.where(mine, padding, other_padding)
    allowed = visible(
        lax.dynamic_index_in_dim(use_lengths, micro, 0, keepdims=False),
        lax.dynamic_index_in_dim(use_padding, micro, 0, keepdims=False),
    )

    x_rows, dy_rows, gathered = gather_all(mesh, tokens, cotangent, packed)
    entering = x_rows.reshape(-1, D).astype(F32)
    first = gathered[0]
    qkv_weight = first[:, :, : 3 * heads_width]
    out_weight_t = first[:, :, 3 * heads_width :]
    up_weight = gathered[1]
    down_weight_t = gathered[2]

    normed, inverse = normalize(entering)
    first_input = pair_gather((normed * gain_first).astype(BF16))
    triple = jnp.einsum("rd,hdn->hrn", first_input, qkv_weight, preferred_element_type=F32).astype(
        BF16
    )
    rows = first_input.shape[0]
    stacked = (
        triple.reshape(half, rows, 3, -1, HD).transpose(1, 2, 0, 3, 4).reshape(rows, 3, -1, HD)
    )
    mixture, highest, totals = attend(stacked, allowed)
    mix_rounded = mixture.reshape(rows, half, -1).astype(BF16)
    middle = entering + pair_scatter(
        jnp.einsum("rhn,hdn->rd", mix_rounded, out_weight_t, preferred_element_type=F32)
    )
    normed_two, inverse_two = normalize(middle)
    second_input = pair_gather((normed_two * gain_second).astype(BF16))
    hidden_pre = jnp.einsum("rd,hdn->hrn", second_input, up_weight, preferred_element_type=F32)
    activated = gelu_exact(hidden_pre).astype(BF16)
    layer_rows = middle + pair_scatter(
        jnp.einsum("hrn,hdn->rd", activated, down_weight_t, preferred_element_type=F32)
    )

    incoming = dy_rows.reshape(-1, D).astype(F32)
    grad_down = pair_gather(dy_rows.reshape(-1, D))
    down_part = jnp.einsum("rd,hrn->hdn", grad_down, activated, preferred_element_type=F32)
    grad_act = jnp.einsum("rd,hdn->hrn", grad_down, down_weight_t, preferred_element_type=F32)
    pulled = jax.vjp(gelu_exact, hidden_pre)
    grad_pre = pulled[1](grad_act)[0].astype(BF16)
    up_part = jnp.einsum("rd,hrn->hdn", second_input, grad_pre, preferred_element_type=F32)
    grad_norm_two = pair_scatter(
        jnp.einsum("hrn,hdn->rd", grad_pre, up_weight, preferred_element_type=F32)
    )
    gain_two_part = jnp.sum(grad_norm_two * normed_two, axis=0)
    incoming = incoming + norm_back(grad_norm_two, gain_second, normed_two, inverse_two)
    grad_branch = pair_gather(incoming.astype(BF16))
    out_part = jnp.einsum("rd,rhn->hdn", grad_branch, mix_rounded, preferred_element_type=F32)
    grad_mix = (
        jnp.einsum("rd,hdn->rhn", grad_branch, out_weight_t, preferred_element_type=F32)
        .astype(BF16)
        .reshape(rows, -1, HD)
    )
    grad_triple = attend_back(stacked, allowed, highest, totals, grad_mix)
    flat_triple = (
        grad_triple.reshape(rows, 3, half, -1).transpose(2, 0, 1, 3).reshape(half, rows, -1)
    )
    qkv_part = jnp.einsum("rd,hrn->hdn", first_input, flat_triple, preferred_element_type=F32)
    grad_norm_one = pair_scatter(
        jnp.einsum("hrn,hdn->rd", flat_triple, qkv_weight, preferred_element_type=F32)
    )
    gain_one_part = jnp.sum(grad_norm_one * normed, axis=0)
    incoming = incoming + norm_back(grad_norm_one, gain_first, normed, inverse)
    grads = jnp.stack(
        [
            jnp.concatenate([qkv_part.astype(BF16), out_part.astype(BF16)], axis=2),
            up_part.astype(BF16),
            down_part.astype(BF16),
        ]
    )
    shape = x_rows.shape
    summed, y_back, dx_back = scatter_all(
        mesh,
        grads,
        layer_rows.astype(BF16).reshape(shape),
        incoming.astype(BF16).reshape(shape),
        shard,
    )
    gain_flat = jnp.concatenate([gain_one_part, gain_two_part])
    gain_result = lax.psum_scatter(gain_flat, ("dp", "tensor"), scatter_dimension=0, tiled=True)
    qkv_grad = summed[0, :, : 3 * heads_width].reshape(1, shard, 3, heads_width)
    out_grad = summed[0, :, 3 * heads_width :].T[None]
    up_grad = summed[1][None]
    down_grad = summed[2].T[None]
    return (
        y_back.astype(F32),
        dx_back.astype(F32),
        gain_result,
        qkv_grad,
        out_grad,
        up_grad,
        down_grad,
    )


def collect_weights(ln_gain, w_qkv, w_out, w_up, w_down, layer_index):
    return (
        lax.all_gather(ln_gain[layer_index], "dp", axis=1, tiled=True),
        lax.all_gather(w_qkv[layer_index], "dp", axis=0, tiled=True),
        lax.all_gather(w_out[layer_index], "dp", axis=1, tiled=True),
        lax.all_gather(w_up[layer_index], "dp", axis=0, tiled=True),
        lax.all_gather(w_down[layer_index], "dp", axis=1, tiled=True),
    )


def spread(block_rows):
    return lax.all_gather(block_rows, "tensor", axis=0, tiled=True)


def spread_grad(block_rows):
    return lax.all_gather(block_rows, "tensor", axis=0, tiled=True)


def collect_rows(operand, weight):
    return lax.psum_scatter(
        jnp.dot(operand, weight, preferred_element_type=jnp.float32),
        "tensor",
        scatter_dimension=0,
        tiled=True,
    )


def return_rows(operand, weight):
    return lax.psum_scatter(
        lax.dot_general(
            operand, weight, (((1,), (1,)), ((), ())), preferred_element_type=jnp.float32
        ),
        "tensor",
        scatter_dimension=0,
        tiled=True,
    )


def reduce_grads(pieces):
    return (
        lax.psum_scatter(pieces[0], "dp", scatter_dimension=0, tiled=True),
        lax.psum_scatter(pieces[1], "dp", scatter_dimension=1, tiled=True),
        lax.psum_scatter(pieces[2], "dp", scatter_dimension=0, tiled=True),
        lax.psum_scatter(pieces[3], "dp", scatter_dimension=1, tiled=True),
    )


def body(tokens, cotangent, lengths, padding, ln_gain, w_qkv, w_out, w_up, w_down):
    layer_count = w_qkv.shape[0]
    micro_count = tokens.shape[0]
    residual = [tokens[batch_index].astype(jnp.float32) for batch_index in range(micro_count)]
    visibility = [
        visible(lengths[batch_index, 0], padding[batch_index]) for batch_index in range(micro_count)
    ]
    saved = []
    stored_weights = []
    layer_index = 0
    stored_weights.append(None)
    for batch_index in range(micro_count):
        weights = collect_weights(ln_gain, w_qkv, w_out, w_up, w_down, layer_index)
        gain_pair, qkv_weight, out_weight, up_weight, down_weight = weights
        gain_first = gain_pair[0].astype(jnp.float32)
        gain_second = gain_pair[1].astype(jnp.float32)
        entering = residual[batch_index]
        normed, inverse = normalize(entering)
        first_input = spread((normed * gain_first).astype(jnp.bfloat16))
        triple = jnp.einsum(
            "rd,dcn->rcn", first_input, qkv_weight, preferred_element_type=jnp.float32
        ).astype(jnp.bfloat16)
        stacked = triple.reshape(triple.shape[0], 3, -1, HD)
        mixture, highest, totals = attend(stacked, visibility[batch_index])
        mix_rounded = mixture.reshape(mixture.shape[0], -1).astype(jnp.bfloat16)
        middle = entering + collect_rows(mix_rounded, out_weight)
        normed_two, inverse_two = normalize(middle)
        second_input = spread((normed_two * gain_second).astype(jnp.bfloat16))
        hidden_pre = jnp.dot(second_input, up_weight, preferred_element_type=jnp.float32)
        activated = gelu_exact(hidden_pre).astype(jnp.bfloat16)
        residual[batch_index] = middle + collect_rows(activated, down_weight)
        saved.append(
            (
                entering,
                first_input,
                stacked,
                highest,
                totals,
                mix_rounded,
                middle,
                second_input,
                hidden_pre,
                activated,
            )
        )
    gradients = [cotangent[batch_index].astype(jnp.float32) for batch_index in range(micro_count)]
    gain_parts = [jnp.zeros((2, D), jnp.float32)]
    weight_results = [None]
    for layer_index in reversed(range(layer_count)):
        summed = None
        for batch_index in range(micro_count):
            weights = collect_weights(ln_gain, w_qkv, w_out, w_up, w_down, layer_index)
            gain_pair, qkv_weight, out_weight, up_weight, down_weight = weights
            gain_first = gain_pair[0].astype(jnp.float32)
            gain_second = gain_pair[1].astype(jnp.float32)
            (
                entering,
                first_input,
                stacked,
                highest,
                totals,
                mix_rounded,
                middle,
                second_input,
                hidden_pre,
                activated,
            ) = saved[layer_index * micro_count + batch_index]
            incoming = gradients[batch_index]
            grad_down = spread_grad(incoming.astype(jnp.bfloat16))
            down_part = jnp.einsum(
                "rf,rd->fd", activated, grad_down, preferred_element_type=jnp.float32
            )
            grad_act = lax.dot_general(
                grad_down, down_weight, (((1,), (1,)), ((), ())), preferred_element_type=jnp.float32
            )
            pulled = jax.vjp(gelu_exact, hidden_pre)
            grad_pre = pulled[1](grad_act)[0].astype(jnp.bfloat16)
            up_part = jnp.einsum(
                "rd,rf->df", second_input, grad_pre, preferred_element_type=jnp.float32
            )
            grad_norm_two = return_rows(grad_pre, up_weight)
            normed_two, inverse_two = normalize(middle)
            gain_two_part = jnp.sum(grad_norm_two * normed_two, axis=0)
            incoming = incoming + norm_back(grad_norm_two, gain_second, normed_two, inverse_two)
            grad_branch = spread_grad(incoming.astype(jnp.bfloat16))
            out_part = jnp.einsum(
                "rk,rd->kd", mix_rounded, grad_branch, preferred_element_type=jnp.float32
            )
            grad_mix = lax.dot_general(
                grad_branch,
                out_weight,
                (((1,), (1,)), ((), ())),
                preferred_element_type=jnp.float32,
            )
            grad_mix = grad_mix.astype(jnp.bfloat16).reshape(grad_mix.shape[0], -1, HD)
            grad_triple = attend_back(stacked, visibility[batch_index], highest, totals, grad_mix)
            flat_triple = grad_triple.reshape(grad_triple.shape[0], 3, -1)
            qkv_part = jnp.einsum(
                "rd,rcn->dcn", first_input, flat_triple, preferred_element_type=jnp.float32
            )
            grad_norm_one = return_rows(
                flat_triple.reshape(flat_triple.shape[0], -1),
                qkv_weight.reshape(qkv_weight.shape[0], -1),
            )
            normed, inverse = normalize(entering)
            gain_one_part = jnp.sum(grad_norm_one * normed, axis=0)
            incoming = incoming + norm_back(grad_norm_one, gain_first, normed, inverse)
            gradients[batch_index] = incoming
            gain_parts[layer_index] = gain_parts[layer_index] + jnp.stack(
                [gain_one_part, gain_two_part]
            )
            pieces = (qkv_part, out_part, up_part, down_part)
            if summed is None:
                summed = pieces
            else:
                summed = tuple((older + newer for older, newer in zip(summed, pieces)))
        summed = reduce_grads(summed)
        weight_results[layer_index] = summed
    gain_flat = jnp.stack(gain_parts).reshape(-1)
    gain_result = lax.psum_scatter(gain_flat, ("dp", "tensor"), scatter_dimension=0, tiled=True)
    layer_out = jnp.stack(residual)
    input_grad = jnp.stack(gradients)
    qkv_grad = jnp.stack([weight_results[0][0]])
    out_grad = jnp.stack([weight_results[0][1]])
    up_grad = jnp.stack([weight_results[0][2]])
    down_grad = jnp.stack([weight_results[0][3]])
    return (layer_out, input_grad, gain_result, qkv_grad, out_grad, up_grad, down_grad)


def fits(mesh):
    dp_size, depth = mesh.shape["dp"], mesh.shape["tensor"]
    columns = dp_size // 2
    return (
        depth == 4 and dp_size >= 4 and columns & (columns - 1) == 0 and D % (dp_size * 16) == 0
    )


def solution(mesh):
    program = functools.partial(block_body, mesh) if fits(mesh) else body
    return jax.shard_map(
        program,
        mesh=mesh,
        in_specs=(
            P(None, ("dp", "tensor"), None),
            P(None, ("dp", "tensor"), None),
            P(None, "dp", None),
            P(None, "dp"),
            P(None, None, "dp"),
            P(None, "dp", None, "tensor"),
            P(None, "tensor", "dp"),
            P(None, "dp", "tensor"),
            P(None, "tensor", "dp"),
        ),
        out_specs=(
            P(None, ("dp", "tensor"), None),
            P(None, ("dp", "tensor"), None),
            P(("dp", "tensor")),
            P(None, "dp", None, "tensor"),
            P(None, "tensor", "dp"),
            P(None, "dp", "tensor"),
            P(None, "tensor", "dp"),
        ),
        check_vma=False,
    )
```

```python
import functools

import jax
import jax.numpy as jnp
from jax import lax
from jax.experimental import pallas as pl
from jax.experimental.pallas import tpu as pltpu
from jax.sharding import PartitionSpec as P

D = 768
HD = 64
NEGATIVE = -1e30
EPSILON = 1e-06
MESH = pl.DeviceIdType.MESH
F32 = jnp.float32
BF16 = jnp.bfloat16
KINDS = 3
TILE = 256
SCALE = HD**-0.5


def flip(value, bit):
    size = 1 << bit
    return value + size * (1 - 2 * ((value // size) % 2))


def flip_mask(value, mask):
    bit = 0
    while mask >> bit:
        if (mask >> bit) & 1:
            value = flip(value, bit)
        bit += 1
    return value


def submasks(bits):
    masks = [0]
    for bit in bits:
        masks = masks + [mask | (1 << bit) for mask in masks]
    return masks


def color_order(color, bit_count):
    order = list(range(bit_count))
    return order if color == 0 else order[::-1]


def device(p, c, z):
    return (2 * p + c, z)


def dot(left, right):
    return jnp.dot(left, right, preferred_element_type=F32)


def dot_nt(left, right):
    return lax.dot_general(left, right, (((1,), (1,)), ((), ())), preferred_element_type=F32)


def normalize(row_block):
    average = jnp.mean(row_block, axis=-1, keepdims=True)
    centred = row_block - average
    variance = jnp.mean(centred * centred, axis=-1, keepdims=True)
    inverse = lax.rsqrt(variance + EPSILON)
    return (centred * inverse, inverse)


def norm_back(grad_out, gain_row, normed, inverse):
    scaled = grad_out * gain_row
    mean_grad = jnp.mean(scaled, axis=-1, keepdims=True)
    second = jnp.mean(scaled * normed, axis=-1, keepdims=True)
    return inverse * (scaled - mean_grad - normed * second)


def remote(source, target, send_sem, recv_sem, dest):
    return pltpu.make_async_remote_copy(
        source, target, send_sem, recv_sem, device_id=dest, device_id_type=MESH
    )


def wait_bytes(ref, sem):
    pltpu.make_async_copy(ref, ref, sem).wait()


SEMS = (
    "tok_s",
    "tok_r",
    "gain_s",
    "gain_r",
    "code_s",
    "code_l",
    "code_r",
    "z_s",
    "z_r",
    "rel_s",
    "x_s",
    "x_r",
    "rs_s",
    "rs_r",
    "rz_s",
    "rz_r",
    "out_s",
    "out_r",
    "pa_s",
    "pa_r",
    "pr_s",
    "pr_r",
    "sum_s",
    "sum_r",
    "all_s",
    "all_r",
)


def layer_kernel(depth, bit_count, shard, rows, *refs):
    (tok, cot, packed, gain_in, code_in, y_out, dx_out, g_out, gm_out) = refs[:9]
    (
        xb,
        dyb,
        ab,
        bnb,
        wts,
        wq,
        qkv,
        qtz,
        vt,
        kt,
        pt,
        bias,
        ott,
        orow,
        dorow,
        mid,
        gact,
        dgel,
        prs,
        prr,
        stage,
        rx,
        zrx,
        gbuf,
        code,
        gsum,
        sum_rx,
        all_rx,
        delta,
    ) = refs[9:38]
    sem = dict(zip(SEMS, refs[38:]))
    half = depth // 2
    columns = 1 << bit_count
    own_rows = rows // 2
    chunks = own_rows // TILE
    dp = lax.axis_index("dp")
    z = lax.axis_index("tensor")
    c = dp % 2
    p = dp // 2
    buddy = device(p, 1 - c, z)
    mine = pl.multiple_of(own_rows * c, own_rows)
    theirs = pl.multiple_of(own_rows * (1 - c), own_rows)
    lane = lax.broadcasted_iota(jnp.int32, (1, 128), 1)
    low = lane < HD

    def same(to_c, to_z):
        return jnp.logical_and(to_c == c, to_z == z)

    def shard_rows(column, color):
        return pl.ds(pl.multiple_of((2 * column + color) * shard, 32), shard)

    def send_or_copy(is_self, source, target, send_sem, recv_sem, dest):
        @pl.when(is_self)
        def _():
            pltpu.make_async_copy(source, target, recv_sem).start()

        @pl.when(jnp.logical_not(is_self))
        def _():
            remote(source, target, send_sem, recv_sem, dest).start()

    def wait_send(is_self, source, send_sem):
        @pl.when(jnp.logical_not(is_self))
        def _():
            wait_bytes(source, send_sem)

    column_peers = []
    for dz in range(depth):
        for dc in range(2):
            if dz or dc:
                column_peers.append((c if dc == 0 else 1 - c, (z + dz) % depth))
    plane_peers = [flip_mask(p, mask) for mask in range(1, columns)]

    def entry_barrier():
        barrier = pltpu.get_barrier_semaphore()
        peers = [device(p, cc, zz) for cc, zz in column_peers]
        peers += [device(pp, c, z) for pp in plane_peers]
        peers += [device(pp, 1 - c, z) for pp in plane_peers]
        for peer in peers:
            pl.semaphore_signal(barrier, inc=1, device_id=peer, device_id_type=MESH)
        pl.semaphore_wait(barrier, len(peers))

    def send_small():
        remote(code_in, code.at[c], sem["code_s"], sem["code_r"], buddy).start()
        pltpu.make_async_copy(code_in, code.at[c], sem["code_l"]).start()
        index = 0
        for pp in [p] + plane_peers:
            for cc in (c, 1 - c):
                if index:
                    remote(
                        gain_in,
                        gbuf.at[dp],
                        sem["gain_s"].at[index],
                        sem["gain_r"].at[dp],
                        device(pp, cc, z),
                    ).start()
                index += 1
        pltpu.make_async_copy(gain_in, gbuf.at[dp], sem["gain_r"].at[dp]).start()

    def finish_small():
        wait_bytes(code_in, sem["code_s"])
        wait_bytes(code_in, sem["code_l"])
        wait_bytes(code.at[1 - c], sem["code_r"])
        for source in range(2 * columns):
            wait_bytes(gbuf.at[source], sem["gain_r"].at[source])
        for index in range(1, 2 * columns):
            wait_bytes(gain_in, sem["gain_s"].at[index])
        total = gbuf[0]
        for source in range(1, 2 * columns):
            total = total + gbuf[source]
        gbuf[0] = total

    def row_targets():
        for m in range(2):
            to_z, to_c = 2 * m + c, z // half
            yield m, to_c, to_z, same(to_c, to_z)

    def row_target(which, slot):
        if which == 0:
            return xb.at[slot]
        return dyb.at[pl.ds(pl.multiple_of(own_rows * c + TILE * slot, TILE), TILE)]

    def row_landing(which, slot, to_c):
        if which == 0:
            return xb.at[slot]
        return dyb.at[pl.ds(pl.multiple_of(own_rows * to_c + TILE * slot, TILE), TILE)]

    def send_rows(which, array):
        for m, to_c, to_z, is_self in row_targets():
            slot = z % half
            send_or_copy(
                is_self,
                array.at[m],
                row_landing(which, slot, to_c),
                sem["tok_s"].at[which, m],
                sem["tok_r"].at[which, slot],
                device(p, to_c, to_z),
            )

    def rows_sent(which, array):
        for m, to_c, to_z, is_self in row_targets():
            wait_send(is_self, array.at[m], sem["tok_s"].at[which, m])

    def rows_landed(which):
        for slot in range(half):
            wait_bytes(row_target(which, slot), sem["tok_r"].at[which, slot])

    def send_back(which, target):
        for slot in range(half):
            to_c, to_z = z % 2, half * c + slot
            send_or_copy(
                same(to_c, to_z),
                stage.at[slot],
                target.at[z // 2],
                sem["out_s"].at[which, slot],
                sem["out_r"].at[which, z // 2],
                device(p, to_c, to_z),
            )

    def back_sent(which):
        for slot in range(half):
            is_self = same(z % 2, half * c + slot)
            wait_send(is_self, stage.at[slot], sem["out_s"].at[which, slot])

    def back_landed(which, target):
        for m in range(2):
            wait_bytes(target.at[m], sem["out_r"].at[which, m])

    last = depth - 1

    def z_targets():
        for dz in range(depth):
            to_z = (z + dz) % depth
            far = jnp.logical_or(
                jnp.logical_and(z == 0, to_z == last), jnp.logical_and(z == last, to_z == 0)
            )
            yield dz, z // half, to_z, far

    def gather_z(k):
        for dz, to_c, to_z, far in z_targets():
            source = packed.at[k]
            target = wts.at[k, z % half, shard_rows(p, c)]
            recv = sem["z_r"].at[k, c, z % half]
            if dz == 0:
                send_or_copy(
                    to_c == c, source, target, sem["z_s"].at[k, dz], recv, device(p, to_c, to_z)
                )
            else:

                @pl.when(jnp.logical_not(far))
                def _():
                    remote(
                        source, target, sem["z_s"].at[k, dz], recv, device(p, to_c, to_z)
                    ).start()

    def gather_z_sent(k):
        for dz, to_c, to_z, far in z_targets():
            skip = to_c == c if dz == 0 else far
            wait_send(skip, packed.at[k], sem["z_s"].at[k, dz])

    relays = jnp.logical_or(
        jnp.logical_and(c == 0, z == last - 1), jnp.logical_and(c == 1, z == 1)
    )
    relay_slot = (half - 1) * c
    relay_to = device(p, c, last * (1 - c))

    def relay_block(k, color):
        return wts.at[k, relay_slot, shard_rows(p, color)]

    def after_z(k):
        for color in range(2):
            for slot in range(half):
                wait_bytes(wts.at[k, slot, shard_rows(p, color)], sem["z_r"].at[k, color, slot])
        for color in range(2):
            gather_step(k, color, 0)

        @pl.when(relays)
        def _():
            for color in range(2):
                block = relay_block(k, color)
                remote(
                    block,
                    block,
                    sem["rel_s"].at[k, color],
                    sem["z_r"].at[k, color, relay_slot],
                    relay_to,
                ).start()

    def gather_step(k, color, s):
        order = color_order(color, bit_count)
        for index, mask in enumerate(submasks(order[:s])):
            block = wts.at[k, :, shard_rows(flip_mask(p, mask), color)]
            remote(
                block,
                block,
                sem["x_s"].at[k, color, s, index],
                sem["x_r"].at[k, color, s, index],
                device(flip(p, order[s]), c, z),
            ).start()

    def gather_next(k, s):
        for color in range(2):
            order = color_order(color, bit_count)
            for index, mask in enumerate(submasks(order[:s])):
                landed = flip(flip_mask(p, mask), order[s])
                wait_bytes(
                    wts.at[k, :, shard_rows(landed, color)], sem["x_r"].at[k, color, s, index]
                )
            if s + 1 < bit_count:
                gather_step(k, color, s + 1)

    def gather_sent(k):
        gather_z_sent(k)

        @pl.when(relays)
        def _():
            for color in range(2):
                wait_bytes(relay_block(k, color), sem["rel_s"].at[k, color])

        for color in range(2):
            order = color_order(color, bit_count)
            for s in range(bit_count):
                for index, mask in enumerate(submasks(order[:s])):
                    block = wts.at[k, :, shard_rows(flip_mask(p, mask), color)]
                    wait_bytes(block, sem["x_s"].at[k, color, s, index])

    place = {2: 0, 1: 1, 0: 2}

    def rx_slot(k, color, s, index):
        return rx.at[k, color, (1 << bit_count) - (1 << (bit_count - s)) + index]

    def scatter_order(color):
        return color_order(color, bit_count)[::-1]

    def scatter_blocks(k, color, s, away):
        order = scatter_order(color)
        for index, mask in enumerate(submasks(order[s + 1 :])):
            column = flip_mask(p, mask)
            if away:
                column = flip(column, order[s])
            yield index, wts.at[place[k], :, shard_rows(column, color)]

    def scatter_step(k, s):
        for color in range(2):
            to = device(flip(p, scatter_order(color)[s]), c, z)
            for index, block in scatter_blocks(k, color, s, True):
                remote(
                    block,
                    rx_slot(k, color, s, index),
                    sem["rs_s"].at[k, color, s, index],
                    sem["rs_r"].at[k, color, s, index],
                    to,
                ).start()

    def scatter_next(k, s):
        for color in range(2):
            for index, block in scatter_blocks(k, color, s, False):
                got = rx_slot(k, color, s, index)
                wait_bytes(got, sem["rs_r"].at[k, color, s, index])
                block[...] = (block[...].astype(F32) + got[...].astype(F32)).astype(BF16)
        if s + 1 < bit_count:
            scatter_step(k, s + 1)
        else:
            scatter_z(k)

    def scatter_z_blocks(k):
        for color in range(2):
            for slot in range(half):
                to_z = half * c + slot
                block = wts.at[place[k], slot, shard_rows(p, color)]
                yield color, slot, to_z, block, same(color, to_z)

    def scatter_z(k):
        for color, slot, to_z, block, is_self in scatter_z_blocks(k):
            send_or_copy(
                is_self,
                block,
                zrx.at[k, z],
                sem["rz_s"].at[k, color, slot],
                sem["rz_r"].at[k, z],
                device(p, color, to_z),
            )

    def scatter_finish(k):
        for source in range(depth):
            wait_bytes(zrx.at[k, source], sem["rz_r"].at[k, source])
        total = zrx[k, 0].astype(F32)
        for source in range(1, depth):
            total = total + zrx[k, source].astype(F32)
        g_out[k] = total

    def scatter_sent(k):
        for color in range(2):
            for s in range(bit_count):
                for index, block in scatter_blocks(k, color, s, True):
                    wait_bytes(block, sem["rs_s"].at[k, color, s, index])
        for color, slot, to_z, block, is_self in scatter_z_blocks(k):
            wait_send(is_self, block, sem["rz_s"].at[k, color, slot])

    def pair_send(index, buffer):
        own = buffer.at[pl.ds(mine, own_rows)]
        remote(own, own, sem["pa_s"].at[index], sem["pa_r"].at[index], buddy).start()

    def pair_landed(index, buffer):
        wait_bytes(buffer.at[pl.ds(theirs, own_rows)], sem["pa_r"].at[index])

    def pair_sent(index, buffer):
        wait_bytes(buffer.at[pl.ds(mine, own_rows)], sem["pa_s"].at[index])

    def part_send(index):
        remote(
            prs.at[index % 2],
            prr.at[index % 2],
            sem["pr_s"].at[index],
            sem["pr_r"].at[index],
            buddy,
        ).start()

    def part_landed(index):
        wait_bytes(prr.at[index % 2], sem["pr_r"].at[index])

    def part_sent(index):
        wait_bytes(prs.at[index % 2], sem["pr_s"].at[index])

    def each_half(body, second=None):
        def step(i, carry):
            if second is not None:
                pl.when(i == 1)(second)
            body(pl.multiple_of(jnp.where(i == 0, mine, theirs), own_rows))
            return carry

        lax.fori_loop(0, 2, step, 0)

    def own_chunks(body):
        def step(i, carry):
            body(i, pl.multiple_of(i * TILE, TILE), pl.multiple_of(mine + i * TILE, TILE))
            return carry

        lax.fori_loop(0, chunks, step, 0)

    entry_barrier()
    send_small()
    gather_z(0)
    gather_z(1)
    send_rows(0, tok)
    gather_z(2)
    send_rows(1, cot)

    for h in range(6):
        qtz[h, HD * (1 - h % 2) : HD * (1 - h % 2) + HD, :] = jnp.zeros((HD, rows), BF16)
    gsum[...] = jnp.zeros(gsum.shape, F32)
    finish_small()
    gain_first = gbuf[0, 0:1, :]
    gain_second = gbuf[0, 1:2, :]

    micro = z // 2
    owner = z % 2
    query_image = code[owner, pl.ds(micro, 1), :]
    key_code = code[owner, pl.ds(2 + micro, 1), :]
    key_columns = jnp.broadcast_to(key_code, (128, rows)).T
    for block in range(rows // 128):
        span = slice(128 * block, 128 * block + 128)
        key = key_columns[span, 0:1]
        row_id = lax.broadcasted_iota(jnp.int32, (128, rows), 0) + 128 * block
        col_id = lax.broadcasted_iota(jnp.int32, (128, rows), 1)
        seen = jnp.logical_or(key == query_image, row_id == col_id)
        bias[span, :] = jnp.where(seen, 0.0, NEGATIVE).astype(BF16)

    after_z(0)
    gather_next(0, 0)
    after_z(1)
    rows_landed(0)

    def first_norm(i, at, base):
        normed, _ = normalize(xb[i].astype(F32))
        ab[pl.ds(base, TILE), :] = (normed * gain_first).astype(BF16)

    own_chunks(first_norm)
    pair_send(0, ab)
    for s in range(1, bit_count):
        gather_next(0, s)

    def roll(value):
        return pltpu.roll(value, HD, 1)

    for name, offset in (("q", 0), ("k", 384), ("v", 768), ("o", 1152)):
        tile = {"q": 0, "k": 128, "v": 256, "o": 640}[name]
        wq[:, offset : offset + 128] = wts[0, 0, :, tile : tile + 128]
        wq[:, offset + 128 : offset + 256] = wts[0, 1, :, tile : tile + 128]
        mixed = {"q": 384, "k": 384, "v": 512, "o": 512}[name]
        one = wts[0, 0, :, mixed : mixed + 128].astype(F32)
        two = wts[0, 1, :, mixed : mixed + 128].astype(F32)
        if name in ("q", "v"):
            both = jnp.where(low, one, roll(two))
        else:
            both = jnp.where(low, roll(one), two)
        wq[:, offset + 256 : offset + 384] = both.astype(BF16)

    def project(base):
        span = pl.ds(base, own_rows)
        source = ab[span, :]
        for part in range(3):
            result = dot(source, wq[:, 384 * part : 384 * part + 384])
            if part == 0:
                result = result * SCALE
            qkv[span, 384 * part : 384 * part + 384] = result.astype(BF16)
            turned = result.T.astype(BF16)
            if part == 0:
                for h in range(6):
                    at = HD * (h % 2)
                    qtz[h, at : at + HD, span] = turned[HD * h : HD * h + HD]
            elif part == 1:
                kt[:, span] = turned
            else:
                vt[:, span] = turned

    each_half(project, lambda: pair_landed(0, ab))

    def attend(base, hook):
        span = pl.ds(base, own_rows)
        for h in range(6):
            pair = h // 2
            keys = qkv[:, 384 + 128 * pair : 512 + 128 * pair]
            scores = dot(keys, qtz[h, :, span]) + bias[:, span].astype(F32)
            highest = jnp.max(scores, axis=0, keepdims=True)
            exponent = jnp.exp(scores - highest)
            total = jnp.sum(exponent, axis=0, keepdims=True)
            rounded = (exponent * (1.0 / total)).astype(BF16)
            pt[h, :, span] = rounded
            mixed = dot(vt[HD * h : HD * h + HD, :], rounded)
            ott[HD * h : HD * h + HD, span] = mixed.astype(BF16)
            hook(h)
        orow[span, :] = ott[:, span].T

    def attend_loop(i, carry):
        base = pl.multiple_of(jnp.where(i == 0, theirs, mine), own_rows)

        def hook(h):
            if h == 2:

                @pl.when(i == 0)
                def _():
                    gather_next(1, 0)

                @pl.when(i == 1)
                def _():
                    after_z(2)

        attend(base, hook)
        return carry

    lax.fori_loop(0, 2, attend_loop, 0)
    out_weight = wq[:, 1152:1536]
    prs[0] = dot_nt(orow[pl.ds(theirs, own_rows), :], out_weight).astype(BF16)
    part_send(0)

    def own_out(i, at, base):
        mid[pl.ds(at, TILE), :] = dot_nt(orow[pl.ds(base, TILE), :], wq[:, 1152:1536])

    own_chunks(own_out)
    part_landed(0)

    def second_norm(i, at, base):
        here = pl.ds(at, TILE)
        middle = xb[i].astype(F32) + (mid[here, :] + prr[0, here, :].astype(F32))
        mid[here, :] = middle
        normed, _ = normalize(middle)
        bnb[pl.ds(base, TILE), :] = (normed * gain_second).astype(BF16)

    own_chunks(second_norm)
    pair_send(1, bnb)
    for s in range(1, bit_count):
        gather_next(1, s)
    gather_next(2, 0)

    def expand(base):
        def chunk(i, carry):
            span = pl.ds(pl.multiple_of(base + i * TILE, TILE), TILE)
            source = bnb[span, :]
            for j in range(half):
                pre = dot(source, wts[1, j])
                cdf = 0.5 * (1.0 + lax.erf(pre * 0.7071067811865476))
                density = jnp.exp(pre * pre * -0.5) * 0.3989422804014327
                gact[j, span, :] = (pre * cdf).astype(BF16)
                dgel[j, span, :] = (cdf + pre * density).astype(BF16)
            return carry

        lax.fori_loop(0, chunks, chunk, 0)

    each_half(expand, lambda: pair_landed(1, bnb))
    rows_landed(1)
    pair_send(2, dyb)
    gather_sent(0)

    def grad_tiles(source, slot, width_of):
        def tile(t, carry):
            at = pl.multiple_of(t * TILE, TILE)
            turned = source[:, pl.ds(at, TILE)].T
            width_of(turned, slot, pl.ds(at, TILE))
            return carry

        lax.fori_loop(0, D // TILE, tile, 0)

    def down_tile(turned, slot, span):
        for j in range(half):
            wts[slot, j, span, :] = dot(turned, gact[j]).astype(BF16)

    def up_tile(turned, slot, span):
        for j in range(half):
            wts[slot, j, span, :] = dot(turned, dgel[j]).astype(BF16)

    pair_landed(2, dyb)
    grad_tiles(dyb, place[2], down_tile)
    scatter_step(2, 0)
    for s in range(1, bit_count):
        gather_next(2, s)

    def contract(base, j_refs, weight):
        total = dot_nt(j_refs[0, pl.ds(base, TILE), :], wts[weight, 0])
        for j in range(1, half):
            total = total + dot_nt(j_refs[j, pl.ds(base, TILE), :], wts[weight, j])
        return total

    def their_chunks(buffer, weight, into):
        def step(i, carry):
            base = pl.multiple_of(theirs + i * TILE, TILE)
            into[pl.ds(pl.multiple_of(i * TILE, TILE), TILE), :] = contract(
                base, buffer, weight
            ).astype(BF16)
            return carry

        lax.fori_loop(0, chunks, step, 0)

    their_chunks(gact, 2, prs.at[1])
    part_send(1)

    def through_gelu(base):
        def chunk(i, carry):
            span = pl.ds(pl.multiple_of(base + i * TILE, TILE), TILE)
            source = dyb[span, :]
            for j in range(half):
                grad_act = dot(source, wts[2, j])
                dgel[j, span, :] = (grad_act * dgel[j, span, :].astype(F32)).astype(BF16)
            return carry

        lax.fori_loop(0, chunks, chunk, 0)

    each_half(through_gelu)
    part_sent(0)
    their_chunks(dgel, 1, prs.at[0])
    part_landed(1)

    def layer_rows(i, at, base):
        here = pl.ds(at, TILE)
        total = contract(base, gact, 2) + prr[1, here, :].astype(F32)
        stage[i] = (mid[here, :] + total).astype(BF16)

    own_chunks(layer_rows)
    part_send(2)
    send_back(0, y_out)
    pair_sent(2, dyb)
    part_landed(2)

    def second_back(i, at, base):
        here = pl.ds(at, TILE)
        grad = contract(base, dgel, 1) + prr[0, here, :].astype(F32)
        normed, inverse = normalize(mid[here, :])
        gsum[1:2, :] += jnp.sum(grad * normed, axis=0, keepdims=True)
        down = dyb[pl.ds(base, TILE), :].astype(F32) + norm_back(
            grad, gain_second, normed, inverse
        )
        mid[here, :] = down
        dyb[pl.ds(base, TILE), :] = down.astype(BF16)

    own_chunks(second_back)
    pair_send(3, dyb)
    gather_sent(1)
    grad_tiles(bnb, place[1], up_tile)
    scatter_step(1, 0)
    scatter_next(2, 0)

    def spread_mix(base):
        span = pl.ds(base, own_rows)
        result = dot(dyb[span, :], wq[:, 1152:1536])
        dorow[span, :] = result.astype(BF16)
        turned = result.T.astype(BF16)
        for h in range(6):
            at = HD * (h % 2)
            piece = turned[HD * h : HD * h + HD]
            qtz[h, at : at + HD, span] = piece
            product = piece.astype(F32) * ott[HD * h : HD * h + HD, span].astype(F32)
            delta[h, :, span] = jnp.sum(product, axis=0, keepdims=True)

    each_half(spread_mix, lambda: pair_landed(3, dyb))

    def attend_back(pair, carry):
        def tile(offset):
            return pl.ds(pl.multiple_of(offset + 128 * pair, 128), 128)

        parts = []
        for hh in range(2):
            h = 2 * pair + hh
            grad_values = dot(pt[h], dorow[:, tile(0)])
            for q in range(rows // own_rows):
                span = slice(q * own_rows, (q + 1) * own_rows)
                grad_prob = dot(qkv[:, tile(768)], qtz[h, :, span])
                chance = pt[h, :, span].astype(F32)
                pt[h, :, span] = (chance * (grad_prob - delta[h, :, span])).astype(BF16)
            grad_keys = dot(pt[h], qkv[:, tile(0)])
            head = pl.ds(pl.multiple_of(HD * h, HD), HD)
            grad_queries = dot(kt[head, :], pt[h]) * SCALE
            parts.append((grad_queries, grad_keys, grad_values))
        qkv[:, tile(768)] = jnp.where(low, parts[0][2], parts[1][2]).astype(BF16)
        qkv[:, tile(384)] = jnp.where(low, parts[0][1], parts[1][1]).astype(BF16)
        turned = jnp.concatenate([parts[0][0], parts[1][0]], axis=0).T
        qkv[:, tile(0)] = turned.astype(BF16)

        @pl.when(pair == 0)
        def _():
            for s in range(1, bit_count):
                scatter_next(2, s)

        @pl.when(pair == 1)
        def _():
            scatter_next(1, 0)

        @pl.when(pair == 2)
        def _():
            for s in range(1, bit_count):
                scatter_next(1, s)

        return carry

    lax.fori_loop(0, 3, attend_back, 0)

    gather_sent(2)

    def first_tiles(t, carry):
        at = pl.multiple_of(t * TILE, TILE)
        span = pl.ds(at, TILE)
        slot = place[0]
        qkv_part = dot(ab[:, span].T, qkv[...])
        out_part = dot(dyb[:, span].T, orow[...])
        for i, target in ((0, 0), (1, 128), (2, 256)):
            for j in range(2):
                at = 384 * i + 128 * j
                wts[slot, j, span, target : target + 128] = qkv_part[:, at : at + 128].astype(BF16)
        for j in range(2):
            wts[slot, j, span, 640:768] = out_part[:, 128 * j : 128 * j + 128].astype(BF16)
        mixed_q = qkv_part[:, 256:384]
        mixed_k = qkv_part[:, 640:768]
        mixed_v = qkv_part[:, 1024:1152]
        mixed_o = out_part[:, 256:384]
        wts[slot, 0, span, 384:512] = jnp.where(low, mixed_q, roll(mixed_k)).astype(BF16)
        wts[slot, 1, span, 384:512] = jnp.where(low, roll(mixed_q), mixed_k).astype(BF16)
        wts[slot, 0, span, 512:640] = jnp.where(low, mixed_v, roll(mixed_o)).astype(BF16)
        wts[slot, 1, span, 512:640] = jnp.where(low, roll(mixed_v), mixed_o).astype(BF16)
        return carry

    lax.fori_loop(0, D // TILE, first_tiles, 0)
    scatter_step(0, 0)

    def first_contract(base, size):
        return dot_nt(qkv[pl.ds(base, size), :], wq[:, 0:1152])

    part_sent(1)
    prs[1] = first_contract(theirs, own_rows).astype(BF16)
    part_send(3)
    back_sent(0)
    back_landed(0, y_out)
    part_landed(3)

    def first_back(i, at, base):
        here = pl.ds(at, TILE)
        grad = first_contract(base, TILE) + prr[1, here, :].astype(F32)
        normed, inverse = normalize(xb[i].astype(F32))
        gsum[0:1, :] += jnp.sum(grad * normed, axis=0, keepdims=True)
        result = mid[here, :] + norm_back(grad, gain_first, normed, inverse)
        stage[i] = result.astype(BF16)

    own_chunks(first_back)
    send_back(1, dx_out)

    me = 2 * z + c
    for index, (cc, zz) in enumerate(column_peers):
        remote(
            gsum,
            sum_rx.at[me],
            sem["sum_s"].at[index],
            sem["sum_r"].at[me],
            device(p, cc, zz),
        ).start()
    pltpu.make_async_copy(gsum, sum_rx.at[me], sem["sum_r"].at[me]).start()

    scatter_next(0, 0)
    for source in range(2 * depth):
        wait_bytes(sum_rx.at[source], sem["sum_r"].at[source])
    for index in range(len(column_peers)):
        wait_bytes(gsum, sem["sum_s"].at[index])
    total = sum_rx[0]
    for source in range(1, 2 * depth):
        total = total + sum_rx[source]
    gsum[...] = total
    for index, pp in enumerate(plane_peers):
        remote(
            gsum, all_rx.at[p], sem["all_s"].at[index], sem["all_r"].at[p], device(pp, c, z)
        ).start()
    pltpu.make_async_copy(gsum, all_rx.at[p], sem["all_r"].at[p]).start()
    scatter_finish(2)
    scatter_finish(1)
    for source in range(columns):
        wait_bytes(all_rx.at[source], sem["all_r"].at[source])
    for index in range(len(plane_peers)):
        wait_bytes(gsum, sem["all_s"].at[index])
    total = all_rx[0]
    for source in range(1, columns):
        total = total + all_rx[source]
    gm_out[...] = total
    for s in range(1, bit_count):
        scatter_next(0, s)
    scatter_finish(0)

    back_landed(1, dx_out)
    back_sent(1)
    rows_sent(0, tok)
    rows_sent(1, cot)
    pair_sent(0, ab)
    pair_sent(1, bnb)
    pair_sent(3, dyb)
    part_sent(2)
    part_sent(3)
    for k in range(KINDS):
        scatter_sent(k)


def whole_layer(mesh, tok, cot, packed, gains, codes):
    depth = mesh.shape["tensor"]
    bit_count = (mesh.shape["dp"] // 2).bit_length() - 1
    columns = 1 << bit_count
    shard = packed.shape[1]
    half = depth // 2
    rows = codes.shape[1]
    own = rows // 2
    vmem = pl.BlockSpec(memory_space=pltpu.VMEM)
    hbm = pl.BlockSpec(memory_space=pl.ANY)
    sem = pltpu.SemaphoreType.DMA
    blocks = 1 << (bit_count - 1)
    scratch = [
        ((half, TILE, D), BF16),
        ((rows, D), BF16),
        ((rows, D), BF16),
        ((rows, D), BF16),
        ((KINDS, half, D, D), BF16),
        ((D, 2 * D), BF16),
        ((rows, 1152), BF16),
        ((6, 128, rows), BF16),
        ((384, rows), BF16),
        ((384, rows), BF16),
        ((6, rows, rows), BF16),
        ((rows, rows), BF16),
        ((384, rows), BF16),
        ((rows, 384), BF16),
        ((rows, 384), BF16),
        ((own, D), F32),
        ((half, rows, D), BF16),
        ((half, rows, D), BF16),
        ((2, own, D), BF16),
        ((2, own, D), BF16),
        ((half, TILE, D), BF16),
        ((KINDS, 2, columns - 1, half, shard, D), BF16),
        ((KINDS, depth, shard, D), BF16),
        ((2 * columns, 8, D), F32),
        ((2,) + codes.shape, F32),
        ((8, D), F32),
        ((2 * depth, 8, D), F32),
        ((columns, 8, D), F32),
        ((6, 1, rows), F32),
    ]
    sems = {
        "tok_s": (2, 2),
        "tok_r": (2, half),
        "gain_s": (2 * columns,),
        "gain_r": (2 * columns,),
        "code_s": (),
        "code_l": (),
        "code_r": (),
        "z_s": (KINDS, depth),
        "z_r": (KINDS, 2, half),
        "rel_s": (KINDS, 2),
        "x_s": (KINDS, 2, bit_count, blocks),
        "x_r": (KINDS, 2, bit_count, blocks),
        "rs_s": (KINDS, 2, bit_count, blocks),
        "rs_r": (KINDS, 2, bit_count, blocks),
        "rz_s": (KINDS, 2, half),
        "rz_r": (KINDS, depth),
        "out_s": (2, half),
        "out_r": (2, 2),
        "pa_s": (4,),
        "pa_r": (4,),
        "pr_s": (4,),
        "pr_r": (4,),
        "sum_s": (2 * depth - 1,),
        "sum_r": (2 * depth,),
        "all_s": (columns - 1,),
        "all_r": (columns,),
    }
    return pl.pallas_call(
        functools.partial(layer_kernel, depth, bit_count, shard, rows),
        out_shape=(
            jax.ShapeDtypeStruct(tok.shape, BF16),
            jax.ShapeDtypeStruct(tok.shape, BF16),
            jax.ShapeDtypeStruct(packed.shape, F32),
            jax.ShapeDtypeStruct((8, D), F32),
        ),
        in_specs=[hbm, hbm, hbm, vmem, vmem],
        out_specs=(hbm, hbm, vmem, vmem),
        scratch_shapes=[pltpu.VMEM(shape, dtype) for shape, dtype in scratch]
        + [sem(sems[name]) for name in SEMS],
        compiler_params=pltpu.CompilerParams(
            collective_id=0, has_side_effects=True, vmem_limit_bytes=67043328
        ),
        name="whole_layer",
    )(tok, cot, packed, gains, codes)


def block_body(mesh, tokens, cotangent, lengths, padding, ln_gain, w_qkv, w_out, w_up, w_down):
    depth = mesh.shape["tensor"]
    dp = lax.axis_index("dp")
    z = lax.axis_index("tensor")
    shard = w_up.shape[1]
    width = w_qkv.shape[3]
    pair = 2 * HD

    qkv = w_qkv[0]
    out_t = w_out[0].T
    packed = jnp.stack(
        [
            jnp.concatenate(
                [
                    qkv[:, 0, :pair],
                    qkv[:, 1, :pair],
                    qkv[:, 2, :pair],
                    qkv[:, 0, pair:],
                    qkv[:, 1, pair:],
                    qkv[:, 2, pair:],
                    out_t[:, pair:],
                    out_t[:, :pair],
                ],
                axis=1,
            ),
            w_up[0],
            w_down[0].T,
        ]
    )
    gain_rows = jnp.zeros((8, D), F32)
    gain_rows = lax.dynamic_update_slice(gain_rows, ln_gain[0].astype(F32), (0, dp * shard))
    places = lax.iota(jnp.int32, padding.shape[1])
    bounds = jnp.cumsum(lengths[:, 0], axis=1)
    picture = jnp.sum((places[None, :, None] >= bounds[:, None, :]).astype(jnp.int32), axis=2)
    key_code = jnp.where(padding == 1, picture, -1)
    codes = jnp.concatenate([picture, key_code, picture, picture], axis=0).astype(F32)

    y_back, dx_back, summed, gain_sum = whole_layer(
        mesh, tokens, cotangent, packed, gain_rows, codes
    )
    part = 2 * D // (mesh.shape["dp"] * depth)
    gain_result = lax.dynamic_slice(gain_sum[:2].reshape(-1), ((dp * depth + z) * part,), (part,))
    first = summed[0]
    qkv_grad = jnp.stack(
        [
            jnp.concatenate(
                [
                    first[:, pair * i : pair * i + pair],
                    first[:, 3 * pair + HD * i : 3 * pair + HD * i + HD],
                ],
                axis=1,
            )
            for i in range(3)
        ],
        axis=1,
    )[None]
    out_grad = jnp.concatenate([first[:, 5 * pair :], first[:, 4 * pair + HD : 5 * pair]], axis=1)
    return (
        y_back.astype(F32),
        dx_back.astype(F32),
        gain_result,
        qkv_grad,
        out_grad.T[None],
        summed[1][None],
        summed[2].T[None],
    )


def visible(lengths_row, padding_row):
    places = lax.iota(jnp.int32, padding_row.shape[0])
    bounds = jnp.cumsum(lengths_row)
    picture = jnp.sum((places[:, None] >= bounds[None, :]).astype(jnp.int32), axis=1)
    same_image = picture[:, None] == picture[None, :]
    return same_image & ((padding_row[None, :] == 1) | (places[:, None] == places[None, :]))


def gelu_exact(pre_values):
    return jax.nn.gelu(pre_values, approximate=False)


def masked_scores(queries, key_rows, allowed):
    scaling = queries.shape[-1] ** (-0.5)
    scores = (
        jnp.einsum("qhd,khd->hqk", queries, key_rows, preferred_element_type=jnp.float32) * scaling
    )
    return (jnp.where(allowed[None], scores, NEGATIVE), scaling)


def attend(stacked, allowed):
    scores, scaling = masked_scores(stacked[:, 0], stacked[:, 1], allowed)
    highest = jnp.max(scores, axis=-1, keepdims=True)
    exponent = jnp.exp(scores - highest)
    totals = jnp.sum(exponent, axis=-1, keepdims=True)
    rounded = (exponent / totals).astype(jnp.bfloat16)
    mixture = jnp.einsum("hqk,khd->qhd", rounded, stacked[:, 2], preferred_element_type=jnp.float32)
    return (mixture, highest, totals)


def attend_back(stacked, allowed, highest, totals, grad_mix):
    queries, key_rows, value_rows = (stacked[:, 0], stacked[:, 1], stacked[:, 2])
    scores, scaling = masked_scores(queries, key_rows, allowed)
    probability = jnp.exp(scores - highest) / totals
    rounded = probability.astype(jnp.bfloat16)
    grad_prob = jnp.einsum("qhd,khd->hqk", grad_mix, value_rows, preferred_element_type=jnp.float32)
    grad_values = jnp.einsum("hqk,qhd->khd", rounded, grad_mix, preferred_element_type=jnp.float32)
    inner_sum = jnp.sum(probability * grad_prob, axis=-1, keepdims=True)
    grad_scores = (probability * (grad_prob - inner_sum)).astype(jnp.bfloat16)
    grad_queries = (
        jnp.einsum("hqk,khd->qhd", grad_scores, key_rows, preferred_element_type=jnp.float32)
        * scaling
    )
    grad_keys = (
        jnp.einsum("hqk,qhd->khd", grad_scores, queries, preferred_element_type=jnp.float32)
        * scaling
    )
    return jnp.stack([grad_queries, grad_keys, grad_values], axis=1).astype(jnp.bfloat16)


def collect_weights(ln_gain, w_qkv, w_out, w_up, w_down, layer_index):
    return (
        lax.all_gather(ln_gain[layer_index], "dp", axis=1, tiled=True),
        lax.all_gather(w_qkv[layer_index], "dp", axis=0, tiled=True),
        lax.all_gather(w_out[layer_index], "dp", axis=1, tiled=True),
        lax.all_gather(w_up[layer_index], "dp", axis=0, tiled=True),
        lax.all_gather(w_down[layer_index], "dp", axis=1, tiled=True),
    )


def spread(block_rows):
    return lax.all_gather(block_rows, "tensor", axis=0, tiled=True)


def spread_grad(block_rows):
    return lax.all_gather(block_rows, "tensor", axis=0, tiled=True)


def collect_rows(operand, weight):
    return lax.psum_scatter(
        jnp.dot(operand, weight, preferred_element_type=jnp.float32),
        "tensor",
        scatter_dimension=0,
        tiled=True,
    )


def return_rows(operand, weight):
    return lax.psum_scatter(
        lax.dot_general(
            operand, weight, (((1,), (1,)), ((), ())), preferred_element_type=jnp.float32
        ),
        "tensor",
        scatter_dimension=0,
        tiled=True,
    )


def reduce_grads(pieces):
    return (
        lax.psum_scatter(pieces[0], "dp", scatter_dimension=0, tiled=True),
        lax.psum_scatter(pieces[1], "dp", scatter_dimension=1, tiled=True),
        lax.psum_scatter(pieces[2], "dp", scatter_dimension=0, tiled=True),
        lax.psum_scatter(pieces[3], "dp", scatter_dimension=1, tiled=True),
    )


def body(tokens, cotangent, lengths, padding, ln_gain, w_qkv, w_out, w_up, w_down):
    layer_count = w_qkv.shape[0]
    micro_count = tokens.shape[0]
    residual = [tokens[batch_index].astype(jnp.float32) for batch_index in range(micro_count)]
    visibility = [
        visible(lengths[batch_index, 0], padding[batch_index]) for batch_index in range(micro_count)
    ]
    saved = []
    stored_weights = []
    layer_index = 0
    stored_weights.append(None)
    for batch_index in range(micro_count):
        weights = collect_weights(ln_gain, w_qkv, w_out, w_up, w_down, layer_index)
        gain_pair, qkv_weight, out_weight, up_weight, down_weight = weights
        gain_first = gain_pair[0].astype(jnp.float32)
        gain_second = gain_pair[1].astype(jnp.float32)
        entering = residual[batch_index]
        normed, inverse = normalize(entering)
        first_input = spread((normed * gain_first).astype(jnp.bfloat16))
        triple = jnp.einsum(
            "rd,dcn->rcn", first_input, qkv_weight, preferred_element_type=jnp.float32
        ).astype(jnp.bfloat16)
        stacked = triple.reshape(triple.shape[0], 3, -1, HD)
        mixture, highest, totals = attend(stacked, visibility[batch_index])
        mix_rounded = mixture.reshape(mixture.shape[0], -1).astype(jnp.bfloat16)
        middle = entering + collect_rows(mix_rounded, out_weight)
        normed_two, inverse_two = normalize(middle)
        second_input = spread((normed_two * gain_second).astype(jnp.bfloat16))
        hidden_pre = jnp.dot(second_input, up_weight, preferred_element_type=jnp.float32)
        activated = gelu_exact(hidden_pre).astype(jnp.bfloat16)
        residual[batch_index] = middle + collect_rows(activated, down_weight)
        saved.append(
            (
                entering,
                first_input,
                stacked,
                highest,
                totals,
                mix_rounded,
                middle,
                second_input,
                hidden_pre,
                activated,
            )
        )
    gradients = [cotangent[batch_index].astype(jnp.float32) for batch_index in range(micro_count)]
    gain_parts = [jnp.zeros((2, D), jnp.float32)]
    weight_results = [None]
    for layer_index in reversed(range(layer_count)):
        summed = None
        for batch_index in range(micro_count):
            weights = collect_weights(ln_gain, w_qkv, w_out, w_up, w_down, layer_index)
            gain_pair, qkv_weight, out_weight, up_weight, down_weight = weights
            gain_first = gain_pair[0].astype(jnp.float32)
            gain_second = gain_pair[1].astype(jnp.float32)
            (
                entering,
                first_input,
                stacked,
                highest,
                totals,
                mix_rounded,
                middle,
                second_input,
                hidden_pre,
                activated,
            ) = saved[layer_index * micro_count + batch_index]
            incoming = gradients[batch_index]
            grad_down = spread_grad(incoming.astype(jnp.bfloat16))
            down_part = jnp.einsum(
                "rf,rd->fd", activated, grad_down, preferred_element_type=jnp.float32
            )
            grad_act = lax.dot_general(
                grad_down, down_weight, (((1,), (1,)), ((), ())), preferred_element_type=jnp.float32
            )
            pulled = jax.vjp(gelu_exact, hidden_pre)
            grad_pre = pulled[1](grad_act)[0].astype(jnp.bfloat16)
            up_part = jnp.einsum(
                "rd,rf->df", second_input, grad_pre, preferred_element_type=jnp.float32
            )
            grad_norm_two = return_rows(grad_pre, up_weight)
            normed_two, inverse_two = normalize(middle)
            gain_two_part = jnp.sum(grad_norm_two * normed_two, axis=0)
            incoming = incoming + norm_back(grad_norm_two, gain_second, normed_two, inverse_two)
            grad_branch = spread_grad(incoming.astype(jnp.bfloat16))
            out_part = jnp.einsum(
                "rk,rd->kd", mix_rounded, grad_branch, preferred_element_type=jnp.float32
            )
            grad_mix = lax.dot_general(
                grad_branch,
                out_weight,
                (((1,), (1,)), ((), ())),
                preferred_element_type=jnp.float32,
            )
            grad_mix = grad_mix.astype(jnp.bfloat16).reshape(grad_mix.shape[0], -1, HD)
            grad_triple = attend_back(stacked, visibility[batch_index], highest, totals, grad_mix)
            flat_triple = grad_triple.reshape(grad_triple.shape[0], 3, -1)
            qkv_part = jnp.einsum(
                "rd,rcn->dcn", first_input, flat_triple, preferred_element_type=jnp.float32
            )
            grad_norm_one = return_rows(
                flat_triple.reshape(flat_triple.shape[0], -1),
                qkv_weight.reshape(qkv_weight.shape[0], -1),
            )
            normed, inverse = normalize(entering)
            gain_one_part = jnp.sum(grad_norm_one * normed, axis=0)
            incoming = incoming + norm_back(grad_norm_one, gain_first, normed, inverse)
            gradients[batch_index] = incoming
            gain_parts[layer_index] = gain_parts[layer_index] + jnp.stack(
                [gain_one_part, gain_two_part]
            )
            pieces = (qkv_part, out_part, up_part, down_part)
            if summed is None:
                summed = pieces
            else:
                summed = tuple((older + newer for older, newer in zip(summed, pieces)))
        summed = reduce_grads(summed)
        weight_results[layer_index] = summed
    gain_flat = jnp.stack(gain_parts).reshape(-1)
    gain_result = lax.psum_scatter(gain_flat, ("dp", "tensor"), scatter_dimension=0, tiled=True)
    layer_out = jnp.stack(residual)
    input_grad = jnp.stack(gradients)
    qkv_grad = jnp.stack([weight_results[0][0]])
    out_grad = jnp.stack([weight_results[0][1]])
    up_grad = jnp.stack([weight_results[0][2]])
    down_grad = jnp.stack([weight_results[0][3]])
    return (layer_out, input_grad, gain_result, qkv_grad, out_grad, up_grad, down_grad)


def fits(mesh, tokens, w_qkv):
    dp_size, depth = mesh.shape["dp"], mesh.shape["tensor"]
    columns = dp_size // 2
    return (
        depth == 4
        and dp_size >= 4
        and columns & (columns - 1) == 0
        and D % (dp_size * 32) == 0
        and tokens.shape[0] == 2
        and tokens.shape[1] == dp_size * depth * TILE
        and w_qkv.shape[0] == 1
    )


def solution(mesh):
    def run(tokens, cotangent, lengths, padding, ln_gain, w_qkv, *rest):
        one_block = fits(mesh, tokens, w_qkv)
        program = functools.partial(block_body, mesh) if one_block else body
        return jax.shard_map(
            program,
            mesh=mesh,
            in_specs=(
                P(None, ("dp", "tensor"), None),
                P(None, ("dp", "tensor"), None),
                P(None, "dp", None),
                P(None, "dp"),
                P(None, None, "dp"),
                P(None, "dp", None, "tensor"),
                P(None, "tensor", "dp"),
                P(None, "dp", "tensor"),
                P(None, "tensor", "dp"),
            ),
            out_specs=(
                P(None, ("dp", "tensor"), None),
                P(None, ("dp", "tensor"), None),
                P(("dp", "tensor")),
                P(None, "dp", None, "tensor"),
                P(None, "tensor", "dp"),
                P(None, "dp", "tensor"),
                P(None, "tensor", "dp"),
            ),
            check_vma=False,
        )(tokens, cotangent, lengths, padding, ln_gain, w_qkv, *rest)

    return run
```

```python
import functools

import jax
import jax.numpy as jnp
from jax import lax
from jax.experimental import pallas as pl
from jax.experimental.pallas import tpu as pltpu
from jax.sharding import PartitionSpec as P

D = 768
HD = 64
NEGATIVE = -1e30
EPSILON = 1e-06
MESH = pl.DeviceIdType.MESH
F32 = jnp.float32
BF16 = jnp.bfloat16
KINDS = 3
HALF = 48
GATHER = ((0, 0, HALF), (0, HALF, HALF), (1, 0, HALF), (1, HALF, HALF), (2, 0, 2 * HALF))
SCATTER = ((2, 0, 2 * HALF), (1, 0, 2 * HALF), (0, 0, HALF), (0, HALF, HALF))
RELAYED = (2, 1, 0)
TILE = 256
SCALE = HD**-0.5


def flip(value, bit):
    size = 1 << bit
    return value + size * (1 - 2 * ((value // size) % 2))


def flip_mask(value, mask):
    bit = 0
    while mask >> bit:
        if (mask >> bit) & 1:
            value = flip(value, bit)
        bit += 1
    return value


def submasks(bits):
    masks = [0]
    for bit in bits:
        masks = masks + [mask | (1 << bit) for mask in masks]
    return masks


def color_order(color, bit_count):
    order = list(range(bit_count))
    return order if color == 0 else order[::-1]


def device(p, c, z):
    return (2 * p + c, z)


def dot(left, right):
    return jnp.dot(left, right, preferred_element_type=F32)


def dot_nt(left, right):
    return lax.dot_general(left, right, (((1,), (1,)), ((), ())), preferred_element_type=F32)


def normalize(row_block):
    average = jnp.mean(row_block, axis=-1, keepdims=True)
    centred = row_block - average
    variance = jnp.mean(centred * centred, axis=-1, keepdims=True)
    inverse = lax.rsqrt(variance + EPSILON)
    return (centred * inverse, inverse)


def norm_back(grad_out, gain_row, normed, inverse):
    scaled = grad_out * gain_row
    mean_grad = jnp.mean(scaled, axis=-1, keepdims=True)
    second = jnp.mean(scaled * normed, axis=-1, keepdims=True)
    return inverse * (scaled - mean_grad - normed * second)


def remote(source, target, send_sem, recv_sem, dest):
    return pltpu.make_async_remote_copy(
        source, target, send_sem, recv_sem, device_id=dest, device_id_type=MESH
    )


def wait_bytes(ref, sem):
    pltpu.make_async_copy(ref, ref, sem).wait()


SEMS = (
    "tok_s",
    "tok_r",
    "gain_s",
    "gain_r",
    "code_s",
    "code_r",
    "z_s",
    "z_r",
    "rel_s",
    "x_s",
    "x_r",
    "rs_s",
    "rs_r",
    "rz_s",
    "rz_r",
    "far_r",
    "out_s",
    "out_r",
    "pa_s",
    "pa_r",
    "pr_s",
    "pr_r",
    "sum_s",
    "sum_r",
    "all_s",
    "all_r",
)


def layer_kernel(depth, bit_count, shard, rows, *refs):
    (tok, cot, first_in, up_in, down_in, gain_in, pad_in, length_in) = refs[:8]
    (y_out, dx_out, g_out, gm_out) = refs[8:12]
    (
        xb,
        dyb,
        ab,
        bnb,
        wts,
        wq,
        qkv,
        qtz,
        vt,
        kt,
        pt,
        bias,
        ott,
        orow,
        dorow,
        mid,
        gact,
        dgel,
        prs,
        prr,
        stage,
        rx,
        zrx,
        far_rx,
        gbuf,
        gains,
        code,
        gsum,
        sum_rx,
        all_rx,
        delta,
    ) = refs[12:43]
    sem = dict(zip(SEMS, refs[43:]))
    half = depth // 2
    columns = 1 << bit_count
    own_rows = rows // 2
    chunks = own_rows // TILE
    dp = lax.axis_index("dp")
    z = lax.axis_index("tensor")
    c = dp % 2
    p = dp // 2
    buddy = device(p, 1 - c, z)
    mine = pl.multiple_of(own_rows * c, own_rows)
    theirs = pl.multiple_of(own_rows * (1 - c), own_rows)
    lane = lax.broadcasted_iota(jnp.int32, (1, 128), 1)
    low = lane < HD

    def same(to_c, to_z):
        return jnp.logical_and(to_c == c, to_z == z)

    def send_or_copy(is_self, source, target, send_sem, recv_sem, dest):
        @pl.when(is_self)
        def _():
            pltpu.make_async_copy(source, target, recv_sem).start()

        @pl.when(jnp.logical_not(is_self))
        def _():
            remote(source, target, send_sem, recv_sem, dest).start()

    def wait_send(is_self, source, send_sem):
        @pl.when(jnp.logical_not(is_self))
        def _():
            wait_bytes(source, send_sem)

    column_peers = []
    for dz in range(depth):
        for dc in range(2):
            if dz or dc:
                column_peers.append((c if dc == 0 else 1 - c, (z + dz) % depth))
    plane_peers = [flip_mask(p, mask) for mask in range(1, columns)]

    def entry_barrier():
        barrier = pltpu.get_barrier_semaphore()
        peers = [device(p, cc, zz) for cc, zz in column_peers]
        peers += [device(pp, c, z) for pp in plane_peers]
        peers += [device(pp, 1 - c, z) for pp in plane_peers]
        for peer in peers:
            pl.semaphore_signal(barrier, inc=1, device_id=peer, device_id_type=MESH)
        pl.semaphore_wait(barrier, len(peers))

    def make_small():
        gbuf[dp] = jnp.zeros(gbuf.shape[1:], F32)
        gbuf[dp, 0:2, 0:shard] = gain_in[...].astype(F32)
        places = lax.broadcasted_iota(jnp.int32, (1, rows), 1)
        for m in range(2):
            image = jnp.zeros((1, rows), jnp.int32)
            bound = 0
            for k in range(length_in.shape[1]):
                bound = bound + length_in[m, k]
                image = image + (places >= bound).astype(jnp.int32)
            key = jnp.where(pad_in[m : m + 1, :] == 1, image, -1)
            code[c, m : m + 1, :] = image.astype(F32)
            code[c, 2 + m : 3 + m, :] = key.astype(F32)

    def send_small():
        remote(code.at[c], code.at[c], sem["code_s"], sem["code_r"], buddy).start()
        index = 0
        for pp in [p] + plane_peers:
            for cc in (c, 1 - c):
                if index:
                    remote(
                        gbuf.at[dp],
                        gbuf.at[dp],
                        sem["gain_s"].at[index],
                        sem["gain_r"].at[dp],
                        device(pp, cc, z),
                    ).start()
                index += 1

    def finish_small():
        wait_bytes(code.at[c], sem["code_s"])
        wait_bytes(code.at[1 - c], sem["code_r"])
        index = 0
        for pp in [p] + plane_peers:
            for cc in (c, 1 - c):
                if index:
                    wait_bytes(gbuf.at[dp], sem["gain_s"].at[index])
                    source = 2 * pp + cc
                    wait_bytes(gbuf.at[source], sem["gain_r"].at[source])
                index += 1
        rest = jnp.zeros((8, D - 128), F32)
        total = jnp.zeros((8, D), F32)
        for source in range(2 * columns):
            wide = jnp.concatenate([gbuf[source], rest], axis=1)
            total = total + (pltpu.roll(wide, shard * source, 1) if source else wide)
        gains[...] = total

    def row_targets():
        for m in range(2):
            to_z, to_c = 2 * m + c, z // half
            yield m, to_c, to_z, same(to_c, to_z)

    def row_target(which, slot):
        if which == 0:
            return xb.at[slot]
        return dyb.at[pl.ds(pl.multiple_of(own_rows * c + TILE * slot, TILE), TILE)]

    def row_landing(which, slot, to_c):
        if which == 0:
            return xb.at[slot]
        return dyb.at[pl.ds(pl.multiple_of(own_rows * to_c + TILE * slot, TILE), TILE)]

    def send_rows(which, array):
        for m, to_c, to_z, is_self in row_targets():
            slot = z % half
            send_or_copy(
                is_self,
                array.at[m],
                row_landing(which, slot, to_c),
                sem["tok_s"].at[which, m],
                sem["tok_r"].at[which, slot],
                device(p, to_c, to_z),
            )

    def rows_sent(which, array):
        for m, to_c, to_z, is_self in row_targets():
            wait_send(is_self, array.at[m], sem["tok_s"].at[which, m])

    def rows_landed(which):
        for slot in range(half):
            wait_bytes(row_target(which, slot), sem["tok_r"].at[which, slot])

    def send_back(which, target):
        for slot in range(half):
            to_c, to_z = z % 2, half * c + slot
            send_or_copy(
                same(to_c, to_z),
                stage.at[slot],
                target.at[z // 2],
                sem["out_s"].at[which, slot],
                sem["out_r"].at[which, z // 2],
                device(p, to_c, to_z),
            )

    def back_sent(which):
        for slot in range(half):
            is_self = same(z % 2, half * c + slot)
            wait_send(is_self, stage.at[slot], sem["out_s"].at[which, slot])

    def back_landed(which, target):
        for m in range(2):
            wait_bytes(target.at[m], sem["out_r"].at[which, m])

    last = depth - 1

    def two_ends(low_core, high_core):
        return jnp.logical_or(
            jnp.logical_and(c == 0, z == low_core), jnp.logical_and(c == 1, z == high_core)
        )

    ends = two_ends(last, 0)
    relays = two_ends(last - 1, 1)
    relay_to = device(p, c, last * (1 - c))
    relay_from = device(p, c, last - 1 + c * (2 - last))

    def unit_rows(unit, column, color):
        _, start, size = unit
        return pl.ds(pl.multiple_of((2 * column + color) * shard + start, 16), size)

    def unit_source(unit):
        return (first_in, up_in, down_in)[unit[0]].at[pl.ds(unit[1], unit[2])]

    def z_targets():
        for dz in range(depth):
            to_z = (z + dz) % depth
            yield dz, z // half, to_z, to_z == last * (1 - z // half)

    def gather_z(u):
        unit = GATHER[u]
        for dz, to_c, to_z, far in z_targets():
            source = unit_source(unit)
            target = wts.at[unit[0], z % half, unit_rows(unit, p, c)]
            recv = sem["z_r"].at[u, c, z % half]
            if dz == 0:
                send_or_copy(
                    to_c == c, source, target, sem["z_s"].at[u, dz], recv, device(p, to_c, to_z)
                )
            else:

                @pl.when(jnp.logical_not(far))
                def _():
                    remote(
                        source, target, sem["z_s"].at[u, dz], recv, device(p, to_c, to_z)
                    ).start()

    def gather_z_sent(u):
        for dz, to_c, to_z, far in z_targets():
            skip = to_c == c if dz == 0 else far
            wait_send(skip, unit_source(GATHER[u]), sem["z_s"].at[u, dz])

    def relay_block(u, color, slot):
        unit = GATHER[u]
        return wts.at[unit[0], slot, unit_rows(unit, p, color)]

    def after_z(u):
        unit = GATHER[u]
        for color in range(2):
            for slot in range(half):
                wait_bytes(
                    wts.at[unit[0], slot, unit_rows(unit, p, color)], sem["z_r"].at[u, color, slot]
                )

        @pl.when(relays)
        def _():
            for color in range(2):
                for slot in range(half):
                    block = relay_block(u, color, slot)
                    remote(
                        block,
                        block,
                        sem["rel_s"].at[u, color, slot],
                        sem["z_r"].at[u, color, slot],
                        relay_to,
                    ).start()

        gather_step(u, 0)

    def gather_blocks(u, color, s, landed):
        unit = GATHER[u]
        order = color_order(color, bit_count)
        for index, mask in enumerate(submasks(order[:s])):
            column = flip_mask(p, mask)
            if landed:
                column = flip(column, order[s])
            yield index, wts.at[unit[0], :, unit_rows(unit, column, color)]

    def gather_step(u, s):
        for color in range(2):
            to = device(flip(p, color_order(color, bit_count)[s]), c, z)
            for index, block in gather_blocks(u, color, s, False):
                remote(
                    block,
                    block,
                    sem["x_s"].at[u, color, s, index],
                    sem["x_r"].at[u, color, s, index],
                    to,
                ).start()

    def gather_next(u, s):
        for color in range(2):
            for index, block in gather_blocks(u, color, s, True):
                wait_bytes(block, sem["x_r"].at[u, color, s, index])
        if s + 1 < bit_count:
            gather_step(u, s + 1)

    def gather_last(*units):
        for u in units:
            for s in range(1, bit_count):
                gather_next(u, s)

    def gather_sent(k):
        for u, unit in enumerate(GATHER):
            if unit[0] == k:
                gather_unit_sent(u)

    def gather_unit_sent(u):
        gather_z_sent(u)

        @pl.when(relays)
        def _():
            for color in range(2):
                for slot in range(half):
                    wait_bytes(relay_block(u, color, slot), sem["rel_s"].at[u, color, slot])

        for color in range(2):
            for s in range(bit_count):
                for index, block in gather_blocks(u, color, s, False):
                    wait_bytes(block, sem["x_s"].at[u, color, s, index])

    place = {2: 0, 1: 1, 0: 2}

    def rx_slot(u, color, s, index):
        unit = SCATTER[u]
        slot = (1 << bit_count) - (1 << (bit_count - s)) + index
        return rx.at[unit[0], color, slot, :, pl.ds(unit[1], unit[2])]

    def scatter_order(color):
        return color_order(color, bit_count)[::-1]

    def scatter_blocks(u, color, s, away):
        unit = SCATTER[u]
        order = scatter_order(color)
        for index, mask in enumerate(submasks(order[s + 1 :])):
            column = flip_mask(p, mask)
            if away:
                column = flip(column, order[s])
            yield index, wts.at[place[unit[0]], :, unit_rows(unit, column, color)]

    def scatter_step(u, s):
        for color in range(2):
            to = device(flip(p, scatter_order(color)[s]), c, z)
            for index, block in scatter_blocks(u, color, s, True):
                remote(
                    block,
                    rx_slot(u, color, s, index),
                    sem["rs_s"].at[u, color, s, index],
                    sem["rs_r"].at[u, color, s, index],
                    to,
                ).start()

    def scatter_next(u, s):
        for color in range(2):
            for index, block in scatter_blocks(u, color, s, False):
                got = rx_slot(u, color, s, index)
                wait_bytes(got, sem["rs_r"].at[u, color, s, index])
                block[...] = (block[...].astype(F32) + got[...].astype(F32)).astype(BF16)
        if s + 1 < bit_count:
            scatter_step(u, s + 1)
        else:
            scatter_z(u)

    def scatter_last(*units):
        for u in units:
            for s in range(1, bit_count):
                scatter_next(u, s)

    def scatter_z_blocks(u):
        unit = SCATTER[u]
        for color in range(2):
            for slot in range(half):
                to_z = half * c + slot
                block = wts.at[place[unit[0]], slot, unit_rows(unit, p, color)]
                yield color, slot, to_z, block

    def summed_on_the_way(u):
        return SCATTER[u][0] in RELAYED

    def landing(u, source):
        unit = SCATTER[u]
        return zrx.at[unit[0], source, pl.ds(unit[1], unit[2])]

    def far_landing(u, color, slot):
        unit = SCATTER[u]
        return far_rx.at[unit[0], color, slot, pl.ds(unit[1], unit[2])]

    def scatter_z(u):
        for color, slot, to_z, block in scatter_z_blocks(u):
            send, recv = sem["rz_s"].at[u, color, slot], sem["rz_r"].at[u, z]
            dest = device(p, color, to_z)
            if not summed_on_the_way(u):
                send_or_copy(same(color, to_z), block, landing(u, z), send, recv, dest)
                continue

            @pl.when(jnp.logical_not(jnp.logical_or(ends, relays)))
            def _():
                send_or_copy(same(color, to_z), block, landing(u, z), send, recv, dest)

            @pl.when(ends)
            def _():
                remote(
                    block,
                    far_landing(u, color, slot),
                    send,
                    sem["far_r"].at[u, color, slot],
                    relay_from,
                ).start()

    def scatter_relay(u):
        @pl.when(relays)
        def _():
            for color, slot, to_z, block in scatter_z_blocks(u):
                got = far_landing(u, color, slot)
                wait_bytes(got, sem["far_r"].at[u, color, slot])
                block[...] = (block[...].astype(F32) + got[...].astype(F32)).astype(BF16)
                send, recv = sem["rz_s"].at[u, color, slot], sem["rz_r"].at[u, z]
                dest = device(p, color, to_z)
                send_or_copy(same(color, to_z), block, landing(u, z), send, recv, dest)

    def scatter_finish(u):
        unit = SCATTER[u]
        for source in range(depth):
            got = functools.partial(wait_bytes, landing(u, source), sem["rz_r"].at[u, source])
            if summed_on_the_way(u) and source in (0, last):
                pl.when(z // half != (last - source) // half)(got)
            else:
                got()
        total = landing(u, 0)[...].astype(F32)
        for source in range(1, depth):
            total = total + landing(u, source)[...].astype(F32)
        g_out[unit[0], unit[1] : unit[1] + unit[2]] = total

    def scatter_sent(u):
        for color in range(2):
            for s in range(bit_count):
                for index, block in scatter_blocks(u, color, s, True):
                    wait_bytes(block, sem["rs_s"].at[u, color, s, index])
        for color, slot, to_z, block in scatter_z_blocks(u):
            local = same(color, to_z)
            if summed_on_the_way(u):
                local = jnp.logical_and(local, jnp.logical_not(ends))
            wait_send(local, block, sem["rz_s"].at[u, color, slot])

    def clear_far():
        for source in (0, last):

            @pl.when(z // half == (last - source) // half)
            def _():
                for k in RELAYED:
                    zrx[k, source] = jnp.zeros(zrx.shape[2:], BF16)

    def pair_send(index, buffer):
        own = buffer.at[pl.ds(mine, own_rows)]
        remote(own, own, sem["pa_s"].at[index], sem["pa_r"].at[index], buddy).start()

    def pair_landed(index, buffer):
        wait_bytes(buffer.at[pl.ds(theirs, own_rows)], sem["pa_r"].at[index])

    def pair_sent(index, buffer):
        wait_bytes(buffer.at[pl.ds(mine, own_rows)], sem["pa_s"].at[index])

    def part_send(index):
        remote(
            prs.at[index % 2],
            prr.at[index % 2],
            sem["pr_s"].at[index],
            sem["pr_r"].at[index],
            buddy,
        ).start()

    def part_landed(index):
        wait_bytes(prr.at[index % 2], sem["pr_r"].at[index])

    def part_sent(index):
        wait_bytes(prs.at[index % 2], sem["pr_s"].at[index])

    def each_half(body, second=None):
        def step(i, carry):
            if second is not None:
                pl.when(i == 1)(second)
            body(pl.multiple_of(jnp.where(i == 0, mine, theirs), own_rows))
            return carry

        lax.fori_loop(0, 2, step, 0)

    def own_chunks(body):
        def step(i, carry):
            body(i, pl.multiple_of(i * TILE, TILE), pl.multiple_of(mine + i * TILE, TILE))
            return carry

        lax.fori_loop(0, chunks, step, 0)

    make_small()
    entry_barrier()
    send_small()
    for u in range(4):
        gather_z(u)
    send_rows(0, tok)

    for h in range(6):
        qtz[h, HD * (1 - h % 2) : HD * (1 - h % 2) + HD, :] = jnp.zeros((HD, rows), BF16)
    gsum[...] = jnp.zeros(gsum.shape, F32)
    clear_far()
    after_z(0)
    finish_small()
    gain_first = gains[0:1, :]
    gain_second = gains[1:2, :]
    after_z(1)
    gather_next(0, 0)

    micro = z // 2
    owner = z % 2
    query_image = code[owner, pl.ds(micro, 1), :]
    key_code = code[owner, pl.ds(2 + micro, 1), :]
    key_columns = jnp.broadcast_to(key_code, (128, rows)).T
    for block in range(rows // 128):
        span = slice(128 * block, 128 * block + 128)
        key = key_columns[span, 0:1]
        row_id = lax.broadcasted_iota(jnp.int32, (128, rows), 0) + 128 * block
        col_id = lax.broadcasted_iota(jnp.int32, (128, rows), 1)
        seen = jnp.logical_or(key == query_image, row_id == col_id)
        bias[span, :] = jnp.where(seen, 0.0, NEGATIVE).astype(BF16)

    after_z(2)
    gather_next(1, 0)
    after_z(3)
    gather_z(4)
    gather_next(2, 0)
    rows_landed(0)
    send_rows(1, cot)

    def first_norm(i, at, base):
        normed, _ = normalize(xb[i].astype(F32))
        ab[pl.ds(base, TILE), :] = (normed * gain_first).astype(BF16)

    own_chunks(first_norm)
    pair_send(0, ab)
    gather_last(0, 1)

    def roll(value):
        return pltpu.roll(value, HD, 1)

    for name, offset in (("q", 0), ("k", 384), ("v", 768), ("o", 1152)):
        tile = {"q": 0, "k": 128, "v": 256, "o": 640}[name]
        wq[:, offset : offset + 128] = wts[0, 0, :, tile : tile + 128]
        wq[:, offset + 128 : offset + 256] = wts[0, 1, :, tile : tile + 128]
        mixed = {"q": 384, "k": 384, "v": 512, "o": 512}[name]
        one = wts[0, 0, :, mixed : mixed + 128].astype(F32)
        two = wts[0, 1, :, mixed : mixed + 128].astype(F32)
        if name in ("q", "v"):
            both = jnp.where(low, one, roll(two))
        else:
            both = jnp.where(low, roll(one), two)
        wq[:, offset + 256 : offset + 384] = both.astype(BF16)

    def project(base):
        span = pl.ds(base, own_rows)
        source = ab[span, :]
        for part in range(3):
            result = dot(source, wq[:, 384 * part : 384 * part + 384])
            if part == 0:
                result = result * SCALE
            qkv[span, 384 * part : 384 * part + 384] = result.astype(BF16)
            turned = result.T.astype(BF16)
            if part == 0:
                for h in range(6):
                    at = HD * (h % 2)
                    qtz[h, at : at + HD, span] = turned[HD * h : HD * h + HD]
            elif part == 1:
                kt[:, span] = turned
            else:
                vt[:, span] = turned

    each_half(project, lambda: pair_landed(0, ab))

    def attend(base, hook):
        span = pl.ds(base, own_rows)
        for h in range(6):
            pair = h // 2
            keys = qkv[:, 384 + 128 * pair : 512 + 128 * pair]
            scores = dot(keys, qtz[h, :, span]) + bias[:, span].astype(F32)
            highest = jnp.max(scores, axis=0, keepdims=True)
            exponent = jnp.exp(scores - highest)
            total = jnp.sum(exponent, axis=0, keepdims=True)
            rounded = (exponent * (1.0 / total)).astype(BF16)
            pt[h, :, span] = rounded
            mixed = dot(vt[HD * h : HD * h + HD, :], rounded)
            ott[HD * h : HD * h + HD, span] = mixed.astype(BF16)
            hook(h)
        orow[span, :] = ott[:, span].T

    def attend_loop(i, carry):
        base = pl.multiple_of(jnp.where(i == 0, theirs, mine), own_rows)

        def hook(h):
            if h == 1:

                @pl.when(i == 0)
                def _():
                    gather_next(3, 0)

            if h == 4:

                @pl.when(i == 0)
                def _():
                    after_z(4)

            if h == 5:

                @pl.when(i == 1)
                def _():
                    gather_next(4, 0)

        attend(base, hook)
        return carry

    lax.fori_loop(0, 2, attend_loop, 0)
    out_weight = wq[:, 1152:1536]
    prs[0] = dot_nt(orow[pl.ds(theirs, own_rows), :], out_weight).astype(BF16)
    part_send(0)

    def own_out(i, at, base):
        mid[pl.ds(at, TILE), :] = dot_nt(orow[pl.ds(base, TILE), :], wq[:, 1152:1536])

    own_chunks(own_out)
    part_landed(0)

    def second_norm(i, at, base):
        here = pl.ds(at, TILE)
        middle = xb[i].astype(F32) + (mid[here, :] + prr[0, here, :].astype(F32))
        mid[here, :] = middle
        normed, _ = normalize(middle)
        bnb[pl.ds(base, TILE), :] = (normed * gain_second).astype(BF16)

    own_chunks(second_norm)
    pair_send(1, bnb)
    gather_last(2, 3)

    def expand(base):
        def chunk(i, carry):
            span = pl.ds(pl.multiple_of(base + i * TILE, TILE), TILE)
            source = bnb[span, :]
            for j in range(half):
                pre = dot(source, wts[1, j])
                cdf = 0.5 * (1.0 + lax.erf(pre * 0.7071067811865476))
                density = jnp.exp(pre * pre * -0.5) * 0.3989422804014327
                gact[j, span, :] = (pre * cdf).astype(BF16)
                dgel[j, span, :] = (cdf + pre * density).astype(BF16)
            return carry

        lax.fori_loop(0, chunks, chunk, 0)

    rows_landed(1)
    pair_send(2, dyb)
    each_half(expand, lambda: pair_landed(1, bnb))
    gather_sent(0)

    def grad_tiles(source, slot, width_of):
        def tile(t, carry):
            at = pl.multiple_of(t * TILE, TILE)
            turned = source[:, pl.ds(at, TILE)].T
            width_of(turned, slot, pl.ds(at, TILE))
            return carry

        lax.fori_loop(0, D // TILE, tile, 0)

    def down_tile(turned, slot, span):
        for j in range(half):
            wts[slot, j, span, :] = dot(turned, gact[j]).astype(BF16)

    def up_tile(turned, slot, span):
        for j in range(half):
            wts[slot, j, span, :] = dot(turned, dgel[j]).astype(BF16)

    pair_landed(2, dyb)
    grad_tiles(dyb, place[2], down_tile)
    scatter_step(0, 0)
    gather_last(4)

    def contract(base, j_refs, weight):
        total = dot_nt(j_refs[0, pl.ds(base, TILE), :], wts[weight, 0])
        for j in range(1, half):
            total = total + dot_nt(j_refs[j, pl.ds(base, TILE), :], wts[weight, j])
        return total

    def their_chunks(buffer, weight, into):
        def step(i, carry):
            base = pl.multiple_of(theirs + i * TILE, TILE)
            into[pl.ds(pl.multiple_of(i * TILE, TILE), TILE), :] = contract(
                base, buffer, weight
            ).astype(BF16)
            return carry

        lax.fori_loop(0, chunks, step, 0)

    their_chunks(gact, 2, prs.at[1])
    part_send(1)

    def through_gelu(base):
        def chunk(i, carry):
            span = pl.ds(pl.multiple_of(base + i * TILE, TILE), TILE)
            source = dyb[span, :]
            for j in range(half):
                grad_act = dot(source, wts[2, j])
                dgel[j, span, :] = (grad_act * dgel[j, span, :].astype(F32)).astype(BF16)
            return carry

        lax.fori_loop(0, chunks, chunk, 0)

    each_half(through_gelu)
    part_sent(0)
    their_chunks(dgel, 1, prs.at[0])
    part_landed(1)

    def layer_rows(i, at, base):
        here = pl.ds(at, TILE)
        total = contract(base, gact, 2) + prr[1, here, :].astype(F32)
        stage[i] = (mid[here, :] + total).astype(BF16)

    own_chunks(layer_rows)
    part_send(2)
    send_back(0, y_out)
    pair_sent(2, dyb)
    part_landed(2)

    def second_back(i, at, base):
        here = pl.ds(at, TILE)
        grad = contract(base, dgel, 1) + prr[0, here, :].astype(F32)
        normed, inverse = normalize(mid[here, :])
        gsum[1:2, :] += jnp.sum(grad * normed, axis=0, keepdims=True)
        down = dyb[pl.ds(base, TILE), :].astype(F32) + norm_back(
            grad, gain_second, normed, inverse
        )
        mid[here, :] = down
        dyb[pl.ds(base, TILE), :] = down.astype(BF16)

    own_chunks(second_back)
    pair_send(3, dyb)
    gather_sent(1)
    scatter_next(0, 0)
    grad_tiles(bnb, place[1], up_tile)
    scatter_step(1, 0)

    def spread_mix(base):
        span = pl.ds(base, own_rows)
        result = dot(dyb[span, :], wq[:, 1152:1536])
        dorow[span, :] = result.astype(BF16)
        turned = result.T.astype(BF16)
        for h in range(6):
            at = HD * (h % 2)
            piece = turned[HD * h : HD * h + HD]
            qtz[h, at : at + HD, span] = piece
            product = piece.astype(F32) * ott[HD * h : HD * h + HD, span].astype(F32)
            delta[h, :, span] = jnp.sum(product, axis=0, keepdims=True)

    each_half(spread_mix, lambda: pair_landed(3, dyb))

    def attend_back(pair, carry):
        def tile(offset):
            return pl.ds(pl.multiple_of(offset + 128 * pair, 128), 128)

        parts = []
        for hh in range(2):
            h = 2 * pair + hh
            grad_values = dot(pt[h], dorow[:, tile(0)])
            for q in range(rows // own_rows):
                span = slice(q * own_rows, (q + 1) * own_rows)
                grad_prob = dot(qkv[:, tile(768)], qtz[h, :, span])
                chance = pt[h, :, span].astype(F32)
                pt[h, :, span] = (chance * (grad_prob - delta[h, :, span])).astype(BF16)
            grad_keys = dot(pt[h], qkv[:, tile(0)])
            head = pl.ds(pl.multiple_of(HD * h, HD), HD)
            grad_queries = dot(kt[head, :], pt[h]) * SCALE
            parts.append((grad_queries, grad_keys, grad_values))
        qkv[:, tile(768)] = jnp.where(low, parts[0][2], parts[1][2]).astype(BF16)
        qkv[:, tile(384)] = jnp.where(low, parts[0][1], parts[1][1]).astype(BF16)
        turned = jnp.concatenate([parts[0][0], parts[1][0]], axis=0).T
        qkv[:, tile(0)] = turned.astype(BF16)

        @pl.when(pair == 0)
        def _():
            scatter_last(0)

        @pl.when(pair == 2)
        def _():
            scatter_next(1, 0)

        return carry

    lax.fori_loop(0, 3, attend_back, 0)

    def first_contract(base, size):
        return dot_nt(qkv[pl.ds(base, size), :], wq[:, 0:1152])

    part_sent(1)
    prs[1] = first_contract(theirs, own_rows).astype(BF16)
    part_send(3)
    gather_sent(2)

    def first_tiles(t, carry):
        at = pl.multiple_of(t * TILE, TILE)
        span = pl.ds(at, TILE)
        slot = place[0]
        qkv_part = dot(ab[:, span].T, qkv[...])
        out_part = dot(dyb[:, span].T, orow[...])
        for i, target in ((0, 0), (1, 128), (2, 256)):
            for j in range(2):
                at = 384 * i + 128 * j
                wts[slot, j, span, target : target + 128] = qkv_part[:, at : at + 128].astype(BF16)
        for j in range(2):
            wts[slot, j, span, 640:768] = out_part[:, 128 * j : 128 * j + 128].astype(BF16)
        mixed_q = qkv_part[:, 256:384]
        mixed_k = qkv_part[:, 640:768]
        mixed_v = qkv_part[:, 1024:1152]
        mixed_o = out_part[:, 256:384]
        wts[slot, 0, span, 384:512] = jnp.where(low, mixed_q, roll(mixed_k)).astype(BF16)
        wts[slot, 1, span, 384:512] = jnp.where(low, roll(mixed_q), mixed_k).astype(BF16)
        wts[slot, 0, span, 512:640] = jnp.where(low, mixed_v, roll(mixed_o)).astype(BF16)
        wts[slot, 1, span, 512:640] = jnp.where(low, roll(mixed_v), mixed_o).astype(BF16)
        return carry

    lax.fori_loop(0, D // TILE, first_tiles, 0)
    scatter_step(2, 0)
    scatter_step(3, 0)

    back_sent(0)
    back_landed(0, y_out)
    scatter_relay(0)
    scatter_last(1)
    part_landed(3)

    def first_back(i, at, base):
        here = pl.ds(at, TILE)
        grad = first_contract(base, TILE) + prr[1, here, :].astype(F32)
        normed, inverse = normalize(xb[i].astype(F32))
        gsum[0:1, :] += jnp.sum(grad * normed, axis=0, keepdims=True)
        result = mid[here, :] + norm_back(grad, gain_first, normed, inverse)
        stage[i] = result.astype(BF16)

    own_chunks(first_back)

    me = 2 * z + c
    for index, (cc, zz) in enumerate(column_peers):
        remote(
            gsum,
            sum_rx.at[me],
            sem["sum_s"].at[index],
            sem["sum_r"].at[me],
            device(p, cc, zz),
        ).start()
    pltpu.make_async_copy(gsum, sum_rx.at[me], sem["sum_r"].at[me]).start()
    send_back(1, dx_out)
    scatter_next(2, 0)
    scatter_next(3, 0)
    scatter_relay(1)
    scatter_last(2)
    scatter_last(3)
    for source in range(2 * depth):
        wait_bytes(sum_rx.at[source], sem["sum_r"].at[source])
    for index in range(len(column_peers)):
        wait_bytes(gsum, sem["sum_s"].at[index])
    total = sum_rx[0]
    for source in range(1, 2 * depth):
        total = total + sum_rx[source]
    gsum[...] = total
    for index, pp in enumerate(plane_peers):
        remote(
            gsum, all_rx.at[p], sem["all_s"].at[index], sem["all_r"].at[p], device(pp, c, z)
        ).start()
    pltpu.make_async_copy(gsum, all_rx.at[p], sem["all_r"].at[p]).start()
    scatter_relay(2)
    scatter_relay(3)
    scatter_finish(0)
    for source in range(columns):
        wait_bytes(all_rx.at[source], sem["all_r"].at[source])
    for index in range(len(plane_peers)):
        wait_bytes(gsum, sem["all_s"].at[index])
    total = all_rx[0]
    for source in range(1, columns):
        total = total + all_rx[source]
    place_of = (2 * D // (2 * columns * depth)) * (dp * depth + z)
    wanted = jnp.where(place_of < D, total[0:1, :], total[1:2, :])
    turn = (D - place_of % D) % D
    gm_out[...] = pltpu.roll(jnp.broadcast_to(wanted, (8, D)), turn, 1)[:, 0:128]
    for u in (1, 2, 3):
        scatter_finish(u)

    back_landed(1, dx_out)
    back_sent(1)
    rows_sent(0, tok)
    rows_sent(1, cot)
    pair_sent(0, ab)
    pair_sent(1, bnb)
    pair_sent(3, dyb)
    part_sent(2)
    part_sent(3)
    for u in range(len(SCATTER)):
        scatter_sent(u)


def whole_layer(mesh, tok, cot, first, up, down, gains, padding, lengths):
    depth = mesh.shape["tensor"]
    bit_count = (mesh.shape["dp"] // 2).bit_length() - 1
    columns = 1 << bit_count
    shard = up.shape[0]
    half = depth // 2
    rows = padding.shape[1]
    own = rows // 2
    vmem = pl.BlockSpec(memory_space=pltpu.VMEM)
    hbm = pl.BlockSpec(memory_space=pl.ANY)
    sem = pltpu.SemaphoreType.DMA
    blocks = 1 << (bit_count - 1)
    scratch = [
        ((half, TILE, D), BF16),
        ((rows, D), BF16),
        ((rows, D), BF16),
        ((rows, D), BF16),
        ((KINDS, half, D, D), BF16),
        ((D, 2 * D), BF16),
        ((rows, 1152), BF16),
        ((6, 128, rows), BF16),
        ((384, rows), BF16),
        ((384, rows), BF16),
        ((6, rows, rows), BF16),
        ((rows, rows), BF16),
        ((384, rows), BF16),
        ((rows, 384), BF16),
        ((rows, 384), BF16),
        ((own, D), F32),
        ((half, rows, D), BF16),
        ((half, rows, D), BF16),
        ((2, own, D), BF16),
        ((2, own, D), BF16),
        ((half, TILE, D), BF16),
        ((KINDS, 2, columns - 1, half, shard, D), BF16),
        ((KINDS, depth, shard, D), BF16),
        ((KINDS, 2, half, shard, D), BF16),
        ((2 * columns, 8, 128), F32),
        ((8, D), F32),
        ((2, 8, rows), F32),
        ((8, D), F32),
        ((2 * depth, 8, D), F32),
        ((columns, 8, D), F32),
        ((6, 1, rows), F32),
    ]
    sems = {
        "tok_s": (2, 2),
        "tok_r": (2, half),
        "gain_s": (2 * columns,),
        "gain_r": (2 * columns,),
        "code_s": (),
        "code_r": (),
        "z_s": (len(GATHER), depth),
        "z_r": (len(GATHER), 2, half),
        "rel_s": (len(GATHER), 2, half),
        "x_s": (len(GATHER), 2, bit_count, blocks),
        "x_r": (len(GATHER), 2, bit_count, blocks),
        "rs_s": (len(SCATTER), 2, bit_count, blocks),
        "rs_r": (len(SCATTER), 2, bit_count, blocks),
        "rz_s": (len(SCATTER), 2, half),
        "rz_r": (len(SCATTER), depth),
        "far_r": (len(SCATTER), 2, half),
        "out_s": (2, half),
        "out_r": (2, 2),
        "pa_s": (4,),
        "pa_r": (4,),
        "pr_s": (4,),
        "pr_r": (4,),
        "sum_s": (2 * depth - 1,),
        "sum_r": (2 * depth,),
        "all_s": (columns - 1,),
        "all_r": (columns,),
    }
    return pl.pallas_call(
        functools.partial(layer_kernel, depth, bit_count, shard, rows),
        out_shape=(
            jax.ShapeDtypeStruct(tok.shape, BF16),
            jax.ShapeDtypeStruct(tok.shape, BF16),
            jax.ShapeDtypeStruct((KINDS,) + up.shape, F32),
            jax.ShapeDtypeStruct((8, 128), F32),
        ),
        in_specs=[hbm] * 5 + [vmem, vmem, pl.BlockSpec(memory_space=pltpu.SMEM)],
        out_specs=(hbm, hbm, vmem, vmem),
        scratch_shapes=[pltpu.VMEM(shape, dtype) for shape, dtype in scratch]
        + [sem(sems[name]) for name in SEMS],
        compiler_params=pltpu.CompilerParams(
            collective_id=0, has_side_effects=True, vmem_limit_bytes=67043328
        ),
        name="whole_layer",
    )(tok, cot, first, up, down, gains, padding, lengths)


def block_body(mesh, tokens, cotangent, lengths, padding, ln_gain, w_qkv, w_out, w_up, w_down):
    depth = mesh.shape["tensor"]
    shard = w_up.shape[1]
    pair = 2 * HD

    qkv = w_qkv[0]
    out_t = w_out[0].T
    packed = jnp.concatenate(
        [
            qkv[:, 0, :pair],
            qkv[:, 1, :pair],
            qkv[:, 2, :pair],
            qkv[:, 0, pair:],
            qkv[:, 1, pair:],
            qkv[:, 2, pair:],
            out_t[:, pair:],
            out_t[:, :pair],
        ],
        axis=1,
    )
    y_back, dx_back, summed, gain_sum = whole_layer(
        mesh,
        tokens,
        cotangent,
        packed,
        w_up[0],
        w_down[0].T,
        ln_gain[0],
        padding,
        lengths[:, 0],
    )
    gain_result = gain_sum[0, : 2 * D // (mesh.shape["dp"] * depth)]
    first = summed[0]
    qkv_grad = jnp.stack(
        [
            jnp.concatenate(
                [
                    first[:, pair * i : pair * i + pair],
                    first[:, 3 * pair + HD * i : 3 * pair + HD * i + HD],
                ],
                axis=1,
            )
            for i in range(3)
        ],
        axis=1,
    )[None]
    out_grad = jnp.concatenate([first[:, 5 * pair :], first[:, 4 * pair + HD : 5 * pair]], axis=1)
    return (
        y_back.astype(F32),
        dx_back.astype(F32),
        gain_result,
        qkv_grad,
        out_grad.T[None],
        summed[1][None],
        summed[2].T[None],
    )


def visible(lengths_row, padding_row):
    places = lax.iota(jnp.int32, padding_row.shape[0])
    bounds = jnp.cumsum(lengths_row)
    picture = jnp.sum((places[:, None] >= bounds[None, :]).astype(jnp.int32), axis=1)
    same_image = picture[:, None] == picture[None, :]
    return same_image & ((padding_row[None, :] == 1) | (places[:, None] == places[None, :]))


def gelu_exact(pre_values):
    return jax.nn.gelu(pre_values, approximate=False)


def masked_scores(queries, key_rows, allowed):
    scaling = queries.shape[-1] ** (-0.5)
    scores = (
        jnp.einsum("qhd,khd->hqk", queries, key_rows, preferred_element_type=jnp.float32) * scaling
    )
    return (jnp.where(allowed[None], scores, NEGATIVE), scaling)


def attend(stacked, allowed):
    scores, scaling = masked_scores(stacked[:, 0], stacked[:, 1], allowed)
    highest = jnp.max(scores, axis=-1, keepdims=True)
    exponent = jnp.exp(scores - highest)
    totals = jnp.sum(exponent, axis=-1, keepdims=True)
    rounded = (exponent / totals).astype(jnp.bfloat16)
    mixture = jnp.einsum("hqk,khd->qhd", rounded, stacked[:, 2], preferred_element_type=jnp.float32)
    return (mixture, highest, totals)


def attend_back(stacked, allowed, highest, totals, grad_mix):
    queries, key_rows, value_rows = (stacked[:, 0], stacked[:, 1], stacked[:, 2])
    scores, scaling = masked_scores(queries, key_rows, allowed)
    probability = jnp.exp(scores - highest) / totals
    rounded = probability.astype(jnp.bfloat16)
    grad_prob = jnp.einsum("qhd,khd->hqk", grad_mix, value_rows, preferred_element_type=jnp.float32)
    grad_values = jnp.einsum("hqk,qhd->khd", rounded, grad_mix, preferred_element_type=jnp.float32)
    inner_sum = jnp.sum(probability * grad_prob, axis=-1, keepdims=True)
    grad_scores = (probability * (grad_prob - inner_sum)).astype(jnp.bfloat16)
    grad_queries = (
        jnp.einsum("hqk,khd->qhd", grad_scores, key_rows, preferred_element_type=jnp.float32)
        * scaling
    )
    grad_keys = (
        jnp.einsum("hqk,qhd->khd", grad_scores, queries, preferred_element_type=jnp.float32)
        * scaling
    )
    return jnp.stack([grad_queries, grad_keys, grad_values], axis=1).astype(jnp.bfloat16)


def collect_weights(ln_gain, w_qkv, w_out, w_up, w_down, layer_index):
    return (
        lax.all_gather(ln_gain[layer_index], "dp", axis=1, tiled=True),
        lax.all_gather(w_qkv[layer_index], "dp", axis=0, tiled=True),
        lax.all_gather(w_out[layer_index], "dp", axis=1, tiled=True),
        lax.all_gather(w_up[layer_index], "dp", axis=0, tiled=True),
        lax.all_gather(w_down[layer_index], "dp", axis=1, tiled=True),
    )


def spread(block_rows):
    return lax.all_gather(block_rows, "tensor", axis=0, tiled=True)


def spread_grad(block_rows):
    return lax.all_gather(block_rows, "tensor", axis=0, tiled=True)


def collect_rows(operand, weight):
    return lax.psum_scatter(
        jnp.dot(operand, weight, preferred_element_type=jnp.float32),
        "tensor",
        scatter_dimension=0,
        tiled=True,
    )


def return_rows(operand, weight):
    return lax.psum_scatter(
        lax.dot_general(
            operand, weight, (((1,), (1,)), ((), ())), preferred_element_type=jnp.float32
        ),
        "tensor",
        scatter_dimension=0,
        tiled=True,
    )


def reduce_grads(pieces):
    return (
        lax.psum_scatter(pieces[0], "dp", scatter_dimension=0, tiled=True),
        lax.psum_scatter(pieces[1], "dp", scatter_dimension=1, tiled=True),
        lax.psum_scatter(pieces[2], "dp", scatter_dimension=0, tiled=True),
        lax.psum_scatter(pieces[3], "dp", scatter_dimension=1, tiled=True),
    )


def body(tokens, cotangent, lengths, padding, ln_gain, w_qkv, w_out, w_up, w_down):
    layer_count = w_qkv.shape[0]
    micro_count = tokens.shape[0]
    residual = [tokens[batch_index].astype(jnp.float32) for batch_index in range(micro_count)]
    visibility = [
        visible(lengths[batch_index, 0], padding[batch_index]) for batch_index in range(micro_count)
    ]
    saved = []
    stored_weights = []
    layer_index = 0
    stored_weights.append(None)
    for batch_index in range(micro_count):
        weights = collect_weights(ln_gain, w_qkv, w_out, w_up, w_down, layer_index)
        gain_pair, qkv_weight, out_weight, up_weight, down_weight = weights
        gain_first = gain_pair[0].astype(jnp.float32)
        gain_second = gain_pair[1].astype(jnp.float32)
        entering = residual[batch_index]
        normed, inverse = normalize(entering)
        first_input = spread((normed * gain_first).astype(jnp.bfloat16))
        triple = jnp.einsum(
            "rd,dcn->rcn", first_input, qkv_weight, preferred_element_type=jnp.float32
        ).astype(jnp.bfloat16)
        stacked = triple.reshape(triple.shape[0], 3, -1, HD)
        mixture, highest, totals = attend(stacked, visibility[batch_index])
        mix_rounded = mixture.reshape(mixture.shape[0], -1).astype(jnp.bfloat16)
        middle = entering + collect_rows(mix_rounded, out_weight)
        normed_two, inverse_two = normalize(middle)
        second_input = spread((normed_two * gain_second).astype(jnp.bfloat16))
        hidden_pre = jnp.dot(second_input, up_weight, preferred_element_type=jnp.float32)
        activated = gelu_exact(hidden_pre).astype(jnp.bfloat16)
        residual[batch_index] = middle + collect_rows(activated, down_weight)
        saved.append(
            (
                entering,
                first_input,
                stacked,
                highest,
                totals,
                mix_rounded,
                middle,
                second_input,
                hidden_pre,
                activated,
            )
        )
    gradients = [cotangent[batch_index].astype(jnp.float32) for batch_index in range(micro_count)]
    gain_parts = [jnp.zeros((2, D), jnp.float32)]
    weight_results = [None]
    for layer_index in reversed(range(layer_count)):
        summed = None
        for batch_index in range(micro_count):
            weights = collect_weights(ln_gain, w_qkv, w_out, w_up, w_down, layer_index)
            gain_pair, qkv_weight, out_weight, up_weight, down_weight = weights
            gain_first = gain_pair[0].astype(jnp.float32)
            gain_second = gain_pair[1].astype(jnp.float32)
            (
                entering,
                first_input,
                stacked,
                highest,
                totals,
                mix_rounded,
                middle,
                second_input,
                hidden_pre,
                activated,
            ) = saved[layer_index * micro_count + batch_index]
            incoming = gradients[batch_index]
            grad_down = spread_grad(incoming.astype(jnp.bfloat16))
            down_part = jnp.einsum(
                "rf,rd->fd", activated, grad_down, preferred_element_type=jnp.float32
            )
            grad_act = lax.dot_general(
                grad_down, down_weight, (((1,), (1,)), ((), ())), preferred_element_type=jnp.float32
            )
            pulled = jax.vjp(gelu_exact, hidden_pre)
            grad_pre = pulled[1](grad_act)[0].astype(jnp.bfloat16)
            up_part = jnp.einsum(
                "rd,rf->df", second_input, grad_pre, preferred_element_type=jnp.float32
            )
            grad_norm_two = return_rows(grad_pre, up_weight)
            normed_two, inverse_two = normalize(middle)
            gain_two_part = jnp.sum(grad_norm_two * normed_two, axis=0)
            incoming = incoming + norm_back(grad_norm_two, gain_second, normed_two, inverse_two)
            grad_branch = spread_grad(incoming.astype(jnp.bfloat16))
            out_part = jnp.einsum(
                "rk,rd->kd", mix_rounded, grad_branch, preferred_element_type=jnp.float32
            )
            grad_mix = lax.dot_general(
                grad_branch,
                out_weight,
                (((1,), (1,)), ((), ())),
                preferred_element_type=jnp.float32,
            )
            grad_mix = grad_mix.astype(jnp.bfloat16).reshape(grad_mix.shape[0], -1, HD)
            grad_triple = attend_back(stacked, visibility[batch_index], highest, totals, grad_mix)
            flat_triple = grad_triple.reshape(grad_triple.shape[0], 3, -1)
            qkv_part = jnp.einsum(
                "rd,rcn->dcn", first_input, flat_triple, preferred_element_type=jnp.float32
            )
            grad_norm_one = return_rows(
                flat_triple.reshape(flat_triple.shape[0], -1),
                qkv_weight.reshape(qkv_weight.shape[0], -1),
            )
            normed, inverse = normalize(entering)
            gain_one_part = jnp.sum(grad_norm_one * normed, axis=0)
            incoming = incoming + norm_back(grad_norm_one, gain_first, normed, inverse)
            gradients[batch_index] = incoming
            gain_parts[layer_index] = gain_parts[layer_index] + jnp.stack(
                [gain_one_part, gain_two_part]
            )
            pieces = (qkv_part, out_part, up_part, down_part)
            if summed is None:
                summed = pieces
            else:
                summed = tuple((older + newer for older, newer in zip(summed, pieces)))
        summed = reduce_grads(summed)
        weight_results[layer_index] = summed
    gain_flat = jnp.stack(gain_parts).reshape(-1)
    gain_result = lax.psum_scatter(gain_flat, ("dp", "tensor"), scatter_dimension=0, tiled=True)
    layer_out = jnp.stack(residual)
    input_grad = jnp.stack(gradients)
    qkv_grad = jnp.stack([weight_results[0][0]])
    out_grad = jnp.stack([weight_results[0][1]])
    up_grad = jnp.stack([weight_results[0][2]])
    down_grad = jnp.stack([weight_results[0][3]])
    return (layer_out, input_grad, gain_result, qkv_grad, out_grad, up_grad, down_grad)


def fits(mesh, tokens, w_qkv):
    dp_size, depth = mesh.shape["dp"], mesh.shape["tensor"]
    columns = dp_size // 2
    return (
        depth == 4
        and dp_size >= 4
        and columns & (columns - 1) == 0
        and D == dp_size * 2 * HALF
        and tokens.shape[0] == 2
        and tokens.shape[1] == dp_size * depth * TILE
        and w_qkv.shape[0] == 1
    )


def solution(mesh):
    def run(tokens, cotangent, lengths, padding, ln_gain, w_qkv, *rest):
        one_block = fits(mesh, tokens, w_qkv)
        program = functools.partial(block_body, mesh) if one_block else body
        return jax.shard_map(
            program,
            mesh=mesh,
            in_specs=(
                P(None, ("dp", "tensor"), None),
                P(None, ("dp", "tensor"), None),
                P(None, "dp", None),
                P(None, "dp"),
                P(None, None, "dp"),
                P(None, "dp", None, "tensor"),
                P(None, "tensor", "dp"),
                P(None, "dp", "tensor"),
                P(None, "tensor", "dp"),
            ),
            out_specs=(
                P(None, ("dp", "tensor"), None),
                P(None, ("dp", "tensor"), None),
                P(("dp", "tensor")),
                P(None, "dp", None, "tensor"),
                P(None, "tensor", "dp"),
                P(None, "dp", "tensor"),
                P(None, "tensor", "dp"),
            ),
            check_vma=False,
        )(tokens, cotangent, lengths, padding, ln_gain, w_qkv, *rest)

    return run
```

```python
import functools

import jax
import jax.numpy as jnp
from jax import lax
from jax.experimental import pallas as pl
from jax.experimental.pallas import tpu as pltpu
from jax.sharding import PartitionSpec as P

D = 768
HD = 64
NEGATIVE = -1e30
EPSILON = 1e-06
MESH = pl.DeviceIdType.MESH
F32 = jnp.float32
BF16 = jnp.bfloat16
KINDS = 3
HALF = 48
GATHER = ((0, 0, HALF), (0, HALF, HALF), (1, 0, HALF), (1, HALF, HALF), (2, 0, 2 * HALF))
SCATTER = ((2, 0, 2 * HALF), (1, 0, 2 * HALF), (0, 0, HALF), (0, HALF, HALF))
RELAYED = (2, 1, 0)
TILE = 256
SCALE = HD**-0.5


def flip(value, bit):
    size = 1 << bit
    return value + size * (1 - 2 * ((value // size) % 2))


def flip_mask(value, mask):
    bit = 0
    while mask >> bit:
        if (mask >> bit) & 1:
            value = flip(value, bit)
        bit += 1
    return value


def submasks(bits):
    masks = [0]
    for bit in bits:
        masks = masks + [mask | (1 << bit) for mask in masks]
    return masks


def color_order(color, bit_count):
    order = list(range(bit_count))
    return order if color == 0 else order[::-1]


def device(p, c, z):
    return (2 * p + c, z)


def dot(left, right):
    return jnp.dot(left, right, preferred_element_type=F32)


def dot_nt(left, right):
    return lax.dot_general(left, right, (((1,), (1,)), ((), ())), preferred_element_type=F32)


def normalize(row_block):
    average = jnp.mean(row_block, axis=-1, keepdims=True)
    centred = row_block - average
    variance = jnp.mean(centred * centred, axis=-1, keepdims=True)
    inverse = lax.rsqrt(variance + EPSILON)
    return (centred * inverse, inverse)


def norm_back(grad_out, gain_row, normed, inverse):
    scaled = grad_out * gain_row
    mean_grad = jnp.mean(scaled, axis=-1, keepdims=True)
    second = jnp.mean(scaled * normed, axis=-1, keepdims=True)
    return inverse * (scaled - mean_grad - normed * second)


def remote(source, target, send_sem, recv_sem, dest):
    return pltpu.make_async_remote_copy(
        source, target, send_sem, recv_sem, device_id=dest, device_id_type=MESH
    )


def wait_bytes(ref, sem):
    pltpu.make_async_copy(ref, ref, sem).wait()


SEMS = (
    "tok_s",
    "tok_r",
    "gain_s",
    "gain_r",
    "code_s",
    "code_r",
    "z_s",
    "z_r",
    "rel_s",
    "x_s",
    "x_r",
    "rs_s",
    "rs_r",
    "rz_s",
    "rz_r",
    "far_r",
    "out_s",
    "out_r",
    "pa_s",
    "pa_r",
    "pr_s",
    "pr_r",
    "sum_s",
    "sum_r",
    "all_s",
    "all_r",
)


def layer_kernel(depth, bit_count, shard, rows, *refs):
    (tok, cot, first_in, up_in, down_in, gain_in, pad_in, length_in) = refs[:8]
    (y_out, dx_out, g_out, gm_out) = refs[8:12]
    (
        xb,
        dyb,
        ab,
        bnb,
        wts,
        wq,
        qkv,
        qtz,
        vt,
        kt,
        pt,
        bias,
        ott,
        orow,
        dorow,
        mid,
        gact,
        dgel,
        prs,
        prr,
        stage,
        rx,
        zrx,
        far_rx,
        gbuf,
        gains,
        code,
        gsum,
        sum_rx,
        all_rx,
        delta,
        shares,
    ) = refs[12:44]
    sem = dict(zip(SEMS, refs[44:]))
    half = depth // 2
    columns = 1 << bit_count
    own_rows = rows // 2
    chunks = own_rows // TILE
    dp = lax.axis_index("dp")
    z = lax.axis_index("tensor")
    c = dp % 2
    p = dp // 2
    buddy = device(p, 1 - c, z)
    mine = pl.multiple_of(own_rows * c, own_rows)
    theirs = pl.multiple_of(own_rows * (1 - c), own_rows)
    lane = lax.broadcasted_iota(jnp.int32, (1, 128), 1)
    low = lane < HD

    def same(to_c, to_z):
        return jnp.logical_and(to_c == c, to_z == z)

    def send_or_copy(is_self, source, target, send_sem, recv_sem, dest):
        @pl.when(is_self)
        def _():
            pltpu.make_async_copy(source, target, recv_sem).start()

        @pl.when(jnp.logical_not(is_self))
        def _():
            remote(source, target, send_sem, recv_sem, dest).start()

    def wait_send(is_self, source, send_sem):
        @pl.when(jnp.logical_not(is_self))
        def _():
            wait_bytes(source, send_sem)

    column_peers = []
    for dz in range(depth):
        for dc in range(2):
            if dz or dc:
                column_peers.append((c if dc == 0 else 1 - c, (z + dz) % depth))
    plane_peers = [flip_mask(p, mask) for mask in range(1, columns)]

    def entry_barrier():
        barrier = pltpu.get_barrier_semaphore()
        peers = [device(p, cc, zz) for cc, zz in column_peers]
        peers += [device(pp, c, z) for pp in plane_peers]
        peers += [device(pp, 1 - c, z) for pp in plane_peers]
        for peer in peers:
            pl.semaphore_signal(barrier, inc=1, device_id=peer, device_id_type=MESH)
        pl.semaphore_wait(barrier, len(peers))

    def make_small():
        gbuf[dp] = jnp.zeros(gbuf.shape[1:], F32)
        gbuf[dp, 0:2, 0:shard] = gain_in[...].astype(F32)
        places = lax.broadcasted_iota(jnp.int32, (1, rows), 1)
        for m in range(2):
            image = jnp.zeros((1, rows), jnp.int32)
            bound = 0
            for k in range(length_in.shape[1]):
                bound = bound + length_in[m, k]
                image = image + (places >= bound).astype(jnp.int32)
            key = jnp.where(pad_in[m : m + 1, :] == 1, image, -1)
            code[c, m : m + 1, :] = image.astype(F32)
            code[c, 2 + m : 3 + m, :] = key.astype(F32)

    def send_small():
        remote(code.at[c], code.at[c], sem["code_s"], sem["code_r"], buddy).start()
        index = 0
        for pp in [p] + plane_peers:
            for cc in (c, 1 - c):
                if index:
                    remote(
                        gbuf.at[dp],
                        gbuf.at[dp],
                        sem["gain_s"].at[index],
                        sem["gain_r"].at[dp],
                        device(pp, cc, z),
                    ).start()
                index += 1

    def finish_small():
        wait_bytes(code.at[c], sem["code_s"])
        wait_bytes(code.at[1 - c], sem["code_r"])
        index = 0
        for pp in [p] + plane_peers:
            for cc in (c, 1 - c):
                if index:
                    wait_bytes(gbuf.at[dp], sem["gain_s"].at[index])
                    source = 2 * pp + cc
                    wait_bytes(gbuf.at[source], sem["gain_r"].at[source])
                index += 1
        rest = jnp.zeros((8, D - 128), F32)
        total = jnp.zeros((8, D), F32)
        for source in range(2 * columns):
            wide = jnp.concatenate([gbuf[source], rest], axis=1)
            total = total + (pltpu.roll(wide, shard * source, 1) if source else wide)
        gains[...] = total

    def row_targets():
        for m in range(2):
            to_z, to_c = 2 * m + c, z // half
            yield m, to_c, to_z, same(to_c, to_z)

    def row_target(which, slot):
        if which == 0:
            return xb.at[slot]
        return dyb.at[pl.ds(pl.multiple_of(own_rows * c + TILE * slot, TILE), TILE)]

    def row_landing(which, slot, to_c):
        if which == 0:
            return xb.at[slot]
        return dyb.at[pl.ds(pl.multiple_of(own_rows * to_c + TILE * slot, TILE), TILE)]

    def send_rows(which, array):
        for m, to_c, to_z, is_self in row_targets():
            slot = z % half
            send_or_copy(
                is_self,
                array.at[m],
                row_landing(which, slot, to_c),
                sem["tok_s"].at[which, m],
                sem["tok_r"].at[which, slot],
                device(p, to_c, to_z),
            )

    def rows_sent(which, array):
        for m, to_c, to_z, is_self in row_targets():
            wait_send(is_self, array.at[m], sem["tok_s"].at[which, m])

    def rows_landed(which):
        for slot in range(half):
            wait_bytes(row_target(which, slot), sem["tok_r"].at[which, slot])

    def send_back(which, target):
        for slot in range(half):
            to_c, to_z = z % 2, half * c + slot
            send_or_copy(
                same(to_c, to_z),
                stage.at[slot],
                target.at[z // 2],
                sem["out_s"].at[which, slot],
                sem["out_r"].at[which, z // 2],
                device(p, to_c, to_z),
            )

    def back_sent(which):
        for slot in range(half):
            is_self = same(z % 2, half * c + slot)
            wait_send(is_self, stage.at[slot], sem["out_s"].at[which, slot])

    def back_landed(which, target):
        for m in range(2):
            wait_bytes(target.at[m], sem["out_r"].at[which, m])

    last = depth - 1

    def two_ends(low_core, high_core):
        return jnp.logical_or(
            jnp.logical_and(c == 0, z == low_core), jnp.logical_and(c == 1, z == high_core)
        )

    ends = two_ends(last, 0)
    relays = two_ends(last - 1, 1)
    relay_to = device(p, c, last * (1 - c))
    relay_from = device(p, c, last - 1 + c * (2 - last))

    def unit_rows(unit, column, color):
        _, start, size = unit
        return pl.ds(pl.multiple_of((2 * column + color) * shard + start, 16), size)

    def unit_source(unit):
        return (first_in, up_in, down_in)[unit[0]].at[pl.ds(unit[1], unit[2])]

    def z_targets():
        for dz in range(depth):
            to_z = (z + dz) % depth
            yield dz, z // half, to_z, to_z == last * (1 - z // half)

    def gather_z(u):
        unit = GATHER[u]
        for dz, to_c, to_z, far in z_targets():
            source = unit_source(unit)
            target = wts.at[unit[0], z % half, unit_rows(unit, p, c)]
            recv = sem["z_r"].at[u, c, z % half]
            if dz == 0:
                send_or_copy(
                    to_c == c, source, target, sem["z_s"].at[u, dz], recv, device(p, to_c, to_z)
                )
            else:

                @pl.when(jnp.logical_not(far))
                def _():
                    remote(
                        source, target, sem["z_s"].at[u, dz], recv, device(p, to_c, to_z)
                    ).start()

    def gather_z_sent(u):
        for dz, to_c, to_z, far in z_targets():
            skip = to_c == c if dz == 0 else far
            wait_send(skip, unit_source(GATHER[u]), sem["z_s"].at[u, dz])

    def relay_block(u, color, slot):
        unit = GATHER[u]
        return wts.at[unit[0], slot, unit_rows(unit, p, color)]

    def gather_z_landed(u):
        unit = GATHER[u]
        for color in range(2):
            for slot in range(half):
                wait_bytes(
                    wts.at[unit[0], slot, unit_rows(unit, p, color)], sem["z_r"].at[u, color, slot]
                )

    def forward(u):
        @pl.when(relays)
        def _():
            gather_z_landed(u)
            for color in range(2):
                for slot in range(half):
                    block = relay_block(u, color, slot)
                    remote(
                        block,
                        block,
                        sem["rel_s"].at[u, color, slot],
                        sem["z_r"].at[u, color, slot],
                        relay_to,
                    ).start()

    def after_z(u):
        pl.when(jnp.logical_not(relays))(functools.partial(gather_z_landed, u))
        gather_step(u, 0)

    def gather_blocks(u, color, s, landed):
        unit = GATHER[u]
        order = color_order(color, bit_count)
        for index, mask in enumerate(submasks(order[:s])):
            column = flip_mask(p, mask)
            if landed:
                column = flip(column, order[s])
            yield index, wts.at[unit[0], :, unit_rows(unit, column, color)]

    def gather_step(u, s):
        for color in range(2):
            to = device(flip(p, color_order(color, bit_count)[s]), c, z)
            for index, block in gather_blocks(u, color, s, False):
                remote(
                    block,
                    block,
                    sem["x_s"].at[u, color, s, index],
                    sem["x_r"].at[u, color, s, index],
                    to,
                ).start()

    def gather_next(u, s):
        for color in range(2):
            for index, block in gather_blocks(u, color, s, True):
                wait_bytes(block, sem["x_r"].at[u, color, s, index])
        if s + 1 < bit_count:
            gather_step(u, s + 1)

    def gather_last(*units):
        for u in units:
            for s in range(1, bit_count):
                gather_next(u, s)

    def gather_sent(k):
        for u, unit in enumerate(GATHER):
            if unit[0] == k:
                gather_unit_sent(u)

    def gather_unit_sent(u):
        gather_z_sent(u)

        @pl.when(relays)
        def _():
            for color in range(2):
                for slot in range(half):
                    wait_bytes(relay_block(u, color, slot), sem["rel_s"].at[u, color, slot])

        for color in range(2):
            for s in range(bit_count):
                for index, block in gather_blocks(u, color, s, False):
                    wait_bytes(block, sem["x_s"].at[u, color, s, index])

    place = {2: 0, 1: 1, 0: 2}

    def rx_slot(u, color, s, index):
        unit = SCATTER[u]
        slot = (1 << bit_count) - (1 << (bit_count - s)) + index
        return rx.at[unit[0], color, slot, :, pl.ds(unit[1], unit[2])]

    def scatter_order(color):
        return color_order(color, bit_count)[::-1]

    def scatter_blocks(u, color, s, away):
        unit = SCATTER[u]
        order = scatter_order(color)
        for index, mask in enumerate(submasks(order[s + 1 :])):
            column = flip_mask(p, mask)
            if away:
                column = flip(column, order[s])
            yield index, wts.at[place[unit[0]], :, unit_rows(unit, column, color)]

    def scatter_step(u, s):
        for color in range(2):
            to = device(flip(p, scatter_order(color)[s]), c, z)
            for index, block in scatter_blocks(u, color, s, True):
                remote(
                    block,
                    rx_slot(u, color, s, index),
                    sem["rs_s"].at[u, color, s, index],
                    sem["rs_r"].at[u, color, s, index],
                    to,
                ).start()

    def scatter_next(u, s):
        for color in range(2):
            for index, block in scatter_blocks(u, color, s, False):
                got = rx_slot(u, color, s, index)
                wait_bytes(got, sem["rs_r"].at[u, color, s, index])
                block[...] = (block[...].astype(F32) + got[...].astype(F32)).astype(BF16)
        if s + 1 < bit_count:
            scatter_step(u, s + 1)
        else:
            scatter_z(u)

    def scatter_last(*units):
        for u in units:
            for s in range(1, bit_count):
                scatter_next(u, s)

    def scatter_z_blocks(u):
        unit = SCATTER[u]
        for color in range(2):
            for slot in range(half):
                to_z = half * c + slot
                block = wts.at[place[unit[0]], slot, unit_rows(unit, p, color)]
                yield color, slot, to_z, block

    def summed_on_the_way(u):
        return SCATTER[u][0] in RELAYED

    def landing(u, source):
        unit = SCATTER[u]
        return zrx.at[unit[0], source, pl.ds(unit[1], unit[2])]

    def far_landing(u, color, slot):
        unit = SCATTER[u]
        return far_rx.at[unit[0], color, slot, pl.ds(unit[1], unit[2])]

    def scatter_z(u):
        for color, slot, to_z, block in scatter_z_blocks(u):
            send, recv = sem["rz_s"].at[u, color, slot], sem["rz_r"].at[u, z]
            dest = device(p, color, to_z)
            if not summed_on_the_way(u):
                send_or_copy(same(color, to_z), block, landing(u, z), send, recv, dest)
                continue

            @pl.when(jnp.logical_not(jnp.logical_or(ends, relays)))
            def _():
                send_or_copy(same(color, to_z), block, landing(u, z), send, recv, dest)

            @pl.when(ends)
            def _():
                remote(
                    block,
                    far_landing(u, color, slot),
                    send,
                    sem["far_r"].at[u, color, slot],
                    relay_from,
                ).start()

    def scatter_relay(u):
        @pl.when(relays)
        def _():
            for color, slot, to_z, block in scatter_z_blocks(u):
                got = far_landing(u, color, slot)
                wait_bytes(got, sem["far_r"].at[u, color, slot])
                block[...] = (block[...].astype(F32) + got[...].astype(F32)).astype(BF16)
                send, recv = sem["rz_s"].at[u, color, slot], sem["rz_r"].at[u, z]
                dest = device(p, color, to_z)
                send_or_copy(same(color, to_z), block, landing(u, z), send, recv, dest)

    def scatter_finish(u):
        unit = SCATTER[u]
        for source in range(depth):
            got = functools.partial(wait_bytes, landing(u, source), sem["rz_r"].at[u, source])
            if summed_on_the_way(u) and source in (0, last):
                pl.when(z // half != (last - source) // half)(got)
            else:
                got()
        total = landing(u, 0)[...].astype(F32)
        for source in range(1, depth):
            total = total + landing(u, source)[...].astype(F32)
        g_out[unit[0], unit[1] : unit[1] + unit[2]] = total

    def scatter_sent(u):
        for color in range(2):
            for s in range(bit_count):
                for index, block in scatter_blocks(u, color, s, True):
                    wait_bytes(block, sem["rs_s"].at[u, color, s, index])
        for color, slot, to_z, block in scatter_z_blocks(u):
            local = same(color, to_z)
            if summed_on_the_way(u):
                local = jnp.logical_and(local, jnp.logical_not(ends))
            wait_send(local, block, sem["rz_s"].at[u, color, slot])

    def clear_far():
        for source in (0, last):

            @pl.when(z // half == (last - source) // half)
            def _():
                for k in RELAYED:
                    zrx[k, source] = jnp.zeros(zrx.shape[2:], BF16)

    def pair_send(index, buffer):
        own = buffer.at[pl.ds(mine, own_rows)]
        remote(own, own, sem["pa_s"].at[index], sem["pa_r"].at[index], buddy).start()

    def pair_landed(index, buffer):
        wait_bytes(buffer.at[pl.ds(theirs, own_rows)], sem["pa_r"].at[index])

    def pair_sent(index, buffer):
        wait_bytes(buffer.at[pl.ds(mine, own_rows)], sem["pa_s"].at[index])

    def part_send(index):
        remote(
            prs.at[index % 2],
            prr.at[index % 2],
            sem["pr_s"].at[index],
            sem["pr_r"].at[index],
            buddy,
        ).start()

    def part_landed(index):
        wait_bytes(prr.at[index % 2], sem["pr_r"].at[index])

    def part_sent(index):
        wait_bytes(prs.at[index % 2], sem["pr_s"].at[index])

    def each_half(body, second=None):
        def step(i, carry):
            if second is not None:
                pl.when(i == 1)(second)
            body(pl.multiple_of(jnp.where(i == 0, mine, theirs), own_rows))
            return carry

        lax.fori_loop(0, 2, step, 0)

    def own_chunks(body):
        def step(i, carry):
            body(i, pl.multiple_of(i * TILE, TILE), pl.multiple_of(mine + i * TILE, TILE))
            return carry

        lax.fori_loop(0, chunks, step, 0)

    make_small()
    entry_barrier()
    send_small()
    for u in range(4):
        gather_z(u)
    send_rows(0, tok)

    for h in range(6):
        qtz[h, HD * (1 - h % 2) : HD * (1 - h % 2) + HD, :] = jnp.zeros((HD, rows), BF16)
    gsum[...] = jnp.zeros(gsum.shape, F32)
    clear_far()
    forward(0)
    after_z(0)
    finish_small()
    gain_first = gains[0:1, :]
    gain_second = gains[1:2, :]
    forward(1)
    after_z(1)
    gather_next(0, 0)

    micro = z // 2
    owner = z % 2
    query_image = code[owner, pl.ds(micro, 1), :]
    key_code = code[owner, pl.ds(2 + micro, 1), :]
    key_columns = jnp.broadcast_to(key_code, (128, rows)).T
    for block in range(rows // 128):
        span = slice(128 * block, 128 * block + 128)
        key = key_columns[span, 0:1]
        row_id = lax.broadcasted_iota(jnp.int32, (128, rows), 0) + 128 * block
        col_id = lax.broadcasted_iota(jnp.int32, (128, rows), 1)
        seen = jnp.logical_or(key == query_image, row_id == col_id)
        bias[span, :] = jnp.where(seen, 0.0, NEGATIVE)

    forward(2)
    after_z(2)
    gather_next(1, 0)
    forward(3)
    after_z(3)
    gather_z(4)
    gather_next(2, 0)
    rows_landed(0)

    def first_norm(i, at, base):
        normed, _ = normalize(xb[i].astype(F32))
        ab[pl.ds(base, TILE), :] = (normed * gain_first).astype(BF16)

    own_chunks(first_norm)
    pair_send(0, ab)
    gather_last(0, 1)

    def roll(value):
        return pltpu.roll(value, HD, 1)

    for name, offset in (("q", 0), ("k", 384), ("v", 768), ("o", 1152)):
        tile = {"q": 0, "k": 128, "v": 256, "o": 640}[name]
        wq[:, offset : offset + 128] = wts[0, 0, :, tile : tile + 128]
        wq[:, offset + 128 : offset + 256] = wts[0, 1, :, tile : tile + 128]
        mixed = {"q": 384, "k": 384, "v": 512, "o": 512}[name]
        one = wts[0, 0, :, mixed : mixed + 128].astype(F32)
        two = wts[0, 1, :, mixed : mixed + 128].astype(F32)
        if name in ("q", "v"):
            both = jnp.where(low, one, roll(two))
        else:
            both = jnp.where(low, roll(one), two)
        wq[:, offset + 256 : offset + 384] = both.astype(BF16)

    def project(base):
        span = pl.ds(base, own_rows)
        source = ab[span, :]
        for part in range(3):
            result = dot(source, wq[:, 384 * part : 384 * part + 384])
            if part == 0:
                result = result * SCALE
            qkv[span, 384 * part : 384 * part + 384] = result.astype(BF16)
            turned = result.T.astype(BF16)
            if part == 0:
                for h in range(6):
                    at = HD * (h % 2)
                    qtz[h, at : at + HD, span] = turned[HD * h : HD * h + HD]
            elif part == 1:
                kt[:, span] = turned
            else:
                vt[:, span] = turned

    each_half(project, lambda: pair_landed(0, ab))
    forward(4)
    send_rows(1, cot)

    def attend(base, hook):
        span = pl.ds(base, own_rows)
        for h in range(6):
            pair = h // 2
            keys = qkv[:, 384 + 128 * pair : 512 + 128 * pair]
            scores = dot(keys, qtz[h, :, span]) + bias[:, span]
            highest = jnp.max(scores, axis=0, keepdims=True)
            exponent = jnp.exp(scores - highest)
            total = jnp.sum(exponent, axis=0, keepdims=True)
            rounded = exponent.astype(BF16)
            pt[h, :, span] = rounded
            share = 1.0 / total
            shares[h, :, span] = share
            mixed = dot(vt[HD * h : HD * h + HD, :], rounded) * share
            ott[HD * h : HD * h + HD, span] = mixed.astype(BF16)
            hook(h)
        orow[span, :] = ott[:, span].T

    def attend_loop(i, carry):
        base = pl.multiple_of(jnp.where(i == 0, theirs, mine), own_rows)

        def hook(h):
            if h == 1:

                @pl.when(i == 0)
                def _():
                    gather_next(3, 0)

            if h == 4:

                @pl.when(i == 0)
                def _():
                    after_z(4)

            if h == 5:

                @pl.when(i == 1)
                def _():
                    gather_next(4, 0)

        attend(base, hook)

        @pl.when(i == 0)
        def _():
            prs[0] = dot_nt(orow[pl.ds(base, own_rows), :], wq[:, 1152:1536]).astype(BF16)
            part_send(0)

        return carry

    lax.fori_loop(0, 2, attend_loop, 0)

    def own_out(i, at, base):
        mid[pl.ds(at, TILE), :] = dot_nt(orow[pl.ds(base, TILE), :], wq[:, 1152:1536])

    own_chunks(own_out)
    part_landed(0)

    def second_norm(i, at, base):
        here = pl.ds(at, TILE)
        middle = xb[i].astype(F32) + (mid[here, :] + prr[0, here, :].astype(F32))
        mid[here, :] = middle
        normed, _ = normalize(middle)
        bnb[pl.ds(base, TILE), :] = (normed * gain_second).astype(BF16)

    own_chunks(second_norm)
    pair_send(1, bnb)
    gather_last(2, 3)

    def expand(base):
        def chunk(i, carry):
            span = pl.ds(pl.multiple_of(base + i * TILE, TILE), TILE)
            source = bnb[span, :]
            for j in range(half):
                pre = dot(source, wts[1, j])
                cdf = 0.5 * (1.0 + lax.erf(pre * 0.7071067811865476))
                density = jnp.exp(pre * pre * -0.5) * 0.3989422804014327
                gact[j, span, :] = (pre * cdf).astype(BF16)
                dgel[j, span, :] = (cdf + pre * density).astype(BF16)
            return carry

        lax.fori_loop(0, chunks, chunk, 0)

    rows_landed(1)
    pair_send(2, dyb)
    each_half(expand, lambda: pair_landed(1, bnb))
    gather_sent(0)

    def grad_tiles(source, slot, width_of):
        def tile(t, carry):
            at = pl.multiple_of(t * TILE, TILE)
            turned = source[:, pl.ds(at, TILE)].T
            width_of(turned, slot, pl.ds(at, TILE))
            return carry

        lax.fori_loop(0, D // TILE, tile, 0)

    def down_tile(turned, slot, span):
        for j in range(half):
            wts[slot, j, span, :] = dot(turned, gact[j]).astype(BF16)

    def up_tile(turned, slot, span):
        for j in range(half):
            wts[slot, j, span, :] = dot(turned, dgel[j]).astype(BF16)

    pair_landed(2, dyb)
    grad_tiles(dyb, place[2], down_tile)
    scatter_step(0, 0)
    gather_last(4)

    def contract(base, j_refs, weight):
        total = dot_nt(j_refs[0, pl.ds(base, TILE), :], wts[weight, 0])
        for j in range(1, half):
            total = total + dot_nt(j_refs[j, pl.ds(base, TILE), :], wts[weight, j])
        return total

    def their_chunks(buffer, weight, into):
        def step(i, carry):
            base = pl.multiple_of(theirs + i * TILE, TILE)
            into[pl.ds(pl.multiple_of(i * TILE, TILE), TILE), :] = contract(
                base, buffer, weight
            ).astype(BF16)
            return carry

        lax.fori_loop(0, chunks, step, 0)

    their_chunks(gact, 2, prs.at[1])
    part_send(1)

    def through_gelu(base):
        def chunk(i, carry):
            span = pl.ds(pl.multiple_of(base + i * TILE, TILE), TILE)
            source = dyb[span, :]
            for j in range(half):
                grad_act = dot(source, wts[2, j])
                dgel[j, span, :] = (grad_act * dgel[j, span, :].astype(F32)).astype(BF16)
            return carry

        lax.fori_loop(0, chunks, chunk, 0)

    each_half(through_gelu)
    part_sent(0)
    their_chunks(dgel, 1, prs.at[0])
    part_send(2)
    part_landed(1)

    def layer_rows(i, at, base):
        here = pl.ds(at, TILE)
        total = contract(base, gact, 2) + prr[1, here, :].astype(F32)
        stage[i] = (mid[here, :] + total).astype(BF16)

    own_chunks(layer_rows)
    send_back(0, y_out)
    pair_sent(2, dyb)
    part_landed(2)

    def second_back(i, at, base):
        here = pl.ds(at, TILE)
        grad = contract(base, dgel, 1) + prr[0, here, :].astype(F32)
        normed, inverse = normalize(mid[here, :])
        gsum[1:2, :] += jnp.sum(grad * normed, axis=0, keepdims=True)
        down = dyb[pl.ds(base, TILE), :].astype(F32) + norm_back(
            grad, gain_second, normed, inverse
        )
        mid[here, :] = down
        dyb[pl.ds(base, TILE), :] = down.astype(BF16)

    own_chunks(second_back)
    pair_send(3, dyb)
    gather_sent(1)
    scatter_next(0, 0)
    grad_tiles(bnb, place[1], up_tile)
    scatter_step(1, 0)

    def spread_mix(base):
        span = pl.ds(base, own_rows)
        result = dot(dyb[span, :], wq[:, 1152:1536])
        result = result.astype(BF16).astype(F32)
        turned = result.T
        pieces = []
        for h in range(6):
            at = HD * (h % 2)
            piece = (turned[HD * h : HD * h + HD] * shares[h, :, span]).astype(BF16)
            pieces.append(piece.astype(F32))
            qtz[h, at : at + HD, span] = piece
            product = piece.astype(F32) * ott[HD * h : HD * h + HD, span].astype(F32)
            delta[h, :, span] = jnp.sum(product, axis=0, keepdims=True)
        dorow[span, :] = jnp.concatenate(pieces, axis=0).T.astype(BF16)

    each_half(spread_mix, lambda: pair_landed(3, dyb))

    def attend_back(pair, carry):
        def tile(offset):
            return pl.ds(pl.multiple_of(offset + 128 * pair, 128), 128)

        parts = []
        for hh in range(2):
            h = 2 * pair + hh
            grad_values = dot(pt[h], dorow[:, tile(0)])
            for q in range(rows // own_rows):
                span = slice(q * own_rows, (q + 1) * own_rows)
                grad_prob = dot(qkv[:, tile(768)], qtz[h, :, span])
                chance = pt[h, :, span].astype(F32)
                pt[h, :, span] = (chance * (grad_prob - delta[h, :, span])).astype(BF16)
            grad_keys = dot(pt[h], qkv[:, tile(0)])
            head = pl.ds(pl.multiple_of(HD * h, HD), HD)
            grad_queries = dot(kt[head, :], pt[h]) * SCALE
            parts.append((grad_queries, grad_keys, grad_values))
        qkv[:, tile(768)] = jnp.where(low, parts[0][2], parts[1][2]).astype(BF16)
        qkv[:, tile(384)] = jnp.where(low, parts[0][1], parts[1][1]).astype(BF16)
        turned = jnp.concatenate([parts[0][0], parts[1][0]], axis=0).T
        qkv[:, tile(0)] = turned.astype(BF16)

        @pl.when(pair == 0)
        def _():
            scatter_last(0)

        @pl.when(pair == 2)
        def _():
            scatter_next(1, 0)

        return carry

    lax.fori_loop(0, 3, attend_back, 0)

    def first_contract(base, size):
        return dot_nt(qkv[pl.ds(base, size), :], wq[:, 0:1152])

    part_sent(1)
    prs[1] = first_contract(theirs, own_rows).astype(BF16)
    part_send(3)
    gather_sent(2)

    def first_tiles(t, carry):
        at = pl.multiple_of(t * TILE, TILE)
        span = pl.ds(at, TILE)
        slot = place[0]
        qkv_part = dot(ab[:, span].T, qkv[...])
        out_part = dot(dyb[:, span].T, orow[...])
        for i, target in ((0, 0), (1, 128), (2, 256)):
            for j in range(2):
                at = 384 * i + 128 * j
                wts[slot, j, span, target : target + 128] = qkv_part[:, at : at + 128].astype(BF16)
        for j in range(2):
            wts[slot, j, span, 640:768] = out_part[:, 128 * j : 128 * j + 128].astype(BF16)
        mixed_q = qkv_part[:, 256:384]
        mixed_k = qkv_part[:, 640:768]
        mixed_v = qkv_part[:, 1024:1152]
        mixed_o = out_part[:, 256:384]
        wts[slot, 0, span, 384:512] = jnp.where(low, mixed_q, roll(mixed_k)).astype(BF16)
        wts[slot, 1, span, 384:512] = jnp.where(low, roll(mixed_q), mixed_k).astype(BF16)
        wts[slot, 0, span, 512:640] = jnp.where(low, mixed_v, roll(mixed_o)).astype(BF16)
        wts[slot, 1, span, 512:640] = jnp.where(low, roll(mixed_v), mixed_o).astype(BF16)
        return carry

    lax.fori_loop(0, D // TILE, first_tiles, 0)
    scatter_step(2, 0)
    scatter_step(3, 0)

    back_sent(0)
    back_landed(0, y_out)
    scatter_relay(0)
    scatter_last(1)
    part_landed(3)

    def first_back(i, at, base):
        here = pl.ds(at, TILE)
        grad = first_contract(base, TILE) + prr[1, here, :].astype(F32)
        normed, inverse = normalize(xb[i].astype(F32))
        gsum[0:1, :] += jnp.sum(grad * normed, axis=0, keepdims=True)
        result = mid[here, :] + norm_back(grad, gain_first, normed, inverse)
        stage[i] = result.astype(BF16)

    own_chunks(first_back)

    me = 2 * z + c
    for index, (cc, zz) in enumerate(column_peers):
        remote(
            gsum,
            sum_rx.at[me],
            sem["sum_s"].at[index],
            sem["sum_r"].at[me],
            device(p, cc, zz),
        ).start()
    pltpu.make_async_copy(gsum, sum_rx.at[me], sem["sum_r"].at[me]).start()
    send_back(1, dx_out)
    scatter_next(2, 0)
    scatter_next(3, 0)
    scatter_relay(1)
    scatter_last(2)
    scatter_last(3)
    for source in range(2 * depth):
        wait_bytes(sum_rx.at[source], sem["sum_r"].at[source])
    for index in range(len(column_peers)):
        wait_bytes(gsum, sem["sum_s"].at[index])
    total = sum_rx[0]
    for source in range(1, 2 * depth):
        total = total + sum_rx[source]
    gsum[...] = total
    for index, pp in enumerate(plane_peers):
        remote(
            gsum, all_rx.at[p], sem["all_s"].at[index], sem["all_r"].at[p], device(pp, c, z)
        ).start()
    pltpu.make_async_copy(gsum, all_rx.at[p], sem["all_r"].at[p]).start()
    scatter_relay(2)
    scatter_relay(3)
    scatter_finish(0)
    for source in range(columns):
        wait_bytes(all_rx.at[source], sem["all_r"].at[source])
    for index in range(len(plane_peers)):
        wait_bytes(gsum, sem["all_s"].at[index])
    total = all_rx[0]
    for source in range(1, columns):
        total = total + all_rx[source]
    place_of = (2 * D // (2 * columns * depth)) * (dp * depth + z)
    wanted = jnp.where(place_of < D, total[0:1, :], total[1:2, :])
    turn = (D - place_of % D) % D
    gm_out[...] = pltpu.roll(jnp.broadcast_to(wanted, (8, D)), turn, 1)[:, 0:128]
    for u in (1, 2, 3):
        scatter_finish(u)

    back_landed(1, dx_out)
    back_sent(1)
    rows_sent(0, tok)
    rows_sent(1, cot)
    pair_sent(0, ab)
    pair_sent(1, bnb)
    pair_sent(3, dyb)
    part_sent(2)
    part_sent(3)
    for u in range(len(SCATTER)):
        scatter_sent(u)


def whole_layer(mesh, tok, cot, first, up, down, gains, padding, lengths):
    depth = mesh.shape["tensor"]
    bit_count = (mesh.shape["dp"] // 2).bit_length() - 1
    columns = 1 << bit_count
    shard = up.shape[0]
    half = depth // 2
    rows = padding.shape[1]
    own = rows // 2
    vmem = pl.BlockSpec(memory_space=pltpu.VMEM)
    hbm = pl.BlockSpec(memory_space=pl.ANY)
    sem = pltpu.SemaphoreType.DMA
    blocks = 1 << (bit_count - 1)
    scratch = [
        ((half, TILE, D), BF16),
        ((rows, D), BF16),
        ((rows, D), BF16),
        ((rows, D), BF16),
        ((KINDS, half, D, D), BF16),
        ((D, 2 * D), BF16),
        ((rows, 1152), BF16),
        ((6, 128, rows), BF16),
        ((384, rows), BF16),
        ((384, rows), BF16),
        ((6, rows, rows), BF16),
        ((rows, rows), F32),
        ((384, rows), BF16),
        ((rows, 384), BF16),
        ((rows, 384), BF16),
        ((own, D), F32),
        ((half, rows, D), BF16),
        ((half, rows, D), BF16),
        ((2, own, D), BF16),
        ((2, own, D), BF16),
        ((half, TILE, D), BF16),
        ((KINDS, 2, columns - 1, half, shard, D), BF16),
        ((KINDS, depth, shard, D), BF16),
        ((KINDS, 2, half, shard, D), BF16),
        ((2 * columns, 8, 128), F32),
        ((8, D), F32),
        ((2, 8, rows), F32),
        ((8, D), F32),
        ((2 * depth, 8, D), F32),
        ((columns, 8, D), F32),
        ((6, 1, rows), F32),
        ((6, 1, rows), F32),
    ]
    sems = {
        "tok_s": (2, 2),
        "tok_r": (2, half),
        "gain_s": (2 * columns,),
        "gain_r": (2 * columns,),
        "code_s": (),
        "code_r": (),
        "z_s": (len(GATHER), depth),
        "z_r": (len(GATHER), 2, half),
        "rel_s": (len(GATHER), 2, half),
        "x_s": (len(GATHER), 2, bit_count, blocks),
        "x_r": (len(GATHER), 2, bit_count, blocks),
        "rs_s": (len(SCATTER), 2, bit_count, blocks),
        "rs_r": (len(SCATTER), 2, bit_count, blocks),
        "rz_s": (len(SCATTER), 2, half),
        "rz_r": (len(SCATTER), depth),
        "far_r": (len(SCATTER), 2, half),
        "out_s": (2, half),
        "out_r": (2, 2),
        "pa_s": (4,),
        "pa_r": (4,),
        "pr_s": (4,),
        "pr_r": (4,),
        "sum_s": (2 * depth - 1,),
        "sum_r": (2 * depth,),
        "all_s": (columns - 1,),
        "all_r": (columns,),
    }
    return pl.pallas_call(
        functools.partial(layer_kernel, depth, bit_count, shard, rows),
        out_shape=(
            jax.ShapeDtypeStruct(tok.shape, BF16),
            jax.ShapeDtypeStruct(tok.shape, BF16),
            jax.ShapeDtypeStruct((KINDS,) + up.shape, F32),
            jax.ShapeDtypeStruct((8, 128), F32),
        ),
        in_specs=[hbm] * 5 + [vmem, vmem, pl.BlockSpec(memory_space=pltpu.SMEM)],
        out_specs=(hbm, hbm, vmem, vmem),
        scratch_shapes=[pltpu.VMEM(shape, dtype) for shape, dtype in scratch]
        + [sem(sems[name]) for name in SEMS],
        compiler_params=pltpu.CompilerParams(
            collective_id=0, has_side_effects=True, vmem_limit_bytes=67043328
        ),
        name="whole_layer",
    )(tok, cot, first, up, down, gains, padding, lengths)


def block_body(mesh, tokens, cotangent, lengths, padding, ln_gain, w_qkv, w_out, w_up, w_down):
    depth = mesh.shape["tensor"]
    shard = w_up.shape[1]
    pair = 2 * HD

    qkv = w_qkv[0]
    out_t = w_out[0].T
    packed = jnp.concatenate(
        [
            qkv[:, 0, :pair],
            qkv[:, 1, :pair],
            qkv[:, 2, :pair],
            qkv[:, 0, pair:],
            qkv[:, 1, pair:],
            qkv[:, 2, pair:],
            out_t[:, pair:],
            out_t[:, :pair],
        ],
        axis=1,
    )
    y_back, dx_back, summed, gain_sum = whole_layer(
        mesh,
        tokens,
        cotangent,
        packed,
        w_up[0],
        w_down[0].T,
        ln_gain[0],
        padding,
        lengths[:, 0],
    )
    gain_result = gain_sum[0, : 2 * D // (mesh.shape["dp"] * depth)]
    first = summed[0]
    qkv_grad = jnp.stack(
        [
            jnp.concatenate(
                [
                    first[:, pair * i : pair * i + pair],
                    first[:, 3 * pair + HD * i : 3 * pair + HD * i + HD],
                ],
                axis=1,
            )
            for i in range(3)
        ],
        axis=1,
    )[None]
    out_grad = jnp.concatenate([first[:, 5 * pair :], first[:, 4 * pair + HD : 5 * pair]], axis=1)
    return (
        y_back.astype(F32),
        dx_back.astype(F32),
        gain_result,
        qkv_grad,
        out_grad.T[None],
        summed[1][None],
        summed[2].T[None],
    )


def visible(lengths_row, padding_row):
    places = lax.iota(jnp.int32, padding_row.shape[0])
    bounds = jnp.cumsum(lengths_row)
    picture = jnp.sum((places[:, None] >= bounds[None, :]).astype(jnp.int32), axis=1)
    same_image = picture[:, None] == picture[None, :]
    return same_image & ((padding_row[None, :] == 1) | (places[:, None] == places[None, :]))


def gelu_exact(pre_values):
    return jax.nn.gelu(pre_values, approximate=False)


def masked_scores(queries, key_rows, allowed):
    scaling = queries.shape[-1] ** (-0.5)
    scores = (
        jnp.einsum("qhd,khd->hqk", queries, key_rows, preferred_element_type=jnp.float32) * scaling
    )
    return (jnp.where(allowed[None], scores, NEGATIVE), scaling)


def attend(stacked, allowed):
    scores, scaling = masked_scores(stacked[:, 0], stacked[:, 1], allowed)
    highest = jnp.max(scores, axis=-1, keepdims=True)
    exponent = jnp.exp(scores - highest)
    totals = jnp.sum(exponent, axis=-1, keepdims=True)
    rounded = (exponent / totals).astype(jnp.bfloat16)
    mixture = jnp.einsum("hqk,khd->qhd", rounded, stacked[:, 2], preferred_element_type=jnp.float32)
    return (mixture, highest, totals)


def attend_back(stacked, allowed, highest, totals, grad_mix):
    queries, key_rows, value_rows = (stacked[:, 0], stacked[:, 1], stacked[:, 2])
    scores, scaling = masked_scores(queries, key_rows, allowed)
    probability = jnp.exp(scores - highest) / totals
    rounded = probability.astype(jnp.bfloat16)
    grad_prob = jnp.einsum("qhd,khd->hqk", grad_mix, value_rows, preferred_element_type=jnp.float32)
    grad_values = jnp.einsum("hqk,qhd->khd", rounded, grad_mix, preferred_element_type=jnp.float32)
    inner_sum = jnp.sum(probability * grad_prob, axis=-1, keepdims=True)
    grad_scores = (probability * (grad_prob - inner_sum)).astype(jnp.bfloat16)
    grad_queries = (
        jnp.einsum("hqk,khd->qhd", grad_scores, key_rows, preferred_element_type=jnp.float32)
        * scaling
    )
    grad_keys = (
        jnp.einsum("hqk,qhd->khd", grad_scores, queries, preferred_element_type=jnp.float32)
        * scaling
    )
    return jnp.stack([grad_queries, grad_keys, grad_values], axis=1).astype(jnp.bfloat16)


def collect_weights(ln_gain, w_qkv, w_out, w_up, w_down, layer_index):
    return (
        lax.all_gather(ln_gain[layer_index], "dp", axis=1, tiled=True),
        lax.all_gather(w_qkv[layer_index], "dp", axis=0, tiled=True),
        lax.all_gather(w_out[layer_index], "dp", axis=1, tiled=True),
        lax.all_gather(w_up[layer_index], "dp", axis=0, tiled=True),
        lax.all_gather(w_down[layer_index], "dp", axis=1, tiled=True),
    )


def spread(block_rows):
    return lax.all_gather(block_rows, "tensor", axis=0, tiled=True)


def spread_grad(block_rows):
    return lax.all_gather(block_rows, "tensor", axis=0, tiled=True)


def collect_rows(operand, weight):
    return lax.psum_scatter(
        jnp.dot(operand, weight, preferred_element_type=jnp.float32),
        "tensor",
        scatter_dimension=0,
        tiled=True,
    )


def return_rows(operand, weight):
    return lax.psum_scatter(
        lax.dot_general(
            operand, weight, (((1,), (1,)), ((), ())), preferred_element_type=jnp.float32
        ),
        "tensor",
        scatter_dimension=0,
        tiled=True,
    )


def reduce_grads(pieces):
    return (
        lax.psum_scatter(pieces[0], "dp", scatter_dimension=0, tiled=True),
        lax.psum_scatter(pieces[1], "dp", scatter_dimension=1, tiled=True),
        lax.psum_scatter(pieces[2], "dp", scatter_dimension=0, tiled=True),
        lax.psum_scatter(pieces[3], "dp", scatter_dimension=1, tiled=True),
    )


def body(tokens, cotangent, lengths, padding, ln_gain, w_qkv, w_out, w_up, w_down):
    layer_count = w_qkv.shape[0]
    micro_count = tokens.shape[0]
    residual = [tokens[batch_index].astype(jnp.float32) for batch_index in range(micro_count)]
    visibility = [
        visible(lengths[batch_index, 0], padding[batch_index]) for batch_index in range(micro_count)
    ]
    saved = []
    stored_weights = []
    layer_index = 0
    stored_weights.append(None)
    for batch_index in range(micro_count):
        weights = collect_weights(ln_gain, w_qkv, w_out, w_up, w_down, layer_index)
        gain_pair, qkv_weight, out_weight, up_weight, down_weight = weights
        gain_first = gain_pair[0].astype(jnp.float32)
        gain_second = gain_pair[1].astype(jnp.float32)
        entering = residual[batch_index]
        normed, inverse = normalize(entering)
        first_input = spread((normed * gain_first).astype(jnp.bfloat16))
        triple = jnp.einsum(
            "rd,dcn->rcn", first_input, qkv_weight, preferred_element_type=jnp.float32
        ).astype(jnp.bfloat16)
        stacked = triple.reshape(triple.shape[0], 3, -1, HD)
        mixture, highest, totals = attend(stacked, visibility[batch_index])
        mix_rounded = mixture.reshape(mixture.shape[0], -1).astype(jnp.bfloat16)
        middle = entering + collect_rows(mix_rounded, out_weight)
        normed_two, inverse_two = normalize(middle)
        second_input = spread((normed_two * gain_second).astype(jnp.bfloat16))
        hidden_pre = jnp.dot(second_input, up_weight, preferred_element_type=jnp.float32)
        activated = gelu_exact(hidden_pre).astype(jnp.bfloat16)
        residual[batch_index] = middle + collect_rows(activated, down_weight)
        saved.append(
            (
                entering,
                first_input,
                stacked,
                highest,
                totals,
                mix_rounded,
                middle,
                second_input,
                hidden_pre,
                activated,
            )
        )
    gradients = [cotangent[batch_index].astype(jnp.float32) for batch_index in range(micro_count)]
    gain_parts = [jnp.zeros((2, D), jnp.float32)]
    weight_results = [None]
    for layer_index in reversed(range(layer_count)):
        summed = None
        for batch_index in range(micro_count):
            weights = collect_weights(ln_gain, w_qkv, w_out, w_up, w_down, layer_index)
            gain_pair, qkv_weight, out_weight, up_weight, down_weight = weights
            gain_first = gain_pair[0].astype(jnp.float32)
            gain_second = gain_pair[1].astype(jnp.float32)
            (
                entering,
                first_input,
                stacked,
                highest,
                totals,
                mix_rounded,
                middle,
                second_input,
                hidden_pre,
                activated,
            ) = saved[layer_index * micro_count + batch_index]
            incoming = gradients[batch_index]
            grad_down = spread_grad(incoming.astype(jnp.bfloat16))
            down_part = jnp.einsum(
                "rf,rd->fd", activated, grad_down, preferred_element_type=jnp.float32
            )
            grad_act = lax.dot_general(
                grad_down, down_weight, (((1,), (1,)), ((), ())), preferred_element_type=jnp.float32
            )
            pulled = jax.vjp(gelu_exact, hidden_pre)
            grad_pre = pulled[1](grad_act)[0].astype(jnp.bfloat16)
            up_part = jnp.einsum(
                "rd,rf->df", second_input, grad_pre, preferred_element_type=jnp.float32
            )
            grad_norm_two = return_rows(grad_pre, up_weight)
            normed_two, inverse_two = normalize(middle)
            gain_two_part = jnp.sum(grad_norm_two * normed_two, axis=0)
            incoming = incoming + norm_back(grad_norm_two, gain_second, normed_two, inverse_two)
            grad_branch = spread_grad(incoming.astype(jnp.bfloat16))
            out_part = jnp.einsum(
                "rk,rd->kd", mix_rounded, grad_branch, preferred_element_type=jnp.float32
            )
            grad_mix = lax.dot_general(
                grad_branch,
                out_weight,
                (((1,), (1,)), ((), ())),
                preferred_element_type=jnp.float32,
            )
            grad_mix = grad_mix.astype(jnp.bfloat16).reshape(grad_mix.shape[0], -1, HD)
            grad_triple = attend_back(stacked, visibility[batch_index], highest, totals, grad_mix)
            flat_triple = grad_triple.reshape(grad_triple.shape[0], 3, -1)
            qkv_part = jnp.einsum(
                "rd,rcn->dcn", first_input, flat_triple, preferred_element_type=jnp.float32
            )
            grad_norm_one = return_rows(
                flat_triple.reshape(flat_triple.shape[0], -1),
                qkv_weight.reshape(qkv_weight.shape[0], -1),
            )
            normed, inverse = normalize(entering)
            gain_one_part = jnp.sum(grad_norm_one * normed, axis=0)
            incoming = incoming + norm_back(grad_norm_one, gain_first, normed, inverse)
            gradients[batch_index] = incoming
            gain_parts[layer_index] = gain_parts[layer_index] + jnp.stack(
                [gain_one_part, gain_two_part]
            )
            pieces = (qkv_part, out_part, up_part, down_part)
            if summed is None:
                summed = pieces
            else:
                summed = tuple((older + newer for older, newer in zip(summed, pieces)))
        summed = reduce_grads(summed)
        weight_results[layer_index] = summed
    gain_flat = jnp.stack(gain_parts).reshape(-1)
    gain_result = lax.psum_scatter(gain_flat, ("dp", "tensor"), scatter_dimension=0, tiled=True)
    layer_out = jnp.stack(residual)
    input_grad = jnp.stack(gradients)
    qkv_grad = jnp.stack([weight_results[0][0]])
    out_grad = jnp.stack([weight_results[0][1]])
    up_grad = jnp.stack([weight_results[0][2]])
    down_grad = jnp.stack([weight_results[0][3]])
    return (layer_out, input_grad, gain_result, qkv_grad, out_grad, up_grad, down_grad)


def fits(mesh, tokens, w_qkv):
    dp_size, depth = mesh.shape["dp"], mesh.shape["tensor"]
    columns = dp_size // 2
    return (
        depth == 4
        and dp_size >= 4
        and columns & (columns - 1) == 0
        and D == dp_size * 2 * HALF
        and tokens.shape[0] == 2
        and tokens.shape[1] == dp_size * depth * TILE
        and w_qkv.shape[0] == 1
    )


def solution(mesh):
    def run(tokens, cotangent, lengths, padding, ln_gain, w_qkv, *rest):
        one_block = fits(mesh, tokens, w_qkv)
        program = functools.partial(block_body, mesh) if one_block else body
        return jax.shard_map(
            program,
            mesh=mesh,
            in_specs=(
                P(None, ("dp", "tensor"), None),
                P(None, ("dp", "tensor"), None),
                P(None, "dp", None),
                P(None, "dp"),
                P(None, None, "dp"),
                P(None, "dp", None, "tensor"),
                P(None, "tensor", "dp"),
                P(None, "dp", "tensor"),
                P(None, "tensor", "dp"),
            ),
            out_specs=(
                P(None, ("dp", "tensor"), None),
                P(None, ("dp", "tensor"), None),
                P(("dp", "tensor")),
                P(None, "dp", None, "tensor"),
                P(None, "tensor", "dp"),
                P(None, "dp", "tensor"),
                P(None, "tensor", "dp"),
            ),
            check_vma=False,
        )(tokens, cotangent, lengths, padding, ln_gain, w_qkv, *rest)

    return run
```

```python
import functools

import jax
import jax.numpy as jnp
from jax import lax
from jax.experimental import pallas as pl
from jax.experimental.pallas import tpu as pltpu
from jax.sharding import PartitionSpec as P

D = 768
HD = 64
NEGATIVE = -1e30
EPSILON = 1e-06
MESH = pl.DeviceIdType.MESH
F32 = jnp.float32
BF16 = jnp.bfloat16
KINDS = 3
HALF = 48
GATHER = (
    (0, 0, 16),
    (0, 16, 32),
    (0, HALF, HALF),
    (1, 0, HALF),
    (1, HALF, HALF),
    (2, 0, 2 * HALF),
)
SCATTER = (
    (2, 0, HALF),
    (2, HALF, HALF),
    (1, 0, HALF),
    (1, HALF, HALF),
    (0, 0, HALF),
    (0, HALF, HALF),
)
RELAYED = (2, 1, 0)
TILE = 256
SCALE = HD**-0.5


def flip(value, bit):
    size = 1 << bit
    return value + size * (1 - 2 * ((value // size) % 2))


def flip_mask(value, mask):
    bit = 0
    while mask >> bit:
        if (mask >> bit) & 1:
            value = flip(value, bit)
        bit += 1
    return value


def submasks(bits):
    masks = [0]
    for bit in bits:
        masks = masks + [mask | (1 << bit) for mask in masks]
    return masks


def color_order(color, bit_count):
    order = list(range(bit_count))
    return order if color == 0 else order[::-1]


def device(p, c, z):
    return (2 * p + c, z)


def dot(left, right):
    return jnp.dot(left, right, preferred_element_type=F32)


def dot_nt(left, right):
    return lax.dot_general(left, right, (((1,), (1,)), ((), ())), preferred_element_type=F32)


def normalize(row_block):
    average = jnp.mean(row_block, axis=-1, keepdims=True)
    centred = row_block - average
    variance = jnp.mean(centred * centred, axis=-1, keepdims=True)
    inverse = lax.rsqrt(variance + EPSILON)
    return (centred * inverse, inverse)


def norm_back(grad_out, gain_row, normed, inverse):
    scaled = grad_out * gain_row
    mean_grad = jnp.mean(scaled, axis=-1, keepdims=True)
    second = jnp.mean(scaled * normed, axis=-1, keepdims=True)
    return inverse * (scaled - mean_grad - normed * second)


def remote(source, target, send_sem, recv_sem, dest):
    return pltpu.make_async_remote_copy(
        source, target, send_sem, recv_sem, device_id=dest, device_id_type=MESH
    )


def wait_bytes(ref, sem):
    pltpu.make_async_copy(ref, ref, sem).wait()


SEMS = (
    "tok_s",
    "tok_r",
    "gain_s",
    "gain_r",
    "code_s",
    "code_r",
    "z_s",
    "z_r",
    "rel_s",
    "x_s",
    "x_r",
    "rs_s",
    "rs_r",
    "rz_s",
    "rz_r",
    "far_r",
    "out_s",
    "out_r",
    "pa_s",
    "pa_r",
    "pr_s",
    "pr_r",
    "sum_s",
    "sum_r",
    "all_s",
    "all_r",
)


def layer_kernel(depth, bit_count, shard, rows, *refs):
    (tok, cot, first_in, up_in, down_in, gain_in, pad_in, length_in) = refs[:8]
    (y_out, dx_out, g_out, gm_out) = refs[8:12]
    (
        xb,
        dyb,
        ab,
        bnb,
        wts,
        wq,
        qkv,
        qtz,
        vt,
        kt,
        pt,
        bias,
        ott,
        orow,
        dorow,
        mid,
        gact,
        dgel,
        prs,
        prr,
        stage,
        rx,
        zrx,
        far_rx,
        gbuf,
        gains,
        code,
        gsum,
        sum_rx,
        all_rx,
        delta,
        shares,
    ) = refs[12:44]
    sem = dict(zip(SEMS, refs[44:]))
    half = depth // 2
    columns = 1 << bit_count
    own_rows = rows // 2
    chunks = own_rows // TILE
    dp = lax.axis_index("dp")
    z = lax.axis_index("tensor")
    c = dp % 2
    p = dp // 2
    buddy = device(p, 1 - c, z)
    mine = pl.multiple_of(own_rows * c, own_rows)
    theirs = pl.multiple_of(own_rows * (1 - c), own_rows)
    lane = lax.broadcasted_iota(jnp.int32, (1, 128), 1)
    low = lane < HD

    def same(to_c, to_z):
        return jnp.logical_and(to_c == c, to_z == z)

    def send_or_copy(is_self, source, target, send_sem, recv_sem, dest):
        @pl.when(is_self)
        def _():
            pltpu.make_async_copy(source, target, recv_sem).start()

        @pl.when(jnp.logical_not(is_self))
        def _():
            remote(source, target, send_sem, recv_sem, dest).start()

    def wait_send(is_self, source, send_sem):
        @pl.when(jnp.logical_not(is_self))
        def _():
            wait_bytes(source, send_sem)

    column_peers = []
    for dz in range(depth):
        for dc in range(2):
            if dz or dc:
                column_peers.append((c if dc == 0 else 1 - c, (z + dz) % depth))
    plane_peers = [flip_mask(p, mask) for mask in range(1, columns)]

    def entry_barrier():
        barrier = pltpu.get_barrier_semaphore()
        peers = [device(p, cc, zz) for cc, zz in column_peers]
        peers += [device(pp, c, z) for pp in plane_peers]
        peers += [device(pp, 1 - c, z) for pp in plane_peers]
        for peer in peers:
            pl.semaphore_signal(barrier, inc=1, device_id=peer, device_id_type=MESH)
        pl.semaphore_wait(barrier, len(peers))

    def make_small():
        gbuf[dp] = jnp.zeros(gbuf.shape[1:], F32)
        gbuf[dp, 0:2, 0:shard] = gain_in[...].astype(F32)
        places = lax.broadcasted_iota(jnp.int32, (1, rows), 1)
        for m in range(2):
            image = jnp.zeros((1, rows), jnp.int32)
            bound = 0
            for k in range(length_in.shape[1]):
                bound = bound + length_in[m, k]
                image = image + (places >= bound).astype(jnp.int32)
            key = jnp.where(pad_in[m : m + 1, :] == 1, image, -1)
            code[c, m : m + 1, :] = image.astype(F32)
            code[c, 2 + m : 3 + m, :] = key.astype(F32)

    def send_small():
        remote(code.at[c], code.at[c], sem["code_s"], sem["code_r"], buddy).start()
        index = 0
        for pp in [p] + plane_peers:
            for cc in (c, 1 - c):
                if index:
                    remote(
                        gbuf.at[dp],
                        gbuf.at[dp],
                        sem["gain_s"].at[index],
                        sem["gain_r"].at[dp],
                        device(pp, cc, z),
                    ).start()
                index += 1

    def finish_small():
        wait_bytes(code.at[c], sem["code_s"])
        wait_bytes(code.at[1 - c], sem["code_r"])
        index = 0
        for pp in [p] + plane_peers:
            for cc in (c, 1 - c):
                if index:
                    wait_bytes(gbuf.at[dp], sem["gain_s"].at[index])
                    source = 2 * pp + cc
                    wait_bytes(gbuf.at[source], sem["gain_r"].at[source])
                index += 1
        rest = jnp.zeros((8, D - 128), F32)
        total = jnp.zeros((8, D), F32)
        for source in range(2 * columns):
            wide = jnp.concatenate([gbuf[source], rest], axis=1)
            total = total + (pltpu.roll(wide, shard * source, 1) if source else wide)
        gains[...] = total

    def row_targets():
        for m in range(2):
            to_z, to_c = 2 * m + c, z // half
            yield m, to_c, to_z, same(to_c, to_z)

    def row_target(which, slot):
        if which == 0:
            return xb.at[slot]
        return dyb.at[pl.ds(pl.multiple_of(own_rows * c + TILE * slot, TILE), TILE)]

    def row_landing(which, slot, to_c):
        if which == 0:
            return xb.at[slot]
        return dyb.at[pl.ds(pl.multiple_of(own_rows * to_c + TILE * slot, TILE), TILE)]

    def send_rows(which, array):
        for m, to_c, to_z, is_self in row_targets():
            slot = z % half
            send_or_copy(
                is_self,
                array.at[m],
                row_landing(which, slot, to_c),
                sem["tok_s"].at[which, m],
                sem["tok_r"].at[which, slot],
                device(p, to_c, to_z),
            )

    def rows_sent(which, array):
        for m, to_c, to_z, is_self in row_targets():
            wait_send(is_self, array.at[m], sem["tok_s"].at[which, m])

    def rows_landed(which):
        for slot in range(half):
            wait_bytes(row_target(which, slot), sem["tok_r"].at[which, slot])

    def send_back(which, target):
        for slot in range(half):
            to_c, to_z = z % 2, half * c + slot
            send_or_copy(
                same(to_c, to_z),
                stage.at[slot],
                target.at[z // 2],
                sem["out_s"].at[which, slot],
                sem["out_r"].at[which, z // 2],
                device(p, to_c, to_z),
            )

    def back_sent(which):
        for slot in range(half):
            is_self = same(z % 2, half * c + slot)
            wait_send(is_self, stage.at[slot], sem["out_s"].at[which, slot])

    def back_landed(which, target):
        for m in range(2):
            wait_bytes(target.at[m], sem["out_r"].at[which, m])

    last = depth - 1

    def two_ends(low_core, high_core):
        return jnp.logical_or(
            jnp.logical_and(c == 0, z == low_core), jnp.logical_and(c == 1, z == high_core)
        )

    ends = two_ends(last, 0)
    relays = two_ends(last - 1, 1)
    relay_to = device(p, c, last * (1 - c))
    relay_from = device(p, c, last - 1 + c * (2 - last))

    def unit_rows(unit, column, color):
        _, start, size = unit
        return pl.ds(pl.multiple_of((2 * column + color) * shard + start, 16), size)

    def unit_source(unit):
        return (first_in, up_in, down_in)[unit[0]].at[pl.ds(unit[1], unit[2])]

    def z_targets():
        for dz in range(depth):
            to_z = (z + dz) % depth
            yield dz, z // half, to_z, to_z == last * (1 - z // half)

    def gather_z(u):
        unit = GATHER[u]
        for dz, to_c, to_z, far in z_targets():
            source = unit_source(unit)
            target = wts.at[unit[0], z % half, unit_rows(unit, p, c)]
            recv = sem["z_r"].at[u, c, z % half]
            if dz == 0:
                send_or_copy(
                    to_c == c, source, target, sem["z_s"].at[u, dz], recv, device(p, to_c, to_z)
                )
            else:

                @pl.when(jnp.logical_not(far))
                def _():
                    remote(
                        source, target, sem["z_s"].at[u, dz], recv, device(p, to_c, to_z)
                    ).start()

    def gather_z_sent(u):
        for dz, to_c, to_z, far in z_targets():
            skip = to_c == c if dz == 0 else far
            wait_send(skip, unit_source(GATHER[u]), sem["z_s"].at[u, dz])

    def relay_block(u, color, slot):
        unit = GATHER[u]
        return wts.at[unit[0], slot, unit_rows(unit, p, color)]

    def gather_z_landed(u):
        unit = GATHER[u]
        for color in range(2):
            for slot in range(half):
                wait_bytes(
                    wts.at[unit[0], slot, unit_rows(unit, p, color)], sem["z_r"].at[u, color, slot]
                )

    def forward(u):
        @pl.when(relays)
        def _():
            gather_z_landed(u)
            for color in range(2):
                for slot in range(half):
                    block = relay_block(u, color, slot)
                    remote(
                        block,
                        block,
                        sem["rel_s"].at[u, color, slot],
                        sem["z_r"].at[u, color, slot],
                        relay_to,
                    ).start()

    def after_z(u):
        pl.when(jnp.logical_not(relays))(functools.partial(gather_z_landed, u))
        gather_step(u, 0)

    def gather_blocks(u, color, s, landed):
        unit = GATHER[u]
        order = color_order(color, bit_count)
        for index, mask in enumerate(submasks(order[:s])):
            column = flip_mask(p, mask)
            if landed:
                column = flip(column, order[s])
            yield index, wts.at[unit[0], :, unit_rows(unit, column, color)]

    def gather_step(u, s):
        for color in range(2):
            to = device(flip(p, color_order(color, bit_count)[s]), c, z)
            for index, block in gather_blocks(u, color, s, False):
                remote(
                    block,
                    block,
                    sem["x_s"].at[u, color, s, index],
                    sem["x_r"].at[u, color, s, index],
                    to,
                ).start()

    def gather_next(u, s):
        for color in range(2):
            for index, block in gather_blocks(u, color, s, True):
                wait_bytes(block, sem["x_r"].at[u, color, s, index])
        if s + 1 < bit_count:
            gather_step(u, s + 1)

    def gather_last(*units):
        for u in units:
            for s in range(1, bit_count):
                gather_next(u, s)

    def gather_sent(k):
        for u, unit in enumerate(GATHER):
            if unit[0] == k:
                gather_unit_sent(u)

    def gather_unit_sent(u):
        gather_z_sent(u)

        @pl.when(relays)
        def _():
            for color in range(2):
                for slot in range(half):
                    wait_bytes(relay_block(u, color, slot), sem["rel_s"].at[u, color, slot])

        for color in range(2):
            for s in range(bit_count):
                for index, block in gather_blocks(u, color, s, False):
                    wait_bytes(block, sem["x_s"].at[u, color, s, index])

    place = {2: 0, 1: 1, 0: 2}

    def rx_slot(u, color, s, index):
        unit = SCATTER[u]
        slot = (1 << bit_count) - (1 << (bit_count - s)) + index
        return rx.at[unit[0], color, slot, :, pl.ds(unit[1], unit[2])]

    def scatter_order(color):
        return color_order(color, bit_count)[::-1]

    def scatter_blocks(u, color, s, away):
        unit = SCATTER[u]
        order = scatter_order(color)
        for index, mask in enumerate(submasks(order[s + 1 :])):
            column = flip_mask(p, mask)
            if away:
                column = flip(column, order[s])
            yield index, wts.at[place[unit[0]], :, unit_rows(unit, column, color)]

    def scatter_step(u, s):
        for color in range(2):
            to = device(flip(p, scatter_order(color)[s]), c, z)
            for index, block in scatter_blocks(u, color, s, True):
                remote(
                    block,
                    rx_slot(u, color, s, index),
                    sem["rs_s"].at[u, color, s, index],
                    sem["rs_r"].at[u, color, s, index],
                    to,
                ).start()

    def scatter_next(u, s):
        for color in range(2):
            for index, block in scatter_blocks(u, color, s, False):
                got = rx_slot(u, color, s, index)
                wait_bytes(got, sem["rs_r"].at[u, color, s, index])
                block[...] = (block[...].astype(F32) + got[...].astype(F32)).astype(BF16)
        if s + 1 < bit_count:
            scatter_step(u, s + 1)
        else:
            scatter_z(u)

    def scatter_last(*units):
        for u in units:
            for s in range(1, bit_count):
                scatter_next(u, s)

    def scatter_z_blocks(u):
        unit = SCATTER[u]
        for color in range(2):
            for slot in range(half):
                to_z = half * c + slot
                block = wts.at[place[unit[0]], slot, unit_rows(unit, p, color)]
                yield color, slot, to_z, block

    def summed_on_the_way(u):
        return SCATTER[u][0] in RELAYED

    def landing(u, source):
        unit = SCATTER[u]
        return zrx.at[unit[0], source, pl.ds(unit[1], unit[2])]

    def far_landing(u, color, slot):
        unit = SCATTER[u]
        return far_rx.at[unit[0], color, slot, pl.ds(unit[1], unit[2])]

    def scatter_z(u):
        for color, slot, to_z, block in scatter_z_blocks(u):
            send, recv = sem["rz_s"].at[u, color, slot], sem["rz_r"].at[u, z]
            dest = device(p, color, to_z)
            if not summed_on_the_way(u):
                send_or_copy(same(color, to_z), block, landing(u, z), send, recv, dest)
                continue

            @pl.when(jnp.logical_not(jnp.logical_or(ends, relays)))
            def _():
                send_or_copy(same(color, to_z), block, landing(u, z), send, recv, dest)

            @pl.when(ends)
            def _():
                remote(
                    block,
                    far_landing(u, color, slot),
                    send,
                    sem["far_r"].at[u, color, slot],
                    relay_from,
                ).start()

    def scatter_relay(u):
        @pl.when(relays)
        def _():
            for color, slot, to_z, block in scatter_z_blocks(u):
                got = far_landing(u, color, slot)
                wait_bytes(got, sem["far_r"].at[u, color, slot])
                block[...] = (block[...].astype(F32) + got[...].astype(F32)).astype(BF16)
                send, recv = sem["rz_s"].at[u, color, slot], sem["rz_r"].at[u, z]
                dest = device(p, color, to_z)
                send_or_copy(same(color, to_z), block, landing(u, z), send, recv, dest)

    def scatter_finish(u):
        unit = SCATTER[u]
        for source in range(depth):
            got = functools.partial(wait_bytes, landing(u, source), sem["rz_r"].at[u, source])
            if summed_on_the_way(u) and source in (0, last):
                pl.when(z // half != (last - source) // half)(got)
            else:
                got()
        total = landing(u, 0)[...].astype(F32)
        for source in range(1, depth):
            total = total + landing(u, source)[...].astype(F32)
        g_out[unit[0], unit[1] : unit[1] + unit[2]] = total

    def scatter_sent(u):
        for color in range(2):
            for s in range(bit_count):
                for index, block in scatter_blocks(u, color, s, True):
                    wait_bytes(block, sem["rs_s"].at[u, color, s, index])
        for color, slot, to_z, block in scatter_z_blocks(u):
            local = same(color, to_z)
            if summed_on_the_way(u):
                local = jnp.logical_and(local, jnp.logical_not(ends))
            wait_send(local, block, sem["rz_s"].at[u, color, slot])

    def clear_far():
        for source in (0, last):

            @pl.when(z // half == (last - source) // half)
            def _():
                for k in RELAYED:
                    zrx[k, source] = jnp.zeros(zrx.shape[2:], BF16)

    def pair_send(index, buffer):
        own = buffer.at[pl.ds(mine, own_rows)]
        remote(own, own, sem["pa_s"].at[index], sem["pa_r"].at[index], buddy).start()

    def pair_landed(index, buffer):
        wait_bytes(buffer.at[pl.ds(theirs, own_rows)], sem["pa_r"].at[index])

    def pair_sent(index, buffer):
        wait_bytes(buffer.at[pl.ds(mine, own_rows)], sem["pa_s"].at[index])

    def part_send(index):
        remote(
            prs.at[index % 2],
            prr.at[index % 2],
            sem["pr_s"].at[index],
            sem["pr_r"].at[index],
            buddy,
        ).start()

    def part_landed(index):
        wait_bytes(prr.at[index % 2], sem["pr_r"].at[index])

    def part_sent(index):
        wait_bytes(prs.at[index % 2], sem["pr_s"].at[index])

    def each_half(body, second=None):
        def step(i, carry):
            if second is not None:
                pl.when(i == 1)(second)
            body(pl.multiple_of(jnp.where(i == 0, mine, theirs), own_rows))
            return carry

        lax.fori_loop(0, 2, step, 0)

    def own_chunks(body):
        def step(i, carry):
            body(i, pl.multiple_of(i * TILE, TILE), pl.multiple_of(mine + i * TILE, TILE))
            return carry

        lax.fori_loop(0, chunks, step, 0)

    make_small()
    entry_barrier()
    send_small()
    for u in range(5):
        gather_z(u)
    send_rows(0, tok)

    for h in range(6):
        qtz[h, HD * (1 - h % 2) : HD * (1 - h % 2) + HD, :] = jnp.zeros((HD, rows), BF16)
    gsum[...] = jnp.zeros(gsum.shape, F32)
    clear_far()
    forward(0)
    after_z(0)
    finish_small()
    gain_first = gains[0:1, :]
    gain_second = gains[1:2, :]
    forward(1)
    after_z(1)
    gather_next(0, 0)

    forward(2)
    after_z(2)
    gather_next(1, 0)
    forward(3)
    after_z(3)
    gather_next(2, 0)
    forward(4)
    after_z(4)
    gather_z(5)
    micro = z // 2
    owner = z % 2
    query_image = code[owner, pl.ds(micro, 1), :]
    key_code = code[owner, pl.ds(2 + micro, 1), :]
    key_columns = jnp.broadcast_to(key_code, (128, rows)).T
    for block in range(rows // 128):
        span = slice(128 * block, 128 * block + 128)
        key = key_columns[span, 0:1]
        row_id = lax.broadcasted_iota(jnp.int32, (128, rows), 0) + 128 * block
        col_id = lax.broadcasted_iota(jnp.int32, (128, rows), 1)
        seen = jnp.logical_or(key == query_image, row_id == col_id)
        bias[span, :] = jnp.where(seen, 0.0, NEGATIVE)

    gather_next(3, 0)
    rows_landed(0)

    def first_norm(i, at, base):
        normed, _ = normalize(xb[i].astype(F32))
        ab[pl.ds(base, TILE), :] = (normed * gain_first).astype(BF16)

    own_chunks(first_norm)
    pair_send(0, ab)
    gather_last(0, 1, 2)

    def roll(value):
        return pltpu.roll(value, HD, 1)

    for name, offset in (("q", 0), ("k", 384), ("v", 768), ("o", 1152)):
        tile = {"q": 0, "k": 128, "v": 256, "o": 640}[name]
        wq[:, offset : offset + 128] = wts[0, 0, :, tile : tile + 128]
        wq[:, offset + 128 : offset + 256] = wts[0, 1, :, tile : tile + 128]
        mixed = {"q": 384, "k": 384, "v": 512, "o": 512}[name]
        one = wts[0, 0, :, mixed : mixed + 128].astype(F32)
        two = wts[0, 1, :, mixed : mixed + 128].astype(F32)
        if name in ("q", "v"):
            both = jnp.where(low, one, roll(two))
        else:
            both = jnp.where(low, roll(one), two)
        wq[:, offset + 256 : offset + 384] = both.astype(BF16)

    def project(base):
        span = pl.ds(base, own_rows)
        source = ab[span, :]
        for part in range(3):
            result = dot(source, wq[:, 384 * part : 384 * part + 384])
            if part == 0:
                result = result * SCALE
            qkv[span, 384 * part : 384 * part + 384] = result.astype(BF16)
            turned = result.T.astype(BF16)
            if part == 0:
                for h in range(6):
                    at = HD * (h % 2)
                    qtz[h, at : at + HD, span] = turned[HD * h : HD * h + HD]
            elif part == 1:
                kt[:, span] = turned
            else:
                vt[:, span] = turned

    forward(5)
    each_half(project, lambda: pair_landed(0, ab))

    def attend(base, hook):
        span = pl.ds(base, own_rows)
        for h in range(6):
            pair = h // 2
            keys = qkv[:, 384 + 128 * pair : 512 + 128 * pair]
            scores = dot(keys, qtz[h, :, span]) + bias[:, span]
            highest = jnp.max(scores, axis=0, keepdims=True)
            exponent = jnp.exp(scores - highest)
            total = jnp.sum(exponent, axis=0, keepdims=True)
            rounded = exponent.astype(BF16)
            pt[h, :, span] = rounded
            share = 1.0 / total
            shares[h, :, span] = share
            mixed = dot(vt[HD * h : HD * h + HD, :], rounded) * share
            ott[HD * h : HD * h + HD, span] = mixed.astype(BF16)
            hook(h)
        orow[span, :] = ott[:, span].T

    def attend_loop(i, carry):
        base = pl.multiple_of(jnp.where(i == 0, theirs, mine), own_rows)

        def hook(h):
            if h == 0:

                @pl.when(i == 1)
                def _():
                    send_rows(1, cot)

            if h == 1:

                @pl.when(i == 0)
                def _():
                    gather_next(4, 0)

            if h == 4:

                @pl.when(i == 0)
                def _():
                    after_z(5)

            if h == 5:

                @pl.when(i == 1)
                def _():
                    gather_next(5, 0)

        attend(base, hook)

        @pl.when(i == 0)
        def _():
            prs[0] = dot_nt(orow[pl.ds(base, own_rows), :], wq[:, 1152:1536]).astype(BF16)
            part_send(0)

        return carry

    lax.fori_loop(0, 2, attend_loop, 0)

    def own_out(i, at, base):
        mid[pl.ds(at, TILE), :] = dot_nt(orow[pl.ds(base, TILE), :], wq[:, 1152:1536])

    own_chunks(own_out)
    part_landed(0)

    def second_norm(i, at, base):
        here = pl.ds(at, TILE)
        middle = xb[i].astype(F32) + (mid[here, :] + prr[0, here, :].astype(F32))
        mid[here, :] = middle
        normed, _ = normalize(middle)
        bnb[pl.ds(base, TILE), :] = (normed * gain_second).astype(BF16)

    own_chunks(second_norm)
    pair_send(1, bnb)
    gather_last(3, 4)

    def expand(base):
        def chunk(i, carry):
            span = pl.ds(pl.multiple_of(base + i * TILE, TILE), TILE)
            source = bnb[span, :]
            for j in range(half):
                pre = dot(source, wts[1, j])
                cdf = 0.5 * (1.0 + lax.erf(pre * 0.7071067811865476))
                density = jnp.exp(pre * pre * -0.5) * 0.3989422804014327
                gact[j, span, :] = (pre * cdf).astype(BF16)
                dgel[j, span, :] = (cdf + pre * density).astype(BF16)
            return carry

        lax.fori_loop(0, chunks, chunk, 0)

    rows_landed(1)
    pair_send(2, dyb)
    each_half(expand, lambda: pair_landed(1, bnb))
    gather_sent(0)

    def grad_tiles(source, slot, width_of):
        def tile(t, carry):
            at = pl.multiple_of(t * TILE, TILE)
            turned = source[:, pl.ds(at, TILE)].T
            width_of(turned, slot, pl.ds(at, TILE))
            return carry

        lax.fori_loop(0, D // TILE, tile, 0)

    def down_tile(turned, slot, span):
        for j in range(half):
            wts[slot, j, span, :] = dot(turned, gact[j]).astype(BF16)

    def up_tile(turned, slot, span):
        for j in range(half):
            wts[slot, j, span, :] = dot(turned, dgel[j]).astype(BF16)

    pair_landed(2, dyb)
    grad_tiles(dyb, place[2], down_tile)
    scatter_step(0, 0)
    scatter_step(1, 0)
    gather_last(5)

    def contract(base, j_refs, weight):
        total = dot_nt(j_refs[0, pl.ds(base, TILE), :], wts[weight, 0])
        for j in range(1, half):
            total = total + dot_nt(j_refs[j, pl.ds(base, TILE), :], wts[weight, j])
        return total

    def their_chunks(buffer, weight, into):
        def step(i, carry):
            base = pl.multiple_of(theirs + i * TILE, TILE)
            into[pl.ds(pl.multiple_of(i * TILE, TILE), TILE), :] = contract(
                base, buffer, weight
            ).astype(BF16)
            return carry

        lax.fori_loop(0, chunks, step, 0)

    their_chunks(gact, 2, prs.at[1])
    part_send(1)

    def through_gelu(base):
        def chunk(i, carry):
            span = pl.ds(pl.multiple_of(base + i * TILE, TILE), TILE)
            source = dyb[span, :]
            for j in range(half):
                grad_act = dot(source, wts[2, j])
                dgel[j, span, :] = (grad_act * dgel[j, span, :].astype(F32)).astype(BF16)
            return carry

        lax.fori_loop(0, chunks, chunk, 0)

    each_half(through_gelu)
    part_sent(0)
    their_chunks(dgel, 1, prs.at[0])
    part_send(2)
    part_landed(1)

    def layer_rows(i, at, base):
        here = pl.ds(at, TILE)
        total = contract(base, gact, 2) + prr[1, here, :].astype(F32)
        stage[i] = (mid[here, :] + total).astype(BF16)

    own_chunks(layer_rows)
    scatter_next(0, 0)
    send_back(0, y_out)
    pair_sent(2, dyb)
    part_landed(2)

    def second_back(i, at, base):
        here = pl.ds(at, TILE)
        grad = contract(base, dgel, 1) + prr[0, here, :].astype(F32)
        normed, inverse = normalize(mid[here, :])
        gsum[1:2, :] += jnp.sum(grad * normed, axis=0, keepdims=True)
        down = dyb[pl.ds(base, TILE), :].astype(F32) + norm_back(
            grad, gain_second, normed, inverse
        )
        mid[here, :] = down
        dyb[pl.ds(base, TILE), :] = down.astype(BF16)

    own_chunks(second_back)
    pair_send(3, dyb)
    gather_sent(1)
    scatter_next(1, 0)
    grad_tiles(bnb, place[1], up_tile)
    scatter_step(2, 0)
    scatter_step(3, 0)

    def spread_mix(base):
        span = pl.ds(base, own_rows)
        result = dot(dyb[span, :], wq[:, 1152:1536])
        result = result.astype(BF16).astype(F32)
        turned = result.T
        pieces = []
        for h in range(6):
            at = HD * (h % 2)
            piece = (turned[HD * h : HD * h + HD] * shares[h, :, span]).astype(BF16)
            pieces.append(piece.astype(F32))
            qtz[h, at : at + HD, span] = piece
            product = piece.astype(F32) * ott[HD * h : HD * h + HD, span].astype(F32)
            delta[h, :, span] = jnp.sum(product, axis=0, keepdims=True)
        dorow[span, :] = jnp.concatenate(pieces, axis=0).T.astype(BF16)

    each_half(spread_mix, lambda: pair_landed(3, dyb))
    scatter_last(0)

    def attend_back(pair, carry):
        def tile(offset):
            return pl.ds(pl.multiple_of(offset + 128 * pair, 128), 128)

        parts = []
        for hh in range(2):
            h = 2 * pair + hh
            grad_values = dot(pt[h], dorow[:, tile(0)])
            for q in range(rows // own_rows):
                span = slice(q * own_rows, (q + 1) * own_rows)
                grad_prob = dot(qkv[:, tile(768)], qtz[h, :, span])
                chance = pt[h, :, span].astype(F32)
                pt[h, :, span] = (chance * (grad_prob - delta[h, :, span])).astype(BF16)
            grad_keys = dot(pt[h], qkv[:, tile(0)])
            head = pl.ds(pl.multiple_of(HD * h, HD), HD)
            grad_queries = dot(kt[head, :], pt[h]) * SCALE
            parts.append((grad_queries, grad_keys, grad_values))
        qkv[:, tile(768)] = jnp.where(low, parts[0][2], parts[1][2]).astype(BF16)
        qkv[:, tile(384)] = jnp.where(low, parts[0][1], parts[1][1]).astype(BF16)
        turned = jnp.concatenate([parts[0][0], parts[1][0]], axis=0).T
        qkv[:, tile(0)] = turned.astype(BF16)

        @pl.when(pair == 0)
        def _():
            scatter_last(1)

        @pl.when(pair == 1)
        def _():
            scatter_next(2, 0)

        @pl.when(pair == 2)
        def _():
            scatter_next(3, 0)

        return carry

    lax.fori_loop(0, 3, attend_back, 0)

    def first_contract(base, size):
        return dot_nt(qkv[pl.ds(base, size), :], wq[:, 0:1152])

    part_sent(1)
    prs[1] = first_contract(theirs, own_rows).astype(BF16)
    part_send(3)
    gather_sent(2)

    def first_tiles(t, carry):
        at = pl.multiple_of(t * TILE, TILE)
        span = pl.ds(at, TILE)
        slot = place[0]
        qkv_part = dot(ab[:, span].T, qkv[...])
        out_part = dot(dyb[:, span].T, orow[...])
        for i, target in ((0, 0), (1, 128), (2, 256)):
            for j in range(2):
                at = 384 * i + 128 * j
                wts[slot, j, span, target : target + 128] = qkv_part[:, at : at + 128].astype(BF16)
        for j in range(2):
            wts[slot, j, span, 640:768] = out_part[:, 128 * j : 128 * j + 128].astype(BF16)
        mixed_q = qkv_part[:, 256:384]
        mixed_k = qkv_part[:, 640:768]
        mixed_v = qkv_part[:, 1024:1152]
        mixed_o = out_part[:, 256:384]
        wts[slot, 0, span, 384:512] = jnp.where(low, mixed_q, roll(mixed_k)).astype(BF16)
        wts[slot, 1, span, 384:512] = jnp.where(low, roll(mixed_q), mixed_k).astype(BF16)
        wts[slot, 0, span, 512:640] = jnp.where(low, mixed_v, roll(mixed_o)).astype(BF16)
        wts[slot, 1, span, 512:640] = jnp.where(low, roll(mixed_v), mixed_o).astype(BF16)
        return carry

    lax.fori_loop(0, D // TILE, first_tiles, 0)
    scatter_step(4, 0)
    scatter_step(5, 0)

    back_sent(0)
    back_landed(0, y_out)
    scatter_relay(0)
    scatter_last(2)
    scatter_relay(1)
    part_landed(3)

    def first_back(i, at, base):
        here = pl.ds(at, TILE)
        grad = first_contract(base, TILE) + prr[1, here, :].astype(F32)
        normed, inverse = normalize(xb[i].astype(F32))
        gsum[0:1, :] += jnp.sum(grad * normed, axis=0, keepdims=True)
        result = mid[here, :] + norm_back(grad, gain_first, normed, inverse)
        stage[i] = result.astype(BF16)

    own_chunks(first_back)

    me = 2 * z + c
    for index, (cc, zz) in enumerate(column_peers):
        remote(
            gsum,
            sum_rx.at[me],
            sem["sum_s"].at[index],
            sem["sum_r"].at[me],
            device(p, cc, zz),
        ).start()
    pltpu.make_async_copy(gsum, sum_rx.at[me], sem["sum_r"].at[me]).start()
    scatter_last(3)
    send_back(1, dx_out)
    scatter_next(4, 0)
    scatter_relay(2)
    scatter_next(5, 0)
    scatter_relay(3)
    scatter_last(4)
    scatter_last(5)
    for source in range(2 * depth):
        wait_bytes(sum_rx.at[source], sem["sum_r"].at[source])
    for index in range(len(column_peers)):
        wait_bytes(gsum, sem["sum_s"].at[index])
    total = sum_rx[0]
    for source in range(1, 2 * depth):
        total = total + sum_rx[source]
    gsum[...] = total
    for index, pp in enumerate(plane_peers):
        remote(
            gsum, all_rx.at[p], sem["all_s"].at[index], sem["all_r"].at[p], device(pp, c, z)
        ).start()
    pltpu.make_async_copy(gsum, all_rx.at[p], sem["all_r"].at[p]).start()
    scatter_relay(4)
    scatter_relay(5)
    scatter_finish(0)
    scatter_finish(1)
    for source in range(columns):
        wait_bytes(all_rx.at[source], sem["all_r"].at[source])
    for index in range(len(plane_peers)):
        wait_bytes(gsum, sem["all_s"].at[index])
    total = all_rx[0]
    for source in range(1, columns):
        total = total + all_rx[source]
    place_of = (2 * D // (2 * columns * depth)) * (dp * depth + z)
    wanted = jnp.where(place_of < D, total[0:1, :], total[1:2, :])
    turn = (D - place_of % D) % D
    gm_out[...] = pltpu.roll(jnp.broadcast_to(wanted, (8, D)), turn, 1)[:, 0:128]
    for u in (2, 3, 4, 5):
        scatter_finish(u)

    back_landed(1, dx_out)
    back_sent(1)
    rows_sent(0, tok)
    rows_sent(1, cot)
    pair_sent(0, ab)
    pair_sent(1, bnb)
    pair_sent(3, dyb)
    part_sent(2)
    part_sent(3)
    for u in range(len(SCATTER)):
        scatter_sent(u)


def whole_layer(mesh, tok, cot, first, up, down, gains, padding, lengths):
    depth = mesh.shape["tensor"]
    bit_count = (mesh.shape["dp"] // 2).bit_length() - 1
    columns = 1 << bit_count
    shard = up.shape[0]
    half = depth // 2
    rows = padding.shape[1]
    own = rows // 2
    vmem = pl.BlockSpec(memory_space=pltpu.VMEM)
    hbm = pl.BlockSpec(memory_space=pl.ANY)
    sem = pltpu.SemaphoreType.DMA
    blocks = 1 << (bit_count - 1)
    scratch = [
        ((half, TILE, D), BF16),
        ((rows, D), BF16),
        ((rows, D), BF16),
        ((rows, D), BF16),
        ((KINDS, half, D, D), BF16),
        ((D, 2 * D), BF16),
        ((rows, 1152), BF16),
        ((6, 128, rows), BF16),
        ((384, rows), BF16),
        ((384, rows), BF16),
        ((6, rows, rows), BF16),
        ((rows, rows), F32),
        ((384, rows), BF16),
        ((rows, 384), BF16),
        ((rows, 384), BF16),
        ((own, D), F32),
        ((half, rows, D), BF16),
        ((half, rows, D), BF16),
        ((2, own, D), BF16),
        ((2, own, D), BF16),
        ((half, TILE, D), BF16),
        ((KINDS, 2, columns - 1, half, shard, D), BF16),
        ((KINDS, depth, shard, D), BF16),
        ((KINDS, 2, half, shard, D), BF16),
        ((2 * columns, 8, 128), F32),
        ((8, D), F32),
        ((2, 8, rows), F32),
        ((8, D), F32),
        ((2 * depth, 8, D), F32),
        ((columns, 8, D), F32),
        ((6, 1, rows), F32),
        ((6, 1, rows), F32),
    ]
    sems = {
        "tok_s": (2, 2),
        "tok_r": (2, half),
        "gain_s": (2 * columns,),
        "gain_r": (2 * columns,),
        "code_s": (),
        "code_r": (),
        "z_s": (len(GATHER), depth),
        "z_r": (len(GATHER), 2, half),
        "rel_s": (len(GATHER), 2, half),
        "x_s": (len(GATHER), 2, bit_count, blocks),
        "x_r": (len(GATHER), 2, bit_count, blocks),
        "rs_s": (len(SCATTER), 2, bit_count, blocks),
        "rs_r": (len(SCATTER), 2, bit_count, blocks),
        "rz_s": (len(SCATTER), 2, half),
        "rz_r": (len(SCATTER), depth),
        "far_r": (len(SCATTER), 2, half),
        "out_s": (2, half),
        "out_r": (2, 2),
        "pa_s": (4,),
        "pa_r": (4,),
        "pr_s": (4,),
        "pr_r": (4,),
        "sum_s": (2 * depth - 1,),
        "sum_r": (2 * depth,),
        "all_s": (columns - 1,),
        "all_r": (columns,),
    }
    return pl.pallas_call(
        functools.partial(layer_kernel, depth, bit_count, shard, rows),
        out_shape=(
            jax.ShapeDtypeStruct(tok.shape, BF16),
            jax.ShapeDtypeStruct(tok.shape, BF16),
            jax.ShapeDtypeStruct((KINDS,) + up.shape, F32),
            jax.ShapeDtypeStruct((8, 128), F32),
        ),
        in_specs=[hbm] * 5 + [vmem, vmem, pl.BlockSpec(memory_space=pltpu.SMEM)],
        out_specs=(hbm, hbm, vmem, vmem),
        scratch_shapes=[pltpu.VMEM(shape, dtype) for shape, dtype in scratch]
        + [sem(sems[name]) for name in SEMS],
        compiler_params=pltpu.CompilerParams(
            collective_id=0, has_side_effects=True, vmem_limit_bytes=67043328
        ),
        name="whole_layer",
    )(tok, cot, first, up, down, gains, padding, lengths)


def block_body(mesh, tokens, cotangent, lengths, padding, ln_gain, w_qkv, w_out, w_up, w_down):
    depth = mesh.shape["tensor"]
    shard = w_up.shape[1]
    pair = 2 * HD

    qkv = w_qkv[0]
    out_t = w_out[0].T
    packed = jnp.concatenate(
        [
            qkv[:, 0, :pair],
            qkv[:, 1, :pair],
            qkv[:, 2, :pair],
            qkv[:, 0, pair:],
            qkv[:, 1, pair:],
            qkv[:, 2, pair:],
            out_t[:, pair:],
            out_t[:, :pair],
        ],
        axis=1,
    )
    y_back, dx_back, summed, gain_sum = whole_layer(
        mesh,
        tokens,
        cotangent,
        packed,
        w_up[0],
        w_down[0].T,
        ln_gain[0],
        padding,
        lengths[:, 0],
    )
    gain_result = gain_sum[0, : 2 * D // (mesh.shape["dp"] * depth)]
    first = summed[0]
    qkv_grad = jnp.stack(
        [
            jnp.concatenate(
                [
                    first[:, pair * i : pair * i + pair],
                    first[:, 3 * pair + HD * i : 3 * pair + HD * i + HD],
                ],
                axis=1,
            )
            for i in range(3)
        ],
        axis=1,
    )[None]
    out_grad = jnp.concatenate([first[:, 5 * pair :], first[:, 4 * pair + HD : 5 * pair]], axis=1)
    return (
        y_back.astype(F32),
        dx_back.astype(F32),
        gain_result,
        qkv_grad,
        out_grad.T[None],
        summed[1][None],
        summed[2].T[None],
    )


def visible(lengths_row, padding_row):
    places = lax.iota(jnp.int32, padding_row.shape[0])
    bounds = jnp.cumsum(lengths_row)
    picture = jnp.sum((places[:, None] >= bounds[None, :]).astype(jnp.int32), axis=1)
    same_image = picture[:, None] == picture[None, :]
    return same_image & ((padding_row[None, :] == 1) | (places[:, None] == places[None, :]))


def gelu_exact(pre_values):
    return jax.nn.gelu(pre_values, approximate=False)


def masked_scores(queries, key_rows, allowed):
    scaling = queries.shape[-1] ** (-0.5)
    scores = (
        jnp.einsum("qhd,khd->hqk", queries, key_rows, preferred_element_type=jnp.float32) * scaling
    )
    return (jnp.where(allowed[None], scores, NEGATIVE), scaling)


def attend(stacked, allowed):
    scores, scaling = masked_scores(stacked[:, 0], stacked[:, 1], allowed)
    highest = jnp.max(scores, axis=-1, keepdims=True)
    exponent = jnp.exp(scores - highest)
    totals = jnp.sum(exponent, axis=-1, keepdims=True)
    rounded = (exponent / totals).astype(jnp.bfloat16)
    mixture = jnp.einsum("hqk,khd->qhd", rounded, stacked[:, 2], preferred_element_type=jnp.float32)
    return (mixture, highest, totals)


def attend_back(stacked, allowed, highest, totals, grad_mix):
    queries, key_rows, value_rows = (stacked[:, 0], stacked[:, 1], stacked[:, 2])
    scores, scaling = masked_scores(queries, key_rows, allowed)
    probability = jnp.exp(scores - highest) / totals
    rounded = probability.astype(jnp.bfloat16)
    grad_prob = jnp.einsum("qhd,khd->hqk", grad_mix, value_rows, preferred_element_type=jnp.float32)
    grad_values = jnp.einsum("hqk,qhd->khd", rounded, grad_mix, preferred_element_type=jnp.float32)
    inner_sum = jnp.sum(probability * grad_prob, axis=-1, keepdims=True)
    grad_scores = (probability * (grad_prob - inner_sum)).astype(jnp.bfloat16)
    grad_queries = (
        jnp.einsum("hqk,khd->qhd", grad_scores, key_rows, preferred_element_type=jnp.float32)
        * scaling
    )
    grad_keys = (
        jnp.einsum("hqk,qhd->khd", grad_scores, queries, preferred_element_type=jnp.float32)
        * scaling
    )
    return jnp.stack([grad_queries, grad_keys, grad_values], axis=1).astype(jnp.bfloat16)


def collect_weights(ln_gain, w_qkv, w_out, w_up, w_down, layer_index):
    return (
        lax.all_gather(ln_gain[layer_index], "dp", axis=1, tiled=True),
        lax.all_gather(w_qkv[layer_index], "dp", axis=0, tiled=True),
        lax.all_gather(w_out[layer_index], "dp", axis=1, tiled=True),
        lax.all_gather(w_up[layer_index], "dp", axis=0, tiled=True),
        lax.all_gather(w_down[layer_index], "dp", axis=1, tiled=True),
    )


def spread(block_rows):
    return lax.all_gather(block_rows, "tensor", axis=0, tiled=True)


def spread_grad(block_rows):
    return lax.all_gather(block_rows, "tensor", axis=0, tiled=True)


def collect_rows(operand, weight):
    return lax.psum_scatter(
        jnp.dot(operand, weight, preferred_element_type=jnp.float32),
        "tensor",
        scatter_dimension=0,
        tiled=True,
    )


def return_rows(operand, weight):
    return lax.psum_scatter(
        lax.dot_general(
            operand, weight, (((1,), (1,)), ((), ())), preferred_element_type=jnp.float32
        ),
        "tensor",
        scatter_dimension=0,
        tiled=True,
    )


def reduce_grads(pieces):
    return (
        lax.psum_scatter(pieces[0], "dp", scatter_dimension=0, tiled=True),
        lax.psum_scatter(pieces[1], "dp", scatter_dimension=1, tiled=True),
        lax.psum_scatter(pieces[2], "dp", scatter_dimension=0, tiled=True),
        lax.psum_scatter(pieces[3], "dp", scatter_dimension=1, tiled=True),
    )


def body(tokens, cotangent, lengths, padding, ln_gain, w_qkv, w_out, w_up, w_down):
    layer_count = w_qkv.shape[0]
    micro_count = tokens.shape[0]
    residual = [tokens[batch_index].astype(jnp.float32) for batch_index in range(micro_count)]
    visibility = [
        visible(lengths[batch_index, 0], padding[batch_index]) for batch_index in range(micro_count)
    ]
    saved = []
    stored_weights = []
    layer_index = 0
    stored_weights.append(None)
    for batch_index in range(micro_count):
        weights = collect_weights(ln_gain, w_qkv, w_out, w_up, w_down, layer_index)
        gain_pair, qkv_weight, out_weight, up_weight, down_weight = weights
        gain_first = gain_pair[0].astype(jnp.float32)
        gain_second = gain_pair[1].astype(jnp.float32)
        entering = residual[batch_index]
        normed, inverse = normalize(entering)
        first_input = spread((normed * gain_first).astype(jnp.bfloat16))
        triple = jnp.einsum(
            "rd,dcn->rcn", first_input, qkv_weight, preferred_element_type=jnp.float32
        ).astype(jnp.bfloat16)
        stacked = triple.reshape(triple.shape[0], 3, -1, HD)
        mixture, highest, totals = attend(stacked, visibility[batch_index])
        mix_rounded = mixture.reshape(mixture.shape[0], -1).astype(jnp.bfloat16)
        middle = entering + collect_rows(mix_rounded, out_weight)
        normed_two, inverse_two = normalize(middle)
        second_input = spread((normed_two * gain_second).astype(jnp.bfloat16))
        hidden_pre = jnp.dot(second_input, up_weight, preferred_element_type=jnp.float32)
        activated = gelu_exact(hidden_pre).astype(jnp.bfloat16)
        residual[batch_index] = middle + collect_rows(activated, down_weight)
        saved.append(
            (
                entering,
                first_input,
                stacked,
                highest,
                totals,
                mix_rounded,
                middle,
                second_input,
                hidden_pre,
                activated,
            )
        )
    gradients = [cotangent[batch_index].astype(jnp.float32) for batch_index in range(micro_count)]
    gain_parts = [jnp.zeros((2, D), jnp.float32)]
    weight_results = [None]
    for layer_index in reversed(range(layer_count)):
        summed = None
        for batch_index in range(micro_count):
            weights = collect_weights(ln_gain, w_qkv, w_out, w_up, w_down, layer_index)
            gain_pair, qkv_weight, out_weight, up_weight, down_weight = weights
            gain_first = gain_pair[0].astype(jnp.float32)
            gain_second = gain_pair[1].astype(jnp.float32)
            (
                entering,
                first_input,
                stacked,
                highest,
                totals,
                mix_rounded,
                middle,
                second_input,
                hidden_pre,
                activated,
            ) = saved[layer_index * micro_count + batch_index]
            incoming = gradients[batch_index]
            grad_down = spread_grad(incoming.astype(jnp.bfloat16))
            down_part = jnp.einsum(
                "rf,rd->fd", activated, grad_down, preferred_element_type=jnp.float32
            )
            grad_act = lax.dot_general(
                grad_down, down_weight, (((1,), (1,)), ((), ())), preferred_element_type=jnp.float32
            )
            pulled = jax.vjp(gelu_exact, hidden_pre)
            grad_pre = pulled[1](grad_act)[0].astype(jnp.bfloat16)
            up_part = jnp.einsum(
                "rd,rf->df", second_input, grad_pre, preferred_element_type=jnp.float32
            )
            grad_norm_two = return_rows(grad_pre, up_weight)
            normed_two, inverse_two = normalize(middle)
            gain_two_part = jnp.sum(grad_norm_two * normed_two, axis=0)
            incoming = incoming + norm_back(grad_norm_two, gain_second, normed_two, inverse_two)
            grad_branch = spread_grad(incoming.astype(jnp.bfloat16))
            out_part = jnp.einsum(
                "rk,rd->kd", mix_rounded, grad_branch, preferred_element_type=jnp.float32
            )
            grad_mix = lax.dot_general(
                grad_branch,
                out_weight,
                (((1,), (1,)), ((), ())),
                preferred_element_type=jnp.float32,
            )
            grad_mix = grad_mix.astype(jnp.bfloat16).reshape(grad_mix.shape[0], -1, HD)
            grad_triple = attend_back(stacked, visibility[batch_index], highest, totals, grad_mix)
            flat_triple = grad_triple.reshape(grad_triple.shape[0], 3, -1)
            qkv_part = jnp.einsum(
                "rd,rcn->dcn", first_input, flat_triple, preferred_element_type=jnp.float32
            )
            grad_norm_one = return_rows(
                flat_triple.reshape(flat_triple.shape[0], -1),
                qkv_weight.reshape(qkv_weight.shape[0], -1),
            )
            normed, inverse = normalize(entering)
            gain_one_part = jnp.sum(grad_norm_one * normed, axis=0)
            incoming = incoming + norm_back(grad_norm_one, gain_first, normed, inverse)
            gradients[batch_index] = incoming
            gain_parts[layer_index] = gain_parts[layer_index] + jnp.stack(
                [gain_one_part, gain_two_part]
            )
            pieces = (qkv_part, out_part, up_part, down_part)
            if summed is None:
                summed = pieces
            else:
                summed = tuple((older + newer for older, newer in zip(summed, pieces)))
        summed = reduce_grads(summed)
        weight_results[layer_index] = summed
    gain_flat = jnp.stack(gain_parts).reshape(-1)
    gain_result = lax.psum_scatter(gain_flat, ("dp", "tensor"), scatter_dimension=0, tiled=True)
    layer_out = jnp.stack(residual)
    input_grad = jnp.stack(gradients)
    qkv_grad = jnp.stack([weight_results[0][0]])
    out_grad = jnp.stack([weight_results[0][1]])
    up_grad = jnp.stack([weight_results[0][2]])
    down_grad = jnp.stack([weight_results[0][3]])
    return (layer_out, input_grad, gain_result, qkv_grad, out_grad, up_grad, down_grad)


def fits(mesh, tokens, w_qkv):
    dp_size, depth = mesh.shape["dp"], mesh.shape["tensor"]
    columns = dp_size // 2
    return (
        depth == 4
        and dp_size >= 4
        and columns & (columns - 1) == 0
        and D == dp_size * 2 * HALF
        and tokens.shape[0] == 2
        and tokens.shape[1] == dp_size * depth * TILE
        and w_qkv.shape[0] == 1
    )


def solution(mesh):
    def run(tokens, cotangent, lengths, padding, ln_gain, w_qkv, *rest):
        one_block = fits(mesh, tokens, w_qkv)
        program = functools.partial(block_body, mesh) if one_block else body
        return jax.shard_map(
            program,
            mesh=mesh,
            in_specs=(
                P(None, ("dp", "tensor"), None),
                P(None, ("dp", "tensor"), None),
                P(None, "dp", None),
                P(None, "dp"),
                P(None, None, "dp"),
                P(None, "dp", None, "tensor"),
                P(None, "tensor", "dp"),
                P(None, "dp", "tensor"),
                P(None, "tensor", "dp"),
            ),
            out_specs=(
                P(None, ("dp", "tensor"), None),
                P(None, ("dp", "tensor"), None),
                P(("dp", "tensor")),
                P(None, "dp", None, "tensor"),
                P(None, "tensor", "dp"),
                P(None, "dp", "tensor"),
                P(None, "tensor", "dp"),
            ),
            check_vma=False,
        )(tokens, cotangent, lengths, padding, ln_gain, w_qkv, *rest)

    return run
```

```python
import functools

import jax
import jax.numpy as jnp
from jax import lax
from jax.experimental import pallas as pl
from jax.experimental.pallas import tpu as pltpu
from jax.sharding import PartitionSpec as P

D = 768
HD = 64
NEGATIVE = -1e30
EPSILON = 1e-06
MESH = pl.DeviceIdType.MESH
F32 = jnp.float32
BF16 = jnp.bfloat16
KINDS = 3
HALF = 48
GATHER = (
    (0, 0, 16),
    (0, 16, 32),
    (0, HALF, HALF),
    (1, 0, HALF),
    (1, HALF, HALF),
    (2, 0, 2 * HALF),
)
SCATTER = (
    (2, 0, HALF),
    (2, HALF, HALF),
    (1, 0, HALF),
    (1, HALF, HALF),
    (0, 0, HALF),
    (0, HALF, HALF),
)
RELAYED = (2, 1, 0)
TILE = 256
SCALE = HD**-0.5


def flip(value, bit):
    size = 1 << bit
    return value + size * (1 - 2 * ((value // size) % 2))


def flip_mask(value, mask):
    bit = 0
    while mask >> bit:
        if (mask >> bit) & 1:
            value = flip(value, bit)
        bit += 1
    return value


def submasks(bits):
    masks = [0]
    for bit in bits:
        masks = masks + [mask | (1 << bit) for mask in masks]
    return masks


def color_order(color, bit_count):
    order = list(range(bit_count))
    return order if color == 0 else order[::-1]


def device(p, c, z):
    return (2 * p + c, z)


def dot(left, right):
    return jnp.dot(left, right, preferred_element_type=F32)


def dot_nt(left, right):
    return lax.dot_general(left, right, (((1,), (1,)), ((), ())), preferred_element_type=F32)


def normalize(row_block):
    average = jnp.mean(row_block, axis=-1, keepdims=True)
    centred = row_block - average
    variance = jnp.mean(centred * centred, axis=-1, keepdims=True)
    inverse = lax.rsqrt(variance + EPSILON)
    return (centred * inverse, inverse)


def norm_back(grad_out, gain_row, normed, inverse):
    scaled = grad_out * gain_row
    mean_grad = jnp.mean(scaled, axis=-1, keepdims=True)
    second = jnp.mean(scaled * normed, axis=-1, keepdims=True)
    return inverse * (scaled - mean_grad - normed * second)


def remote(source, target, send_sem, recv_sem, dest):
    return pltpu.make_async_remote_copy(
        source, target, send_sem, recv_sem, device_id=dest, device_id_type=MESH
    )


def wait_bytes(ref, sem):
    pltpu.make_async_copy(ref, ref, sem).wait()


SEMS = (
    "tok_s",
    "tok_r",
    "gain_s",
    "gain_r",
    "code_s",
    "code_r",
    "z_s",
    "z_r",
    "rel_s",
    "x_s",
    "x_r",
    "rs_s",
    "rs_r",
    "rz_s",
    "rz_r",
    "far_r",
    "out_s",
    "out_r",
    "pa_s",
    "pa_r",
    "pr_s",
    "pr_r",
    "sum_s",
    "sum_r",
    "all_s",
    "all_r",
)


def layer_kernel(depth, bit_count, shard, rows, *refs):
    (tok, cot, first_in, up_in, down_in, gain_in, pad_in, length_in) = refs[:8]
    (y_out, dx_out, g_out, gm_out) = refs[8:12]
    (
        xb,
        dyb,
        ab,
        bnb,
        wts,
        wq,
        qkv,
        qtz,
        vt,
        kt,
        pt,
        bias,
        ott,
        orow,
        dorow,
        mid,
        gact,
        dgel,
        prs,
        prr,
        stage,
        rx,
        zrx,
        far_rx,
        gbuf,
        gains,
        code,
        gsum,
        sum_rx,
        all_rx,
        delta,
        shares,
    ) = refs[12:44]
    sem = dict(zip(SEMS, refs[44:]))
    half = depth // 2
    columns = 1 << bit_count
    own_rows = rows // 2
    chunks = own_rows // TILE
    dp = lax.axis_index("dp")
    z = lax.axis_index("tensor")
    c = dp % 2
    p = dp // 2
    buddy = device(p, 1 - c, z)
    mine = pl.multiple_of(own_rows * c, own_rows)
    theirs = pl.multiple_of(own_rows * (1 - c), own_rows)
    lane = lax.broadcasted_iota(jnp.int32, (1, 128), 1)
    low = lane < HD

    def same(to_c, to_z):
        return jnp.logical_and(to_c == c, to_z == z)

    def send_or_copy(is_self, source, target, send_sem, recv_sem, dest):
        @pl.when(is_self)
        def _():
            pltpu.make_async_copy(source, target, recv_sem).start()

        @pl.when(jnp.logical_not(is_self))
        def _():
            remote(source, target, send_sem, recv_sem, dest).start()

    def wait_send(is_self, source, send_sem):
        @pl.when(jnp.logical_not(is_self))
        def _():
            wait_bytes(source, send_sem)

    column_peers = []
    for dz in range(depth):
        for dc in range(2):
            if dz or dc:
                column_peers.append((c if dc == 0 else 1 - c, (z + dz) % depth))
    plane_peers = [flip_mask(p, mask) for mask in range(1, columns)]

    def entry_barrier():
        barrier = pltpu.get_barrier_semaphore()
        peers = [device(p, cc, zz) for cc, zz in column_peers]
        peers += [device(pp, c, z) for pp in plane_peers]
        peers += [device(pp, 1 - c, z) for pp in plane_peers]
        for peer in peers:
            pl.semaphore_signal(barrier, inc=1, device_id=peer, device_id_type=MESH)
        pl.semaphore_wait(barrier, len(peers))

    def make_small():
        gbuf[dp] = jnp.zeros(gbuf.shape[1:], F32)
        gbuf[dp, 0:2, 0:shard] = gain_in[...].astype(F32)
        places = lax.broadcasted_iota(jnp.int32, (1, rows), 1)
        for m in range(2):
            image = jnp.zeros((1, rows), jnp.int32)
            bound = 0
            for k in range(length_in.shape[1]):
                bound = bound + length_in[m, k]
                image = image + (places >= bound).astype(jnp.int32)
            key = jnp.where(pad_in[m : m + 1, :] == 1, image, -1)
            code[c, m : m + 1, :] = image.astype(F32)
            code[c, 2 + m : 3 + m, :] = key.astype(F32)

    def send_small():
        remote(code.at[c], code.at[c], sem["code_s"], sem["code_r"], buddy).start()
        index = 0
        for pp in [p] + plane_peers:
            for cc in (c, 1 - c):
                if index:
                    remote(
                        gbuf.at[dp],
                        gbuf.at[dp],
                        sem["gain_s"].at[index],
                        sem["gain_r"].at[dp],
                        device(pp, cc, z),
                    ).start()
                index += 1

    def finish_small():
        wait_bytes(code.at[c], sem["code_s"])
        wait_bytes(code.at[1 - c], sem["code_r"])
        index = 0
        for pp in [p] + plane_peers:
            for cc in (c, 1 - c):
                if index:
                    wait_bytes(gbuf.at[dp], sem["gain_s"].at[index])
                    source = 2 * pp + cc
                    wait_bytes(gbuf.at[source], sem["gain_r"].at[source])
                index += 1
        rest = jnp.zeros((8, D - 128), F32)
        total = jnp.zeros((8, D), F32)
        for source in range(2 * columns):
            wide = jnp.concatenate([gbuf[source], rest], axis=1)
            total = total + (pltpu.roll(wide, shard * source, 1) if source else wide)
        gains[...] = total

    def row_targets():
        for m in range(2):
            to_z, to_c = 2 * m + c, z // half
            yield m, to_c, to_z, same(to_c, to_z)

    def row_target(which, slot):
        if which == 0:
            return xb.at[slot]
        return dyb.at[pl.ds(pl.multiple_of(own_rows * c + TILE * slot, TILE), TILE)]

    def row_landing(which, slot, to_c):
        if which == 0:
            return xb.at[slot]
        return dyb.at[pl.ds(pl.multiple_of(own_rows * to_c + TILE * slot, TILE), TILE)]

    def send_rows(which, array, to_ends=None):
        def send(m, to_c, to_z, is_self):
            slot = z % half
            send_or_copy(
                is_self,
                array.at[m],
                row_landing(which, slot, to_c),
                sem["tok_s"].at[which, m],
                sem["tok_r"].at[which, slot],
                device(p, to_c, to_z),
            )

        for m, to_c, to_z, is_self in row_targets():
            ship = functools.partial(send, m, to_c, to_z, is_self)
            if to_ends is None:
                ship()
            else:
                pl.when((c == m) if to_ends else (c != m))(ship)

    def rows_sent(which, array):
        for m, to_c, to_z, is_self in row_targets():
            wait_send(is_self, array.at[m], sem["tok_s"].at[which, m])

    def rows_landed(which):
        for slot in range(half):
            wait_bytes(row_target(which, slot), sem["tok_r"].at[which, slot])

    def send_back(which, target):
        for slot in range(half):
            to_c, to_z = z % 2, half * c + slot
            send_or_copy(
                same(to_c, to_z),
                stage.at[slot],
                target.at[z // 2],
                sem["out_s"].at[which, slot],
                sem["out_r"].at[which, z // 2],
                device(p, to_c, to_z),
            )

    def back_sent(which):
        for slot in range(half):
            is_self = same(z % 2, half * c + slot)
            wait_send(is_self, stage.at[slot], sem["out_s"].at[which, slot])

    def back_landed(which, target):
        for m in range(2):
            wait_bytes(target.at[m], sem["out_r"].at[which, m])

    last = depth - 1

    def two_ends(low_core, high_core):
        return jnp.logical_or(
            jnp.logical_and(c == 0, z == low_core), jnp.logical_and(c == 1, z == high_core)
        )

    ends = two_ends(last, 0)
    relays = two_ends(last - 1, 1)
    relay_to = device(p, c, last * (1 - c))
    relay_from = device(p, c, last - 1 + c * (2 - last))

    def unit_rows(unit, column, color):
        _, start, size = unit
        return pl.ds(pl.multiple_of((2 * column + color) * shard + start, 16), size)

    def unit_source(unit):
        return (first_in, up_in, down_in)[unit[0]].at[pl.ds(unit[1], unit[2])]

    def z_targets():
        for dz in range(depth):
            to_z = (z + dz) % depth
            yield dz, z // half, to_z, to_z == last * (1 - z // half)

    def gather_z(u):
        unit = GATHER[u]
        for dz, to_c, to_z, far in z_targets():
            source = unit_source(unit)
            target = wts.at[unit[0], z % half, unit_rows(unit, p, c)]
            recv = sem["z_r"].at[u, c, z % half]
            if dz == 0:
                send_or_copy(
                    to_c == c, source, target, sem["z_s"].at[u, dz], recv, device(p, to_c, to_z)
                )
            else:

                @pl.when(jnp.logical_not(far))
                def _():
                    remote(
                        source, target, sem["z_s"].at[u, dz], recv, device(p, to_c, to_z)
                    ).start()

    def gather_z_sent(u):
        for dz, to_c, to_z, far in z_targets():
            skip = to_c == c if dz == 0 else far
            wait_send(skip, unit_source(GATHER[u]), sem["z_s"].at[u, dz])

    def relay_block(u, color, slot):
        unit = GATHER[u]
        return wts.at[unit[0], slot, unit_rows(unit, p, color)]

    def gather_z_landed(u):
        unit = GATHER[u]
        for color in range(2):
            for slot in range(half):
                wait_bytes(
                    wts.at[unit[0], slot, unit_rows(unit, p, color)], sem["z_r"].at[u, color, slot]
                )

    def forward(u):
        @pl.when(relays)
        def _():
            gather_z_landed(u)
            for color in range(2):
                for slot in range(half):
                    block = relay_block(u, color, slot)
                    remote(
                        block,
                        block,
                        sem["rel_s"].at[u, color, slot],
                        sem["z_r"].at[u, color, slot],
                        relay_to,
                    ).start()

    def after_z(u):
        pl.when(jnp.logical_not(relays))(functools.partial(gather_z_landed, u))
        gather_step(u, 0)

    def gather_blocks(u, color, s, landed):
        unit = GATHER[u]
        order = color_order(color, bit_count)
        for index, mask in enumerate(submasks(order[:s])):
            column = flip_mask(p, mask)
            if landed:
                column = flip(column, order[s])
            yield index, wts.at[unit[0], :, unit_rows(unit, column, color)]

    def gather_step(u, s):
        for color in range(2):
            to = device(flip(p, color_order(color, bit_count)[s]), c, z)
            for index, block in gather_blocks(u, color, s, False):
                remote(
                    block,
                    block,
                    sem["x_s"].at[u, color, s, index],
                    sem["x_r"].at[u, color, s, index],
                    to,
                ).start()

    def gather_next(u, s):
        for color in range(2):
            for index, block in gather_blocks(u, color, s, True):
                wait_bytes(block, sem["x_r"].at[u, color, s, index])
        if s + 1 < bit_count:
            gather_step(u, s + 1)

    def gather_last(*units):
        for u in units:
            for s in range(1, bit_count):
                gather_next(u, s)

    def gather_sent(k):
        for u, unit in enumerate(GATHER):
            if unit[0] == k:
                gather_unit_sent(u)

    def gather_unit_sent(u):
        gather_z_sent(u)

        @pl.when(relays)
        def _():
            for color in range(2):
                for slot in range(half):
                    wait_bytes(relay_block(u, color, slot), sem["rel_s"].at[u, color, slot])

        for color in range(2):
            for s in range(bit_count):
                for index, block in gather_blocks(u, color, s, False):
                    wait_bytes(block, sem["x_s"].at[u, color, s, index])

    place = {2: 0, 1: 1, 0: 2}

    def rx_slot(u, color, s, index):
        unit = SCATTER[u]
        slot = (1 << bit_count) - (1 << (bit_count - s)) + index
        return rx.at[unit[0], color, slot, :, pl.ds(unit[1], unit[2])]

    def scatter_order(color):
        return color_order(color, bit_count)[::-1]

    def scatter_blocks(u, color, s, away):
        unit = SCATTER[u]
        order = scatter_order(color)
        for index, mask in enumerate(submasks(order[s + 1 :])):
            column = flip_mask(p, mask)
            if away:
                column = flip(column, order[s])
            yield index, wts.at[place[unit[0]], :, unit_rows(unit, column, color)]

    def scatter_step(u, s):
        for color in range(2):
            to = device(flip(p, scatter_order(color)[s]), c, z)
            for index, block in scatter_blocks(u, color, s, True):
                remote(
                    block,
                    rx_slot(u, color, s, index),
                    sem["rs_s"].at[u, color, s, index],
                    sem["rs_r"].at[u, color, s, index],
                    to,
                ).start()

    def scatter_next(u, s):
        for color in range(2):
            for index, block in scatter_blocks(u, color, s, False):
                got = rx_slot(u, color, s, index)
                wait_bytes(got, sem["rs_r"].at[u, color, s, index])
                block[...] = (block[...].astype(F32) + got[...].astype(F32)).astype(BF16)
        if s + 1 < bit_count:
            scatter_step(u, s + 1)
        else:
            scatter_z(u)

    def scatter_last(*units):
        for u in units:
            for s in range(1, bit_count):
                scatter_next(u, s)

    def scatter_z_blocks(u):
        unit = SCATTER[u]
        for color in range(2):
            for slot in range(half):
                to_z = half * c + slot
                block = wts.at[place[unit[0]], slot, unit_rows(unit, p, color)]
                yield color, slot, to_z, block

    def summed_on_the_way(u):
        return SCATTER[u][0] in RELAYED

    def landing(u, source):
        unit = SCATTER[u]
        return zrx.at[unit[0], source, pl.ds(unit[1], unit[2])]

    def far_landing(u, color, slot):
        unit = SCATTER[u]
        return far_rx.at[unit[0], color, slot, pl.ds(unit[1], unit[2])]

    def scatter_z(u):
        for color, slot, to_z, block in scatter_z_blocks(u):
            send, recv = sem["rz_s"].at[u, color, slot], sem["rz_r"].at[u, z]
            dest = device(p, color, to_z)
            if not summed_on_the_way(u):
                send_or_copy(same(color, to_z), block, landing(u, z), send, recv, dest)
                continue

            @pl.when(jnp.logical_not(jnp.logical_or(ends, relays)))
            def _():
                send_or_copy(same(color, to_z), block, landing(u, z), send, recv, dest)

            @pl.when(ends)
            def _():
                remote(
                    block,
                    far_landing(u, color, slot),
                    send,
                    sem["far_r"].at[u, color, slot],
                    relay_from,
                ).start()

    def scatter_relay(u):
        @pl.when(relays)
        def _():
            for color, slot, to_z, block in scatter_z_blocks(u):
                got = far_landing(u, color, slot)
                wait_bytes(got, sem["far_r"].at[u, color, slot])
                block[...] = (block[...].astype(F32) + got[...].astype(F32)).astype(BF16)
                send, recv = sem["rz_s"].at[u, color, slot], sem["rz_r"].at[u, z]
                dest = device(p, color, to_z)
                send_or_copy(same(color, to_z), block, landing(u, z), send, recv, dest)

    def scatter_finish(u):
        unit = SCATTER[u]
        for source in range(depth):
            got = functools.partial(wait_bytes, landing(u, source), sem["rz_r"].at[u, source])
            if summed_on_the_way(u) and source in (0, last):
                pl.when(z // half != (last - source) // half)(got)
            else:
                got()
        total = landing(u, 0)[...].astype(F32)
        for source in range(1, depth):
            total = total + landing(u, source)[...].astype(F32)
        g_out[unit[0], unit[1] : unit[1] + unit[2]] = total

    def scatter_sent(u):
        for color in range(2):
            for s in range(bit_count):
                for index, block in scatter_blocks(u, color, s, True):
                    wait_bytes(block, sem["rs_s"].at[u, color, s, index])
        for color, slot, to_z, block in scatter_z_blocks(u):
            local = same(color, to_z)
            if summed_on_the_way(u):
                local = jnp.logical_and(local, jnp.logical_not(ends))
            wait_send(local, block, sem["rz_s"].at[u, color, slot])

    def clear_far():
        for source in (0, last):

            @pl.when(z // half == (last - source) // half)
            def _():
                for k in RELAYED:
                    zrx[k, source] = jnp.zeros(zrx.shape[2:], BF16)

    def pair_send(index, buffer):
        own = buffer.at[pl.ds(mine, own_rows)]
        remote(own, own, sem["pa_s"].at[index], sem["pa_r"].at[index], buddy).start()

    def pair_landed(index, buffer):
        wait_bytes(buffer.at[pl.ds(theirs, own_rows)], sem["pa_r"].at[index])

    def pair_sent(index, buffer):
        wait_bytes(buffer.at[pl.ds(mine, own_rows)], sem["pa_s"].at[index])

    def part_send(index):
        remote(
            prs.at[index % 2],
            prr.at[index % 2],
            sem["pr_s"].at[index],
            sem["pr_r"].at[index],
            buddy,
        ).start()

    def part_landed(index):
        wait_bytes(prr.at[index % 2], sem["pr_r"].at[index])

    def part_sent(index):
        wait_bytes(prs.at[index % 2], sem["pr_s"].at[index])

    def each_half(body, second=None):
        def step(i, carry):
            if second is not None:
                pl.when(i == 1)(second)
            body(pl.multiple_of(jnp.where(i == 0, mine, theirs), own_rows))
            return carry

        lax.fori_loop(0, 2, step, 0)

    def own_chunks(body):
        def step(i, carry):
            body(i, pl.multiple_of(i * TILE, TILE), pl.multiple_of(mine + i * TILE, TILE))
            return carry

        lax.fori_loop(0, chunks, step, 0)

    make_small()
    entry_barrier()
    send_small()
    for u in range(5):
        gather_z(u)
    send_rows(0, tok)

    for h in range(6):
        qtz[h, HD * (1 - h % 2) : HD * (1 - h % 2) + HD, :] = jnp.zeros((HD, rows), BF16)
    gsum[...] = jnp.zeros(gsum.shape, F32)
    clear_far()
    forward(0)
    after_z(0)
    finish_small()
    gain_first = gains[0:1, :]
    gain_second = gains[1:2, :]
    forward(1)
    after_z(1)
    gather_next(0, 0)

    forward(2)
    after_z(2)
    gather_next(1, 0)
    forward(3)
    after_z(3)
    gather_next(2, 0)
    forward(4)
    after_z(4)
    gather_z(5)
    micro = z // 2
    owner = z % 2
    query_image = code[owner, pl.ds(micro, 1), :]
    key_code = code[owner, pl.ds(2 + micro, 1), :]
    key_columns = jnp.broadcast_to(key_code, (128, rows)).T
    for block in range(rows // 128):
        span = slice(128 * block, 128 * block + 128)
        key = key_columns[span, 0:1]
        row_id = lax.broadcasted_iota(jnp.int32, (128, rows), 0) + 128 * block
        col_id = lax.broadcasted_iota(jnp.int32, (128, rows), 1)
        seen = jnp.logical_or(key == query_image, row_id == col_id)
        bias[span, :] = jnp.where(seen, 0.0, NEGATIVE)

    gather_next(3, 0)
    rows_landed(0)

    def first_norm(i, at, base):
        normed, _ = normalize(xb[i].astype(F32))
        ab[pl.ds(base, TILE), :] = (normed * gain_first).astype(BF16)

    own_chunks(first_norm)
    pair_send(0, ab)
    gather_last(0, 1, 2)

    def roll(value):
        return pltpu.roll(value, HD, 1)

    for name, offset in (("q", 0), ("k", 384), ("v", 768), ("o", 1152)):
        tile = {"q": 0, "k": 128, "v": 256, "o": 640}[name]
        wq[:, offset : offset + 128] = wts[0, 0, :, tile : tile + 128]
        wq[:, offset + 128 : offset + 256] = wts[0, 1, :, tile : tile + 128]
        mixed = {"q": 384, "k": 384, "v": 512, "o": 512}[name]
        one = wts[0, 0, :, mixed : mixed + 128].astype(F32)
        two = wts[0, 1, :, mixed : mixed + 128].astype(F32)
        if name in ("q", "v"):
            both = jnp.where(low, one, roll(two))
        else:
            both = jnp.where(low, roll(one), two)
        wq[:, offset + 256 : offset + 384] = both.astype(BF16)

    def project(base):
        span = pl.ds(base, own_rows)
        source = ab[span, :]
        for part in range(3):
            result = dot(source, wq[:, 384 * part : 384 * part + 384])
            if part == 0:
                result = result * SCALE
            qkv[span, 384 * part : 384 * part + 384] = result.astype(BF16)
            turned = result.T.astype(BF16)
            if part == 0:
                for h in range(6):
                    at = HD * (h % 2)
                    qtz[h, at : at + HD, span] = turned[HD * h : HD * h + HD]
            elif part == 1:
                kt[:, span] = turned
            else:
                vt[:, span] = turned

    forward(5)
    each_half(project, lambda: pair_landed(0, ab))

    def attend(base, hook):
        span = pl.ds(base, own_rows)
        for h in range(6):
            pair = h // 2
            keys = qkv[:, 384 + 128 * pair : 512 + 128 * pair]
            scores = dot(keys, qtz[h, :, span]) + bias[:, span]
            highest = jnp.max(scores, axis=0, keepdims=True)
            exponent = jnp.exp(scores - highest)
            total = jnp.sum(exponent, axis=0, keepdims=True)
            rounded = exponent.astype(BF16)
            pt[h, :, span] = rounded
            share = 1.0 / total
            shares[h, :, span] = share
            mixed = dot(vt[HD * h : HD * h + HD, :], rounded) * share
            ott[HD * h : HD * h + HD, span] = mixed.astype(BF16)
            hook(h)
        orow[span, :] = ott[:, span].T

    def attend_loop(i, carry):
        base = pl.multiple_of(jnp.where(i == 0, theirs, mine), own_rows)

        def hook(h):
            if h == 0:

                @pl.when(i == 1)
                def _():
                    send_rows(1, cot, True)

            if h == 1:

                @pl.when(i == 0)
                def _():
                    gather_next(4, 0)
                    send_rows(1, cot, False)

            if h == 4:

                @pl.when(i == 0)
                def _():
                    after_z(5)

            if h == 5:

                @pl.when(i == 1)
                def _():
                    gather_next(5, 0)

        attend(base, hook)

        @pl.when(i == 0)
        def _():
            prs[0] = dot_nt(orow[pl.ds(base, own_rows), :], wq[:, 1152:1536]).astype(BF16)
            part_send(0)

        return carry

    lax.fori_loop(0, 2, attend_loop, 0)

    def own_out(i, at, base):
        mid[pl.ds(at, TILE), :] = dot_nt(orow[pl.ds(base, TILE), :], wq[:, 1152:1536])

    own_chunks(own_out)
    part_landed(0)

    def second_norm(i, at, base):
        here = pl.ds(at, TILE)
        middle = xb[i].astype(F32) + (mid[here, :] + prr[0, here, :].astype(F32))
        mid[here, :] = middle
        normed, _ = normalize(middle)
        bnb[pl.ds(base, TILE), :] = (normed * gain_second).astype(BF16)

    own_chunks(second_norm)
    pair_send(1, bnb)
    gather_last(3, 4)

    def expand(base):
        def chunk(i, carry):
            span = pl.ds(pl.multiple_of(base + i * TILE, TILE), TILE)
            source = bnb[span, :]
            for j in range(half):
                pre = dot(source, wts[1, j])
                cdf = 0.5 * (1.0 + lax.erf(pre * 0.7071067811865476))
                density = jnp.exp(pre * pre * -0.5) * 0.3989422804014327
                gact[j, span, :] = (pre * cdf).astype(BF16)
                dgel[j, span, :] = (cdf + pre * density).astype(BF16)
            return carry

        lax.fori_loop(0, chunks, chunk, 0)

    rows_landed(1)
    pair_send(2, dyb)
    each_half(expand, lambda: pair_landed(1, bnb))
    gather_sent(0)

    def grad_tiles(source, slot, width_of):
        def tile(t, carry):
            at = pl.multiple_of(t * TILE, TILE)
            turned = source[:, pl.ds(at, TILE)].T
            width_of(turned, slot, pl.ds(at, TILE))
            return carry

        lax.fori_loop(0, D // TILE, tile, 0)

    def down_tile(turned, slot, span):
        for j in range(half):
            wts[slot, j, span, :] = dot(turned, gact[j]).astype(BF16)

    def up_tile(turned, slot, span):
        for j in range(half):
            wts[slot, j, span, :] = dot(turned, dgel[j]).astype(BF16)

    pair_landed(2, dyb)
    grad_tiles(dyb, place[2], down_tile)
    scatter_step(0, 0)
    scatter_step(1, 0)
    gather_last(5)

    def contract(base, j_refs, weight):
        total = dot_nt(j_refs[0, pl.ds(base, TILE), :], wts[weight, 0])
        for j in range(1, half):
            total = total + dot_nt(j_refs[j, pl.ds(base, TILE), :], wts[weight, j])
        return total

    def their_chunks(buffer, weight, into):
        def step(i, carry):
            base = pl.multiple_of(theirs + i * TILE, TILE)
            into[pl.ds(pl.multiple_of(i * TILE, TILE), TILE), :] = contract(
                base, buffer, weight
            ).astype(BF16)
            return carry

        lax.fori_loop(0, chunks, step, 0)

    their_chunks(gact, 2, prs.at[1])
    part_send(1)

    def through_gelu(base):
        def chunk(i, carry):
            span = pl.ds(pl.multiple_of(base + i * TILE, TILE), TILE)
            source = dyb[span, :]
            for j in range(half):
                grad_act = dot(source, wts[2, j])
                dgel[j, span, :] = (grad_act * dgel[j, span, :].astype(F32)).astype(BF16)
            return carry

        lax.fori_loop(0, chunks, chunk, 0)

    each_half(through_gelu)
    part_sent(0)
    their_chunks(dgel, 1, prs.at[0])
    part_send(2)
    part_landed(1)

    def layer_rows(i, at, base):
        here = pl.ds(at, TILE)
        total = contract(base, gact, 2) + prr[1, here, :].astype(F32)
        stage[i] = (mid[here, :] + total).astype(BF16)

    own_chunks(layer_rows)
    scatter_next(0, 0)
    send_back(0, y_out)
    pair_sent(2, dyb)
    part_landed(2)

    def second_back(i, at, base):
        here = pl.ds(at, TILE)
        grad = contract(base, dgel, 1) + prr[0, here, :].astype(F32)
        normed, inverse = normalize(mid[here, :])
        gsum[1:2, :] += jnp.sum(grad * normed, axis=0, keepdims=True)
        down = dyb[pl.ds(base, TILE), :].astype(F32) + norm_back(
            grad, gain_second, normed, inverse
        )
        mid[here, :] = down
        dyb[pl.ds(base, TILE), :] = down.astype(BF16)

    own_chunks(second_back)
    pair_send(3, dyb)
    gather_sent(1)
    scatter_next(1, 0)
    grad_tiles(bnb, place[1], up_tile)
    scatter_step(2, 0)
    scatter_step(3, 0)

    def spread_mix(base):
        span = pl.ds(base, own_rows)
        result = dot(dyb[span, :], wq[:, 1152:1536])
        result = result.astype(BF16).astype(F32)
        turned = result.T
        pieces = []
        for h in range(6):
            at = HD * (h % 2)
            piece = (turned[HD * h : HD * h + HD] * shares[h, :, span]).astype(BF16)
            pieces.append(piece.astype(F32))
            qtz[h, at : at + HD, span] = piece
            product = piece.astype(F32) * ott[HD * h : HD * h + HD, span].astype(F32)
            delta[h, :, span] = jnp.sum(product, axis=0, keepdims=True)
        dorow[span, :] = jnp.concatenate(pieces, axis=0).T.astype(BF16)

    each_half(spread_mix, lambda: pair_landed(3, dyb))
    scatter_last(0)

    def attend_back(pair, carry):
        def tile(offset):
            return pl.ds(pl.multiple_of(offset + 128 * pair, 128), 128)

        parts = []
        for hh in range(2):
            h = 2 * pair + hh
            grad_values = dot(pt[h], dorow[:, tile(0)])
            for q in range(rows // own_rows):
                span = slice(q * own_rows, (q + 1) * own_rows)
                grad_prob = dot(qkv[:, tile(768)], qtz[h, :, span])
                chance = pt[h, :, span].astype(F32)
                pt[h, :, span] = (chance * (grad_prob - delta[h, :, span])).astype(BF16)
            grad_keys = dot(pt[h], qkv[:, tile(0)])
            head = pl.ds(pl.multiple_of(HD * h, HD), HD)
            grad_queries = dot(kt[head, :], pt[h]) * SCALE
            parts.append((grad_queries, grad_keys, grad_values))
        qkv[:, tile(768)] = jnp.where(low, parts[0][2], parts[1][2]).astype(BF16)
        qkv[:, tile(384)] = jnp.where(low, parts[0][1], parts[1][1]).astype(BF16)
        turned = jnp.concatenate([parts[0][0], parts[1][0]], axis=0).T
        qkv[:, tile(0)] = turned.astype(BF16)

        @pl.when(pair == 0)
        def _():
            scatter_last(1)

        @pl.when(pair == 1)
        def _():
            scatter_next(2, 0)

        @pl.when(pair == 2)
        def _():
            scatter_next(3, 0)

        return carry

    lax.fori_loop(0, 3, attend_back, 0)

    def first_contract(base, size):
        return dot_nt(qkv[pl.ds(base, size), :], wq[:, 0:1152])

    part_sent(1)
    prs[1] = first_contract(theirs, own_rows).astype(BF16)
    part_send(3)
    gather_sent(2)

    def first_tiles(t, carry):
        at = pl.multiple_of(t * TILE, TILE)
        span = pl.ds(at, TILE)
        slot = place[0]
        qkv_part = dot(ab[:, span].T, qkv[...])
        out_part = dot(dyb[:, span].T, orow[...])
        for i, target in ((0, 0), (1, 128), (2, 256)):
            for j in range(2):
                at = 384 * i + 128 * j
                wts[slot, j, span, target : target + 128] = qkv_part[:, at : at + 128].astype(BF16)
        for j in range(2):
            wts[slot, j, span, 640:768] = out_part[:, 128 * j : 128 * j + 128].astype(BF16)
        mixed_q = qkv_part[:, 256:384]
        mixed_k = qkv_part[:, 640:768]
        mixed_v = qkv_part[:, 1024:1152]
        mixed_o = out_part[:, 256:384]
        wts[slot, 0, span, 384:512] = jnp.where(low, mixed_q, roll(mixed_k)).astype(BF16)
        wts[slot, 1, span, 384:512] = jnp.where(low, roll(mixed_q), mixed_k).astype(BF16)
        wts[slot, 0, span, 512:640] = jnp.where(low, mixed_v, roll(mixed_o)).astype(BF16)
        wts[slot, 1, span, 512:640] = jnp.where(low, roll(mixed_v), mixed_o).astype(BF16)
        return carry

    lax.fori_loop(0, D // TILE, first_tiles, 0)
    scatter_step(4, 0)
    scatter_step(5, 0)

    back_sent(0)
    back_landed(0, y_out)
    scatter_relay(0)
    scatter_last(2)
    scatter_relay(1)
    part_landed(3)

    def first_back(i, at, base):
        here = pl.ds(at, TILE)
        grad = first_contract(base, TILE) + prr[1, here, :].astype(F32)
        normed, inverse = normalize(xb[i].astype(F32))
        gsum[0:1, :] += jnp.sum(grad * normed, axis=0, keepdims=True)
        result = mid[here, :] + norm_back(grad, gain_first, normed, inverse)
        stage[i] = result.astype(BF16)

    own_chunks(first_back)

    me = 2 * z + c
    for index, (cc, zz) in enumerate(column_peers):
        remote(
            gsum,
            sum_rx.at[me],
            sem["sum_s"].at[index],
            sem["sum_r"].at[me],
            device(p, cc, zz),
        ).start()
    pltpu.make_async_copy(gsum, sum_rx.at[me], sem["sum_r"].at[me]).start()
    scatter_last(3)
    send_back(1, dx_out)
    scatter_next(4, 0)
    scatter_relay(2)
    scatter_next(5, 0)
    scatter_relay(3)
    scatter_last(4)
    scatter_last(5)
    for source in range(2 * depth):
        wait_bytes(sum_rx.at[source], sem["sum_r"].at[source])
    for index in range(len(column_peers)):
        wait_bytes(gsum, sem["sum_s"].at[index])
    total = sum_rx[0]
    for source in range(1, 2 * depth):
        total = total + sum_rx[source]
    gsum[...] = total
    for index, pp in enumerate(plane_peers):
        remote(
            gsum, all_rx.at[p], sem["all_s"].at[index], sem["all_r"].at[p], device(pp, c, z)
        ).start()
    pltpu.make_async_copy(gsum, all_rx.at[p], sem["all_r"].at[p]).start()
    scatter_relay(4)
    scatter_relay(5)
    scatter_finish(0)
    scatter_finish(1)
    for source in range(columns):
        wait_bytes(all_rx.at[source], sem["all_r"].at[source])
    for index in range(len(plane_peers)):
        wait_bytes(gsum, sem["all_s"].at[index])
    total = all_rx[0]
    for source in range(1, columns):
        total = total + all_rx[source]
    place_of = (2 * D // (2 * columns * depth)) * (dp * depth + z)
    wanted = jnp.where(place_of < D, total[0:1, :], total[1:2, :])
    turn = (D - place_of % D) % D
    gm_out[...] = pltpu.roll(jnp.broadcast_to(wanted, (8, D)), turn, 1)[:, 0:128]
    for u in (2, 3, 4, 5):
        scatter_finish(u)

    back_landed(1, dx_out)
    back_sent(1)
    rows_sent(0, tok)
    rows_sent(1, cot)
    pair_sent(0, ab)
    pair_sent(1, bnb)
    pair_sent(3, dyb)
    part_sent(2)
    part_sent(3)
    for u in range(len(SCATTER)):
        scatter_sent(u)


def whole_layer(mesh, tok, cot, first, up, down, gains, padding, lengths):
    depth = mesh.shape["tensor"]
    bit_count = (mesh.shape["dp"] // 2).bit_length() - 1
    columns = 1 << bit_count
    shard = up.shape[0]
    half = depth // 2
    rows = padding.shape[1]
    own = rows // 2
    vmem = pl.BlockSpec(memory_space=pltpu.VMEM)
    hbm = pl.BlockSpec(memory_space=pl.ANY)
    sem = pltpu.SemaphoreType.DMA
    blocks = 1 << (bit_count - 1)
    scratch = [
        ((half, TILE, D), BF16),
        ((rows, D), BF16),
        ((rows, D), BF16),
        ((rows, D), BF16),
        ((KINDS, half, D, D), BF16),
        ((D, 2 * D), BF16),
        ((rows, 1152), BF16),
        ((6, 128, rows), BF16),
        ((384, rows), BF16),
        ((384, rows), BF16),
        ((6, rows, rows), BF16),
        ((rows, rows), F32),
        ((384, rows), BF16),
        ((rows, 384), BF16),
        ((rows, 384), BF16),
        ((own, D), F32),
        ((half, rows, D), BF16),
        ((half, rows, D), BF16),
        ((2, own, D), BF16),
        ((2, own, D), BF16),
        ((half, TILE, D), BF16),
        ((KINDS, 2, columns - 1, half, shard, D), BF16),
        ((KINDS, depth, shard, D), BF16),
        ((KINDS, 2, half, shard, D), BF16),
        ((2 * columns, 8, 128), F32),
        ((8, D), F32),
        ((2, 8, rows), F32),
        ((8, D), F32),
        ((2 * depth, 8, D), F32),
        ((columns, 8, D), F32),
        ((6, 1, rows), F32),
        ((6, 1, rows), F32),
    ]
    sems = {
        "tok_s": (2, 2),
        "tok_r": (2, half),
        "gain_s": (2 * columns,),
        "gain_r": (2 * columns,),
        "code_s": (),
        "code_r": (),
        "z_s": (len(GATHER), depth),
        "z_r": (len(GATHER), 2, half),
        "rel_s": (len(GATHER), 2, half),
        "x_s": (len(GATHER), 2, bit_count, blocks),
        "x_r": (len(GATHER), 2, bit_count, blocks),
        "rs_s": (len(SCATTER), 2, bit_count, blocks),
        "rs_r": (len(SCATTER), 2, bit_count, blocks),
        "rz_s": (len(SCATTER), 2, half),
        "rz_r": (len(SCATTER), depth),
        "far_r": (len(SCATTER), 2, half),
        "out_s": (2, half),
        "out_r": (2, 2),
        "pa_s": (4,),
        "pa_r": (4,),
        "pr_s": (4,),
        "pr_r": (4,),
        "sum_s": (2 * depth - 1,),
        "sum_r": (2 * depth,),
        "all_s": (columns - 1,),
        "all_r": (columns,),
    }
    return pl.pallas_call(
        functools.partial(layer_kernel, depth, bit_count, shard, rows),
        out_shape=(
            jax.ShapeDtypeStruct(tok.shape, BF16),
            jax.ShapeDtypeStruct(tok.shape, BF16),
            jax.ShapeDtypeStruct((KINDS,) + up.shape, F32),
            jax.ShapeDtypeStruct((8, 128), F32),
        ),
        in_specs=[hbm] * 5 + [vmem, vmem, pl.BlockSpec(memory_space=pltpu.SMEM)],
        out_specs=(hbm, hbm, vmem, vmem),
        scratch_shapes=[pltpu.VMEM(shape, dtype) for shape, dtype in scratch]
        + [sem(sems[name]) for name in SEMS],
        compiler_params=pltpu.CompilerParams(
            collective_id=0, has_side_effects=True, vmem_limit_bytes=67043328
        ),
        name="whole_layer",
    )(tok, cot, first, up, down, gains, padding, lengths)


def block_body(mesh, tokens, cotangent, lengths, padding, ln_gain, w_qkv, w_out, w_up, w_down):
    depth = mesh.shape["tensor"]
    shard = w_up.shape[1]
    pair = 2 * HD

    qkv = w_qkv[0]
    out_t = w_out[0].T
    packed = jnp.concatenate(
        [
            qkv[:, 0, :pair],
            qkv[:, 1, :pair],
            qkv[:, 2, :pair],
            qkv[:, 0, pair:],
            qkv[:, 1, pair:],
            qkv[:, 2, pair:],
            out_t[:, pair:],
            out_t[:, :pair],
        ],
        axis=1,
    )
    y_back, dx_back, summed, gain_sum = whole_layer(
        mesh,
        tokens,
        cotangent,
        packed,
        w_up[0],
        w_down[0].T,
        ln_gain[0],
        padding,
        lengths[:, 0],
    )
    gain_result = gain_sum[0, : 2 * D // (mesh.shape["dp"] * depth)]
    first = summed[0]
    qkv_grad = jnp.stack(
        [
            jnp.concatenate(
                [
                    first[:, pair * i : pair * i + pair],
                    first[:, 3 * pair + HD * i : 3 * pair + HD * i + HD],
                ],
                axis=1,
            )
            for i in range(3)
        ],
        axis=1,
    )[None]
    out_grad = jnp.concatenate([first[:, 5 * pair :], first[:, 4 * pair + HD : 5 * pair]], axis=1)
    return (
        y_back.astype(F32),
        dx_back.astype(F32),
        gain_result,
        qkv_grad,
        out_grad.T[None],
        summed[1][None],
        summed[2].T[None],
    )


def visible(lengths_row, padding_row):
    places = lax.iota(jnp.int32, padding_row.shape[0])
    bounds = jnp.cumsum(lengths_row)
    picture = jnp.sum((places[:, None] >= bounds[None, :]).astype(jnp.int32), axis=1)
    same_image = picture[:, None] == picture[None, :]
    return same_image & ((padding_row[None, :] == 1) | (places[:, None] == places[None, :]))


def gelu_exact(pre_values):
    return jax.nn.gelu(pre_values, approximate=False)


def masked_scores(queries, key_rows, allowed):
    scaling = queries.shape[-1] ** (-0.5)
    scores = (
        jnp.einsum("qhd,khd->hqk", queries, key_rows, preferred_element_type=jnp.float32) * scaling
    )
    return (jnp.where(allowed[None], scores, NEGATIVE), scaling)


def attend(stacked, allowed):
    scores, scaling = masked_scores(stacked[:, 0], stacked[:, 1], allowed)
    highest = jnp.max(scores, axis=-1, keepdims=True)
    exponent = jnp.exp(scores - highest)
    totals = jnp.sum(exponent, axis=-1, keepdims=True)
    rounded = (exponent / totals).astype(jnp.bfloat16)
    mixture = jnp.einsum("hqk,khd->qhd", rounded, stacked[:, 2], preferred_element_type=jnp.float32)
    return (mixture, highest, totals)


def attend_back(stacked, allowed, highest, totals, grad_mix):
    queries, key_rows, value_rows = (stacked[:, 0], stacked[:, 1], stacked[:, 2])
    scores, scaling = masked_scores(queries, key_rows, allowed)
    probability = jnp.exp(scores - highest) / totals
    rounded = probability.astype(jnp.bfloat16)
    grad_prob = jnp.einsum("qhd,khd->hqk", grad_mix, value_rows, preferred_element_type=jnp.float32)
    grad_values = jnp.einsum("hqk,qhd->khd", rounded, grad_mix, preferred_element_type=jnp.float32)
    inner_sum = jnp.sum(probability * grad_prob, axis=-1, keepdims=True)
    grad_scores = (probability * (grad_prob - inner_sum)).astype(jnp.bfloat16)
    grad_queries = (
        jnp.einsum("hqk,khd->qhd", grad_scores, key_rows, preferred_element_type=jnp.float32)
        * scaling
    )
    grad_keys = (
        jnp.einsum("hqk,qhd->khd", grad_scores, queries, preferred_element_type=jnp.float32)
        * scaling
    )
    return jnp.stack([grad_queries, grad_keys, grad_values], axis=1).astype(jnp.bfloat16)


def collect_weights(ln_gain, w_qkv, w_out, w_up, w_down, layer_index):
    return (
        lax.all_gather(ln_gain[layer_index], "dp", axis=1, tiled=True),
        lax.all_gather(w_qkv[layer_index], "dp", axis=0, tiled=True),
        lax.all_gather(w_out[layer_index], "dp", axis=1, tiled=True),
        lax.all_gather(w_up[layer_index], "dp", axis=0, tiled=True),
        lax.all_gather(w_down[layer_index], "dp", axis=1, tiled=True),
    )


def spread(block_rows):
    return lax.all_gather(block_rows, "tensor", axis=0, tiled=True)


def spread_grad(block_rows):
    return lax.all_gather(block_rows, "tensor", axis=0, tiled=True)


def collect_rows(operand, weight):
    return lax.psum_scatter(
        jnp.dot(operand, weight, preferred_element_type=jnp.float32),
        "tensor",
        scatter_dimension=0,
        tiled=True,
    )


def return_rows(operand, weight):
    return lax.psum_scatter(
        lax.dot_general(
            operand, weight, (((1,), (1,)), ((), ())), preferred_element_type=jnp.float32
        ),
        "tensor",
        scatter_dimension=0,
        tiled=True,
    )


def reduce_grads(pieces):
    return (
        lax.psum_scatter(pieces[0], "dp", scatter_dimension=0, tiled=True),
        lax.psum_scatter(pieces[1], "dp", scatter_dimension=1, tiled=True),
        lax.psum_scatter(pieces[2], "dp", scatter_dimension=0, tiled=True),
        lax.psum_scatter(pieces[3], "dp", scatter_dimension=1, tiled=True),
    )


def body(tokens, cotangent, lengths, padding, ln_gain, w_qkv, w_out, w_up, w_down):
    layer_count = w_qkv.shape[0]
    micro_count = tokens.shape[0]
    residual = [tokens[batch_index].astype(jnp.float32) for batch_index in range(micro_count)]
    visibility = [
        visible(lengths[batch_index, 0], padding[batch_index]) for batch_index in range(micro_count)
    ]
    saved = []
    stored_weights = []
    layer_index = 0
    stored_weights.append(None)
    for batch_index in range(micro_count):
        weights = collect_weights(ln_gain, w_qkv, w_out, w_up, w_down, layer_index)
        gain_pair, qkv_weight, out_weight, up_weight, down_weight = weights
        gain_first = gain_pair[0].astype(jnp.float32)
        gain_second = gain_pair[1].astype(jnp.float32)
        entering = residual[batch_index]
        normed, inverse = normalize(entering)
        first_input = spread((normed * gain_first).astype(jnp.bfloat16))
        triple = jnp.einsum(
            "rd,dcn->rcn", first_input, qkv_weight, preferred_element_type=jnp.float32
        ).astype(jnp.bfloat16)
        stacked = triple.reshape(triple.shape[0], 3, -1, HD)
        mixture, highest, totals = attend(stacked, visibility[batch_index])
        mix_rounded = mixture.reshape(mixture.shape[0], -1).astype(jnp.bfloat16)
        middle = entering + collect_rows(mix_rounded, out_weight)
        normed_two, inverse_two = normalize(middle)
        second_input = spread((normed_two * gain_second).astype(jnp.bfloat16))
        hidden_pre = jnp.dot(second_input, up_weight, preferred_element_type=jnp.float32)
        activated = gelu_exact(hidden_pre).astype(jnp.bfloat16)
        residual[batch_index] = middle + collect_rows(activated, down_weight)
        saved.append(
            (
                entering,
                first_input,
                stacked,
                highest,
                totals,
                mix_rounded,
                middle,
                second_input,
                hidden_pre,
                activated,
            )
        )
    gradients = [cotangent[batch_index].astype(jnp.float32) for batch_index in range(micro_count)]
    gain_parts = [jnp.zeros((2, D), jnp.float32)]
    weight_results = [None]
    for layer_index in reversed(range(layer_count)):
        summed = None
        for batch_index in range(micro_count):
            weights = collect_weights(ln_gain, w_qkv, w_out, w_up, w_down, layer_index)
            gain_pair, qkv_weight, out_weight, up_weight, down_weight = weights
            gain_first = gain_pair[0].astype(jnp.float32)
            gain_second = gain_pair[1].astype(jnp.float32)
            (
                entering,
                first_input,
                stacked,
                highest,
                totals,
                mix_rounded,
                middle,
                second_input,
                hidden_pre,
                activated,
            ) = saved[layer_index * micro_count + batch_index]
            incoming = gradients[batch_index]
            grad_down = spread_grad(incoming.astype(jnp.bfloat16))
            down_part = jnp.einsum(
                "rf,rd->fd", activated, grad_down, preferred_element_type=jnp.float32
            )
            grad_act = lax.dot_general(
                grad_down, down_weight, (((1,), (1,)), ((), ())), preferred_element_type=jnp.float32
            )
            pulled = jax.vjp(gelu_exact, hidden_pre)
            grad_pre = pulled[1](grad_act)[0].astype(jnp.bfloat16)
            up_part = jnp.einsum(
                "rd,rf->df", second_input, grad_pre, preferred_element_type=jnp.float32
            )
            grad_norm_two = return_rows(grad_pre, up_weight)
            normed_two, inverse_two = normalize(middle)
            gain_two_part = jnp.sum(grad_norm_two * normed_two, axis=0)
            incoming = incoming + norm_back(grad_norm_two, gain_second, normed_two, inverse_two)
            grad_branch = spread_grad(incoming.astype(jnp.bfloat16))
            out_part = jnp.einsum(
                "rk,rd->kd", mix_rounded, grad_branch, preferred_element_type=jnp.float32
            )
            grad_mix = lax.dot_general(
                grad_branch,
                out_weight,
                (((1,), (1,)), ((), ())),
                preferred_element_type=jnp.float32,
            )
            grad_mix = grad_mix.astype(jnp.bfloat16).reshape(grad_mix.shape[0], -1, HD)
            grad_triple = attend_back(stacked, visibility[batch_index], highest, totals, grad_mix)
            flat_triple = grad_triple.reshape(grad_triple.shape[0], 3, -1)
            qkv_part = jnp.einsum(
                "rd,rcn->dcn", first_input, flat_triple, preferred_element_type=jnp.float32
            )
            grad_norm_one = return_rows(
                flat_triple.reshape(flat_triple.shape[0], -1),
                qkv_weight.reshape(qkv_weight.shape[0], -1),
            )
            normed, inverse = normalize(entering)
            gain_one_part = jnp.sum(grad_norm_one * normed, axis=0)
            incoming = incoming + norm_back(grad_norm_one, gain_first, normed, inverse)
            gradients[batch_index] = incoming
            gain_parts[layer_index] = gain_parts[layer_index] + jnp.stack(
                [gain_one_part, gain_two_part]
            )
            pieces = (qkv_part, out_part, up_part, down_part)
            if summed is None:
                summed = pieces
            else:
                summed = tuple((older + newer for older, newer in zip(summed, pieces)))
        summed = reduce_grads(summed)
        weight_results[layer_index] = summed
    gain_flat = jnp.stack(gain_parts).reshape(-1)
    gain_result = lax.psum_scatter(gain_flat, ("dp", "tensor"), scatter_dimension=0, tiled=True)
    layer_out = jnp.stack(residual)
    input_grad = jnp.stack(gradients)
    qkv_grad = jnp.stack([weight_results[0][0]])
    out_grad = jnp.stack([weight_results[0][1]])
    up_grad = jnp.stack([weight_results[0][2]])
    down_grad = jnp.stack([weight_results[0][3]])
    return (layer_out, input_grad, gain_result, qkv_grad, out_grad, up_grad, down_grad)


def fits(mesh, tokens, w_qkv):
    dp_size, depth = mesh.shape["dp"], mesh.shape["tensor"]
    columns = dp_size // 2
    return (
        depth == 4
        and dp_size >= 4
        and columns & (columns - 1) == 0
        and D == dp_size * 2 * HALF
        and tokens.shape[0] == 2
        and tokens.shape[1] == dp_size * depth * TILE
        and w_qkv.shape[0] == 1
    )


def solution(mesh):
    def run(tokens, cotangent, lengths, padding, ln_gain, w_qkv, *rest):
        one_block = fits(mesh, tokens, w_qkv)
        program = functools.partial(block_body, mesh) if one_block else body
        return jax.shard_map(
            program,
            mesh=mesh,
            in_specs=(
                P(None, ("dp", "tensor"), None),
                P(None, ("dp", "tensor"), None),
                P(None, "dp", None),
                P(None, "dp"),
                P(None, None, "dp"),
                P(None, "dp", None, "tensor"),
                P(None, "tensor", "dp"),
                P(None, "dp", "tensor"),
                P(None, "tensor", "dp"),
            ),
            out_specs=(
                P(None, ("dp", "tensor"), None),
                P(None, ("dp", "tensor"), None),
                P(("dp", "tensor")),
                P(None, "dp", None, "tensor"),
                P(None, "tensor", "dp"),
                P(None, "dp", "tensor"),
                P(None, "tensor", "dp"),
            ),
            check_vma=False,
        )(tokens, cotangent, lengths, padding, ln_gain, w_qkv, *rest)

    return run
```

```python
import functools

import jax
import jax.numpy as jnp
from jax import lax
from jax.experimental import pallas as pl
from jax.experimental.pallas import tpu as pltpu
from jax.sharding import PartitionSpec as P

D = 768
HD = 64
NEGATIVE = -1e30
EPSILON = 1e-06
MESH = pl.DeviceIdType.MESH
F32 = jnp.float32
BF16 = jnp.bfloat16
KINDS = 3
HALF = 48
GATHER = (
    (0, 0, 16),
    (0, 16, 32),
    (0, HALF, HALF),
    (1, 0, HALF),
    (1, HALF, HALF),
    (2, 0, 2 * HALF),
)
SCATTER = (
    (2, 0, HALF),
    (2, HALF, HALF),
    (1, 0, HALF),
    (1, HALF, HALF),
    (0, 0, HALF),
    (0, HALF, HALF),
)
RELAYED = (2, 1, 0)
TILE = 256
SCALE = HD**-0.5


def flip(value, bit):
    size = 1 << bit
    return value + size * (1 - 2 * ((value // size) % 2))


def flip_mask(value, mask):
    bit = 0
    while mask >> bit:
        if (mask >> bit) & 1:
            value = flip(value, bit)
        bit += 1
    return value


def submasks(bits):
    masks = [0]
    for bit in bits:
        masks = masks + [mask | (1 << bit) for mask in masks]
    return masks


def color_order(color, bit_count):
    order = list(range(bit_count))
    return order if color == 0 else order[::-1]


def device(p, c, z):
    return (2 * p + c, z)


def dot(left, right):
    return jnp.dot(left, right, preferred_element_type=F32)


def dot_nt(left, right):
    return lax.dot_general(left, right, (((1,), (1,)), ((), ())), preferred_element_type=F32)


def normalize(row_block):
    average = jnp.mean(row_block, axis=-1, keepdims=True)
    centred = row_block - average
    variance = jnp.mean(centred * centred, axis=-1, keepdims=True)
    inverse = lax.rsqrt(variance + EPSILON)
    return (centred * inverse, inverse)


def norm_back(grad_out, gain_row, normed, inverse):
    scaled = grad_out * gain_row
    mean_grad = jnp.mean(scaled, axis=-1, keepdims=True)
    second = jnp.mean(scaled * normed, axis=-1, keepdims=True)
    return inverse * (scaled - mean_grad - normed * second)


def remote(source, target, send_sem, recv_sem, dest):
    return pltpu.make_async_remote_copy(
        source, target, send_sem, recv_sem, device_id=dest, device_id_type=MESH
    )


def wait_bytes(ref, sem):
    pltpu.make_async_copy(ref, ref, sem).wait()


SEMS = (
    "tok_s",
    "tok_r",
    "gain_s",
    "gain_r",
    "code_s",
    "code_r",
    "z_s",
    "z_r",
    "rel_s",
    "x_s",
    "x_r",
    "rs_s",
    "rs_r",
    "rz_s",
    "rz_r",
    "far_r",
    "out_s",
    "out_r",
    "pa_s",
    "pa_r",
    "pr_s",
    "pr_r",
    "sum_s",
    "sum_r",
    "all_s",
    "all_r",
)


def layer_kernel(depth, bit_count, shard, rows, *refs):
    (tok, cot, first_in, up_in, down_in, gain_in, pad_in, length_in) = refs[:8]
    (rows_out, g_out, gm_out) = refs[8:11]
    y_out, dx_out = rows_out.at[0], rows_out.at[1]
    (
        xb,
        dyb,
        ab,
        bnb,
        wts,
        wq,
        qkv,
        qtz,
        vt,
        kt,
        pt,
        bias,
        ott,
        orow,
        dorow,
        mid,
        gact,
        dgel,
        prs,
        prr,
        stage,
        rx,
        zrx,
        far_rx,
        gbuf,
        gains,
        code,
        gsum,
        sum_rx,
        all_rx,
        delta,
        shares,
    ) = refs[11:43]
    sem = dict(zip(SEMS, refs[43:]))
    half = depth // 2
    columns = 1 << bit_count
    own_rows = rows // 2
    chunks = own_rows // TILE
    dp = lax.axis_index("dp")
    z = lax.axis_index("tensor")
    c = dp % 2
    p = dp // 2
    buddy = device(p, 1 - c, z)
    mine = pl.multiple_of(own_rows * c, own_rows)
    theirs = pl.multiple_of(own_rows * (1 - c), own_rows)
    lane = lax.broadcasted_iota(jnp.int32, (1, 128), 1)
    low = lane < HD

    def same(to_c, to_z):
        return jnp.logical_and(to_c == c, to_z == z)

    def send_or_copy(is_self, source, target, send_sem, recv_sem, dest):
        @pl.when(is_self)
        def _():
            pltpu.make_async_copy(source, target, recv_sem).start()

        @pl.when(jnp.logical_not(is_self))
        def _():
            remote(source, target, send_sem, recv_sem, dest).start()

    def wait_send(is_self, source, send_sem):
        @pl.when(jnp.logical_not(is_self))
        def _():
            wait_bytes(source, send_sem)

    column_peers = []
    for dz in range(depth):
        for dc in range(2):
            if dz or dc:
                column_peers.append((c if dc == 0 else 1 - c, (z + dz) % depth))
    plane_peers = [flip_mask(p, mask) for mask in range(1, columns)]

    def entry_barrier():
        barrier = pltpu.get_barrier_semaphore()
        peers = [device(p, cc, zz) for cc, zz in column_peers]
        peers += [device(pp, c, z) for pp in plane_peers]
        peers += [device(pp, 1 - c, z) for pp in plane_peers]
        for peer in peers:
            pl.semaphore_signal(barrier, inc=1, device_id=peer, device_id_type=MESH)
        pl.semaphore_wait(barrier, len(peers))

    def make_small():
        gbuf[dp] = jnp.zeros(gbuf.shape[1:], F32)
        gbuf[dp, 0:2, 0:shard] = gain_in[...].astype(F32)
        places = lax.broadcasted_iota(jnp.int32, (1, rows), 1)
        for m in range(2):
            image = jnp.zeros((1, rows), jnp.int32)
            bound = 0
            for k in range(length_in.shape[1]):
                bound = bound + length_in[m, k]
                image = image + (places >= bound).astype(jnp.int32)
            key = jnp.where(pad_in[m : m + 1, :] == 1, image, -1)
            code[c, m : m + 1, :] = image.astype(F32)
            code[c, 2 + m : 3 + m, :] = key.astype(F32)

    def send_small():
        remote(code.at[c], code.at[c], sem["code_s"], sem["code_r"], buddy).start()
        index = 0
        for pp in [p] + plane_peers:
            for cc in (c, 1 - c):
                if index:
                    remote(
                        gbuf.at[dp],
                        gbuf.at[dp],
                        sem["gain_s"].at[index],
                        sem["gain_r"].at[dp],
                        device(pp, cc, z),
                    ).start()
                index += 1

    def finish_small():
        wait_bytes(code.at[c], sem["code_s"])
        wait_bytes(code.at[1 - c], sem["code_r"])
        index = 0
        for pp in [p] + plane_peers:
            for cc in (c, 1 - c):
                if index:
                    wait_bytes(gbuf.at[dp], sem["gain_s"].at[index])
                    source = 2 * pp + cc
                    wait_bytes(gbuf.at[source], sem["gain_r"].at[source])
                index += 1
        rest = jnp.zeros((8, D - 128), F32)
        total = jnp.zeros((8, D), F32)
        for source in range(2 * columns):
            wide = jnp.concatenate([gbuf[source], rest], axis=1)
            total = total + (pltpu.roll(wide, shard * source, 1) if source else wide)
        gains[...] = total

    def row_targets():
        for m in range(2):
            to_z, to_c = 2 * m + c, z // half
            yield m, to_c, to_z, same(to_c, to_z)

    def row_target(which, slot):
        if which == 0:
            return xb.at[slot]
        return dyb.at[pl.ds(pl.multiple_of(own_rows * c + TILE * slot, TILE), TILE)]

    def row_landing(which, slot, to_c):
        if which == 0:
            return xb.at[slot]
        return dyb.at[pl.ds(pl.multiple_of(own_rows * to_c + TILE * slot, TILE), TILE)]

    def send_rows(which, array, to_ends=None):
        def send(m, to_c, to_z, is_self):
            slot = z % half
            send_or_copy(
                is_self,
                array.at[m],
                row_landing(which, slot, to_c),
                sem["tok_s"].at[which, m],
                sem["tok_r"].at[which, slot],
                device(p, to_c, to_z),
            )

        for m, to_c, to_z, is_self in row_targets():
            ship = functools.partial(send, m, to_c, to_z, is_self)
            if to_ends is None:
                ship()
            else:
                pl.when((c == m) if to_ends else (c != m))(ship)

    def rows_sent(which, array):
        for m, to_c, to_z, is_self in row_targets():
            wait_send(is_self, array.at[m], sem["tok_s"].at[which, m])

    def rows_landed(which):
        for slot in range(half):
            wait_bytes(row_target(which, slot), sem["tok_r"].at[which, slot])

    def send_back(which, target):
        for slot in range(half):
            to_c, to_z = z % 2, half * c + slot
            send_or_copy(
                same(to_c, to_z),
                stage.at[slot],
                target.at[z // 2],
                sem["out_s"].at[which, slot],
                sem["out_r"].at[which, z // 2],
                device(p, to_c, to_z),
            )

    def back_sent(which):
        for slot in range(half):
            is_self = same(z % 2, half * c + slot)
            wait_send(is_self, stage.at[slot], sem["out_s"].at[which, slot])

    def back_landed(which, target):
        for m in range(2):
            wait_bytes(target.at[m], sem["out_r"].at[which, m])

    last = depth - 1

    def two_ends(low_core, high_core):
        return jnp.logical_or(
            jnp.logical_and(c == 0, z == low_core), jnp.logical_and(c == 1, z == high_core)
        )

    ends = two_ends(last, 0)
    relays = two_ends(last - 1, 1)
    relay_to = device(p, c, last * (1 - c))
    relay_from = device(p, c, last - 1 + c * (2 - last))

    def unit_rows(unit, column, color):
        _, start, size = unit
        return pl.ds(pl.multiple_of((2 * column + color) * shard + start, 16), size)

    def unit_source(unit):
        return (first_in, up_in, down_in)[unit[0]].at[pl.ds(unit[1], unit[2])]

    def z_targets():
        for dz in range(depth):
            to_z = (z + dz) % depth
            yield dz, z // half, to_z, to_z == last * (1 - z // half)

    def gather_z(u):
        unit = GATHER[u]
        for dz, to_c, to_z, far in z_targets():
            source = unit_source(unit)
            target = wts.at[unit[0], z % half, unit_rows(unit, p, c)]
            recv = sem["z_r"].at[u, c, z % half]
            if dz == 0:
                send_or_copy(
                    to_c == c, source, target, sem["z_s"].at[u, dz], recv, device(p, to_c, to_z)
                )
            else:

                @pl.when(jnp.logical_not(far))
                def _():
                    remote(
                        source, target, sem["z_s"].at[u, dz], recv, device(p, to_c, to_z)
                    ).start()

    def gather_z_sent(u):
        for dz, to_c, to_z, far in z_targets():
            skip = to_c == c if dz == 0 else far
            wait_send(skip, unit_source(GATHER[u]), sem["z_s"].at[u, dz])

    def relay_block(u, color, slot):
        unit = GATHER[u]
        return wts.at[unit[0], slot, unit_rows(unit, p, color)]

    def gather_z_landed(u):
        unit = GATHER[u]
        for color in range(2):
            for slot in range(half):
                wait_bytes(
                    wts.at[unit[0], slot, unit_rows(unit, p, color)], sem["z_r"].at[u, color, slot]
                )

    def forward(u):
        @pl.when(relays)
        def _():
            gather_z_landed(u)
            for color in range(2):
                for slot in range(half):
                    block = relay_block(u, color, slot)
                    remote(
                        block,
                        block,
                        sem["rel_s"].at[u, color, slot],
                        sem["z_r"].at[u, color, slot],
                        relay_to,
                    ).start()

    def after_z(u):
        pl.when(jnp.logical_not(relays))(functools.partial(gather_z_landed, u))
        gather_step(u, 0)

    def gather_blocks(u, color, s, landed):
        unit = GATHER[u]
        order = color_order(color, bit_count)
        for index, mask in enumerate(submasks(order[:s])):
            column = flip_mask(p, mask)
            if landed:
                column = flip(column, order[s])
            yield index, wts.at[unit[0], :, unit_rows(unit, column, color)]

    def gather_step(u, s):
        for color in range(2):
            to = device(flip(p, color_order(color, bit_count)[s]), c, z)
            for index, block in gather_blocks(u, color, s, False):
                remote(
                    block,
                    block,
                    sem["x_s"].at[u, color, s, index],
                    sem["x_r"].at[u, color, s, index],
                    to,
                ).start()

    def gather_next(u, s):
        for color in range(2):
            for index, block in gather_blocks(u, color, s, True):
                wait_bytes(block, sem["x_r"].at[u, color, s, index])
        if s + 1 < bit_count:
            gather_step(u, s + 1)

    def gather_last(*units):
        for u in units:
            for s in range(1, bit_count):
                gather_next(u, s)

    def gather_sent(k):
        for u, unit in enumerate(GATHER):
            if unit[0] == k:
                gather_unit_sent(u)

    def gather_unit_sent(u):
        gather_z_sent(u)

        @pl.when(relays)
        def _():
            for color in range(2):
                for slot in range(half):
                    wait_bytes(relay_block(u, color, slot), sem["rel_s"].at[u, color, slot])

        for color in range(2):
            for s in range(bit_count):
                for index, block in gather_blocks(u, color, s, False):
                    wait_bytes(block, sem["x_s"].at[u, color, s, index])

    place = {2: 0, 1: 1, 0: 2}

    def rx_slot(u, color, s, index):
        unit = SCATTER[u]
        slot = (1 << bit_count) - (1 << (bit_count - s)) + index
        return rx.at[unit[0], color, slot, :, pl.ds(unit[1], unit[2])]

    def scatter_order(color):
        return color_order(color, bit_count)[::-1]

    def scatter_blocks(u, color, s, away):
        unit = SCATTER[u]
        order = scatter_order(color)
        for index, mask in enumerate(submasks(order[s + 1 :])):
            column = flip_mask(p, mask)
            if away:
                column = flip(column, order[s])
            yield index, wts.at[place[unit[0]], :, unit_rows(unit, column, color)]

    def scatter_step(u, s):
        for color in range(2):
            to = device(flip(p, scatter_order(color)[s]), c, z)
            for index, block in scatter_blocks(u, color, s, True):
                remote(
                    block,
                    rx_slot(u, color, s, index),
                    sem["rs_s"].at[u, color, s, index],
                    sem["rs_r"].at[u, color, s, index],
                    to,
                ).start()

    def scatter_next(u, s):
        for color in range(2):
            for index, block in scatter_blocks(u, color, s, False):
                got = rx_slot(u, color, s, index)
                wait_bytes(got, sem["rs_r"].at[u, color, s, index])
                block[...] = (block[...].astype(F32) + got[...].astype(F32)).astype(BF16)
        if s + 1 < bit_count:
            scatter_step(u, s + 1)
        else:
            scatter_z(u)

    def scatter_last(*units):
        for u in units:
            for s in range(1, bit_count):
                scatter_next(u, s)

    def scatter_z_blocks(u):
        unit = SCATTER[u]
        for color in range(2):
            for slot in range(half):
                to_z = half * c + slot
                block = wts.at[place[unit[0]], slot, unit_rows(unit, p, color)]
                yield color, slot, to_z, block

    def summed_on_the_way(u):
        return SCATTER[u][0] in RELAYED

    def landing(u, source):
        unit = SCATTER[u]
        return zrx.at[unit[0], source, pl.ds(unit[1], unit[2])]

    def far_landing(u, color, slot):
        unit = SCATTER[u]
        return far_rx.at[unit[0], color, slot, pl.ds(unit[1], unit[2])]

    def scatter_z(u):
        for color, slot, to_z, block in scatter_z_blocks(u):
            send, recv = sem["rz_s"].at[u, color, slot], sem["rz_r"].at[u, z]
            dest = device(p, color, to_z)
            if not summed_on_the_way(u):
                send_or_copy(same(color, to_z), block, landing(u, z), send, recv, dest)
                continue

            @pl.when(jnp.logical_not(jnp.logical_or(ends, relays)))
            def _():
                send_or_copy(same(color, to_z), block, landing(u, z), send, recv, dest)

            @pl.when(ends)
            def _():
                remote(
                    block,
                    far_landing(u, color, slot),
                    send,
                    sem["far_r"].at[u, color, slot],
                    relay_from,
                ).start()

    def scatter_relay(u):
        @pl.when(relays)
        def _():
            for color, slot, to_z, block in scatter_z_blocks(u):
                got = far_landing(u, color, slot)
                wait_bytes(got, sem["far_r"].at[u, color, slot])
                block[...] = (block[...].astype(F32) + got[...].astype(F32)).astype(BF16)
                send, recv = sem["rz_s"].at[u, color, slot], sem["rz_r"].at[u, z]
                dest = device(p, color, to_z)
                send_or_copy(same(color, to_z), block, landing(u, z), send, recv, dest)

    def scatter_finish(u):
        unit = SCATTER[u]
        for source in range(depth):
            got = functools.partial(wait_bytes, landing(u, source), sem["rz_r"].at[u, source])
            if summed_on_the_way(u) and source in (0, last):
                pl.when(z // half != (last - source) // half)(got)
            else:
                got()
        total = landing(u, 0)[...].astype(F32)
        for source in range(1, depth):
            total = total + landing(u, source)[...].astype(F32)
        g_out[unit[0], unit[1] : unit[1] + unit[2]] = total

    def scatter_sent(u):
        for color in range(2):
            for s in range(bit_count):
                for index, block in scatter_blocks(u, color, s, True):
                    wait_bytes(block, sem["rs_s"].at[u, color, s, index])
        for color, slot, to_z, block in scatter_z_blocks(u):
            local = same(color, to_z)
            if summed_on_the_way(u):
                local = jnp.logical_and(local, jnp.logical_not(ends))
            wait_send(local, block, sem["rz_s"].at[u, color, slot])

    def clear_far():
        for source in (0, last):

            @pl.when(z // half == (last - source) // half)
            def _():
                for k in RELAYED:
                    zrx[k, source] = jnp.zeros(zrx.shape[2:], BF16)

    def pair_send(index, buffer):
        own = buffer.at[pl.ds(mine, own_rows)]
        remote(own, own, sem["pa_s"].at[index], sem["pa_r"].at[index], buddy).start()

    def pair_landed(index, buffer):
        wait_bytes(buffer.at[pl.ds(theirs, own_rows)], sem["pa_r"].at[index])

    def pair_sent(index, buffer):
        wait_bytes(buffer.at[pl.ds(mine, own_rows)], sem["pa_s"].at[index])

    def part_send(index):
        remote(
            prs.at[index % 2],
            prr.at[index % 2],
            sem["pr_s"].at[index],
            sem["pr_r"].at[index],
            buddy,
        ).start()

    def part_landed(index):
        wait_bytes(prr.at[index % 2], sem["pr_r"].at[index])

    def part_sent(index):
        wait_bytes(prs.at[index % 2], sem["pr_s"].at[index])

    def each_half(body, second=None):
        def step(i, carry):
            if second is not None:
                pl.when(i == 1)(second)
            body(pl.multiple_of(jnp.where(i == 0, mine, theirs), own_rows))
            return carry

        lax.fori_loop(0, 2, step, 0)

    def own_chunks(body):
        def step(i, carry):
            body(i, pl.multiple_of(i * TILE, TILE), pl.multiple_of(mine + i * TILE, TILE))
            return carry

        lax.fori_loop(0, chunks, step, 0)

    make_small()
    entry_barrier()
    send_small()
    for u in range(5):
        gather_z(u)
    send_rows(0, tok)

    for h in range(6):
        qtz[h, HD * (1 - h % 2) : HD * (1 - h % 2) + HD, :] = jnp.zeros((HD, rows), BF16)
    gsum[...] = jnp.zeros(gsum.shape, F32)
    clear_far()
    forward(0)
    after_z(0)
    finish_small()
    gain_first = gains[0:1, :]
    gain_second = gains[1:2, :]
    forward(1)
    after_z(1)
    gather_next(0, 0)

    forward(2)
    after_z(2)
    gather_next(1, 0)
    forward(3)
    after_z(3)
    gather_next(2, 0)
    forward(4)
    after_z(4)
    gather_z(5)
    micro = z // 2
    owner = z % 2
    query_image = code[owner, pl.ds(micro, 1), :]
    key_code = code[owner, pl.ds(2 + micro, 1), :]
    key_columns = jnp.broadcast_to(key_code, (128, rows)).T
    for block in range(rows // 128):
        span = slice(128 * block, 128 * block + 128)
        key = key_columns[span, 0:1]
        row_id = lax.broadcasted_iota(jnp.int32, (128, rows), 0) + 128 * block
        col_id = lax.broadcasted_iota(jnp.int32, (128, rows), 1)
        seen = jnp.logical_or(key == query_image, row_id == col_id)
        bias[span, :] = jnp.where(seen, 0.0, NEGATIVE)

    gather_next(3, 0)
    rows_landed(0)

    def first_norm(i, at, base):
        normed, _ = normalize(xb[i].astype(F32))
        ab[pl.ds(base, TILE), :] = (normed * gain_first).astype(BF16)

    own_chunks(first_norm)
    pair_send(0, ab)
    gather_last(0, 1, 2)

    def roll(value):
        return pltpu.roll(value, HD, 1)

    for name, offset in (("q", 0), ("k", 384), ("v", 768), ("o", 1152)):
        tile = {"q": 0, "k": 128, "v": 256, "o": 640}[name]
        wq[:, offset : offset + 128] = wts[0, 0, :, tile : tile + 128]
        wq[:, offset + 128 : offset + 256] = wts[0, 1, :, tile : tile + 128]
        mixed = {"q": 384, "k": 384, "v": 512, "o": 512}[name]
        one = wts[0, 0, :, mixed : mixed + 128].astype(F32)
        two = wts[0, 1, :, mixed : mixed + 128].astype(F32)
        if name in ("q", "v"):
            both = jnp.where(low, one, roll(two))
        else:
            both = jnp.where(low, roll(one), two)
        wq[:, offset + 256 : offset + 384] = both.astype(BF16)

    def project(base):
        span = pl.ds(base, own_rows)
        source = ab[span, :]
        for part in range(3):
            result = dot(source, wq[:, 384 * part : 384 * part + 384])
            if part == 0:
                result = result * SCALE
            qkv[span, 384 * part : 384 * part + 384] = result.astype(BF16)
            turned = result.T.astype(BF16)
            if part == 0:
                for h in range(6):
                    at = HD * (h % 2)
                    qtz[h, at : at + HD, span] = turned[HD * h : HD * h + HD]
            elif part == 1:
                kt[:, span] = turned
            else:
                vt[:, span] = turned

    forward(5)
    each_half(project, lambda: pair_landed(0, ab))

    def attend(base, hook):
        span = pl.ds(base, own_rows)
        for h in range(6):
            pair = h // 2
            keys = qkv[:, 384 + 128 * pair : 512 + 128 * pair]
            scores = dot(keys, qtz[h, :, span]) + bias[:, span]
            highest = jnp.max(scores, axis=0, keepdims=True)
            exponent = jnp.exp(scores - highest)
            total = jnp.sum(exponent, axis=0, keepdims=True)
            rounded = exponent.astype(BF16)
            pt[h, :, span] = rounded
            share = 1.0 / total
            shares[h, :, span] = share
            mixed = dot(vt[HD * h : HD * h + HD, :], rounded) * share
            ott[HD * h : HD * h + HD, span] = mixed.astype(BF16)
            hook(h)
        orow[span, :] = ott[:, span].T

    def attend_loop(i, carry):
        base = pl.multiple_of(jnp.where(i == 0, theirs, mine), own_rows)

        def hook(h):
            if h == 0:

                @pl.when(i == 1)
                def _():
                    send_rows(1, cot, True)

            if h == 1:

                @pl.when(i == 0)
                def _():
                    gather_next(4, 0)
                    send_rows(1, cot, False)

            if h == 4:

                @pl.when(i == 0)
                def _():
                    after_z(5)

            if h == 5:

                @pl.when(i == 1)
                def _():
                    gather_next(5, 0)

        attend(base, hook)

        @pl.when(i == 0)
        def _():
            prs[0] = dot_nt(orow[pl.ds(base, own_rows), :], wq[:, 1152:1536]).astype(BF16)
            part_send(0)

        return carry

    lax.fori_loop(0, 2, attend_loop, 0)

    def own_out(i, at, base):
        mid[pl.ds(at, TILE), :] = dot_nt(orow[pl.ds(base, TILE), :], wq[:, 1152:1536])

    own_chunks(own_out)
    part_landed(0)

    def second_norm(i, at, base):
        here = pl.ds(at, TILE)
        middle = xb[i].astype(F32) + (mid[here, :] + prr[0, here, :].astype(F32))
        mid[here, :] = middle
        normed, _ = normalize(middle)
        bnb[pl.ds(base, TILE), :] = (normed * gain_second).astype(BF16)

    own_chunks(second_norm)
    pair_send(1, bnb)
    gather_last(3, 4)

    def expand(base):
        def chunk(i, carry):
            span = pl.ds(pl.multiple_of(base + i * TILE, TILE), TILE)
            source = bnb[span, :]
            for j in range(half):
                pre = dot(source, wts[1, j])
                cdf = 0.5 * (1.0 + lax.erf(pre * 0.7071067811865476))
                density = jnp.exp(pre * pre * -0.5) * 0.3989422804014327
                gact[j, span, :] = (pre * cdf).astype(BF16)
                dgel[j, span, :] = (cdf + pre * density).astype(BF16)
            return carry

        lax.fori_loop(0, chunks, chunk, 0)

    rows_landed(1)
    pair_send(2, dyb)
    each_half(expand, lambda: pair_landed(1, bnb))
    gather_sent(0)

    def grad_tiles(source, slot, width_of):
        def tile(t, carry):
            at = pl.multiple_of(t * TILE, TILE)
            turned = source[:, pl.ds(at, TILE)].T
            width_of(turned, slot, pl.ds(at, TILE))
            return carry

        lax.fori_loop(0, D // TILE, tile, 0)

    def down_tile(turned, slot, span):
        for j in range(half):
            wts[slot, j, span, :] = dot(turned, gact[j]).astype(BF16)

    def up_tile(turned, slot, span):
        for j in range(half):
            wts[slot, j, span, :] = dot(turned, dgel[j]).astype(BF16)

    pair_landed(2, dyb)
    grad_tiles(dyb, place[2], down_tile)
    scatter_step(0, 0)
    scatter_step(1, 0)
    gather_last(5)

    def contract(base, j_refs, weight):
        total = dot_nt(j_refs[0, pl.ds(base, TILE), :], wts[weight, 0])
        for j in range(1, half):
            total = total + dot_nt(j_refs[j, pl.ds(base, TILE), :], wts[weight, j])
        return total

    def their_chunks(buffer, weight, into):
        def step(i, carry):
            base = pl.multiple_of(theirs + i * TILE, TILE)
            into[pl.ds(pl.multiple_of(i * TILE, TILE), TILE), :] = contract(
                base, buffer, weight
            ).astype(BF16)
            return carry

        lax.fori_loop(0, chunks, step, 0)

    their_chunks(gact, 2, prs.at[1])
    part_send(1)

    def through_gelu(base):
        def chunk(i, carry):
            span = pl.ds(pl.multiple_of(base + i * TILE, TILE), TILE)
            source = dyb[span, :]
            for j in range(half):
                grad_act = dot(source, wts[2, j])
                dgel[j, span, :] = (grad_act * dgel[j, span, :].astype(F32)).astype(BF16)
            return carry

        lax.fori_loop(0, chunks, chunk, 0)

    each_half(through_gelu)
    part_sent(0)
    their_chunks(dgel, 1, prs.at[0])
    part_send(2)
    part_landed(1)

    def layer_rows(i, at, base):
        here = pl.ds(at, TILE)
        total = contract(base, gact, 2) + prr[1, here, :].astype(F32)
        stage[i] = (mid[here, :] + total).astype(BF16)

    own_chunks(layer_rows)
    scatter_next(0, 0)
    send_back(0, y_out)
    pair_sent(2, dyb)
    part_landed(2)

    def second_back(i, at, base):
        here = pl.ds(at, TILE)
        grad = contract(base, dgel, 1) + prr[0, here, :].astype(F32)
        normed, inverse = normalize(mid[here, :])
        gsum[1:2, :] += jnp.sum(grad * normed, axis=0, keepdims=True)
        down = dyb[pl.ds(base, TILE), :].astype(F32) + norm_back(
            grad, gain_second, normed, inverse
        )
        mid[here, :] = down
        dyb[pl.ds(base, TILE), :] = down.astype(BF16)

    own_chunks(second_back)
    pair_send(3, dyb)
    gather_sent(1)
    scatter_next(1, 0)
    grad_tiles(bnb, place[1], up_tile)
    scatter_step(2, 0)
    scatter_step(3, 0)

    def spread_mix(base):
        span = pl.ds(base, own_rows)
        result = dot(dyb[span, :], wq[:, 1152:1536])
        result = result.astype(BF16).astype(F32)
        turned = result.T
        pieces = []
        for h in range(6):
            at = HD * (h % 2)
            piece = (turned[HD * h : HD * h + HD] * shares[h, :, span]).astype(BF16)
            pieces.append(piece.astype(F32))
            qtz[h, at : at + HD, span] = piece
            product = piece.astype(F32) * ott[HD * h : HD * h + HD, span].astype(F32)
            delta[h, :, span] = jnp.sum(product, axis=0, keepdims=True)
        dorow[span, :] = jnp.concatenate(pieces, axis=0).T.astype(BF16)

    each_half(spread_mix, lambda: pair_landed(3, dyb))
    scatter_last(0)

    def attend_back(pair, carry):
        def tile(offset):
            return pl.ds(pl.multiple_of(offset + 128 * pair, 128), 128)

        parts = []
        for hh in range(2):
            h = 2 * pair + hh
            grad_values = dot(pt[h], dorow[:, tile(0)])
            for q in range(rows // own_rows):
                span = slice(q * own_rows, (q + 1) * own_rows)
                grad_prob = dot(qkv[:, tile(768)], qtz[h, :, span])
                chance = pt[h, :, span].astype(F32)
                pt[h, :, span] = (chance * (grad_prob - delta[h, :, span])).astype(BF16)
            grad_keys = dot(pt[h], qkv[:, tile(0)])
            head = pl.ds(pl.multiple_of(HD * h, HD), HD)
            grad_queries = dot(kt[head, :], pt[h]) * SCALE
            parts.append((grad_queries, grad_keys, grad_values))
        qkv[:, tile(768)] = jnp.where(low, parts[0][2], parts[1][2]).astype(BF16)
        qkv[:, tile(384)] = jnp.where(low, parts[0][1], parts[1][1]).astype(BF16)
        turned = jnp.concatenate([parts[0][0], parts[1][0]], axis=0).T
        qkv[:, tile(0)] = turned.astype(BF16)

        @pl.when(pair == 0)
        def _():
            scatter_last(1)

        @pl.when(pair == 1)
        def _():
            scatter_next(2, 0)

        @pl.when(pair == 2)
        def _():
            scatter_next(3, 0)

        return carry

    lax.fori_loop(0, 3, attend_back, 0)

    def first_contract(base, size):
        return dot_nt(qkv[pl.ds(base, size), :], wq[:, 0:1152])

    part_sent(1)
    prs[1] = first_contract(theirs, own_rows).astype(BF16)
    part_send(3)
    gather_sent(2)

    def first_tiles(t, carry):
        at = pl.multiple_of(t * TILE, TILE)
        span = pl.ds(at, TILE)
        slot = place[0]
        qkv_part = dot(ab[:, span].T, qkv[...])
        out_part = dot(dyb[:, span].T, orow[...])
        for i, target in ((0, 0), (1, 128), (2, 256)):
            for j in range(2):
                at = 384 * i + 128 * j
                wts[slot, j, span, target : target + 128] = qkv_part[:, at : at + 128].astype(BF16)
        for j in range(2):
            wts[slot, j, span, 640:768] = out_part[:, 128 * j : 128 * j + 128].astype(BF16)
        mixed_q = qkv_part[:, 256:384]
        mixed_k = qkv_part[:, 640:768]
        mixed_v = qkv_part[:, 1024:1152]
        mixed_o = out_part[:, 256:384]
        wts[slot, 0, span, 384:512] = jnp.where(low, mixed_q, roll(mixed_k)).astype(BF16)
        wts[slot, 1, span, 384:512] = jnp.where(low, roll(mixed_q), mixed_k).astype(BF16)
        wts[slot, 0, span, 512:640] = jnp.where(low, mixed_v, roll(mixed_o)).astype(BF16)
        wts[slot, 1, span, 512:640] = jnp.where(low, roll(mixed_v), mixed_o).astype(BF16)
        return carry

    lax.fori_loop(0, D // TILE, first_tiles, 0)
    scatter_step(4, 0)
    scatter_step(5, 0)

    back_sent(0)
    back_landed(0, y_out)
    scatter_relay(0)
    scatter_last(2)
    scatter_relay(1)
    part_landed(3)

    def first_back(i, at, base):
        here = pl.ds(at, TILE)
        grad = first_contract(base, TILE) + prr[1, here, :].astype(F32)
        normed, inverse = normalize(xb[i].astype(F32))
        gsum[0:1, :] += jnp.sum(grad * normed, axis=0, keepdims=True)
        result = mid[here, :] + norm_back(grad, gain_first, normed, inverse)
        stage[i] = result.astype(BF16)

    own_chunks(first_back)

    me = 2 * z + c
    for index, (cc, zz) in enumerate(column_peers):
        remote(
            gsum,
            sum_rx.at[me],
            sem["sum_s"].at[index],
            sem["sum_r"].at[me],
            device(p, cc, zz),
        ).start()
    pltpu.make_async_copy(gsum, sum_rx.at[me], sem["sum_r"].at[me]).start()
    scatter_last(3)
    send_back(1, dx_out)
    scatter_next(4, 0)
    scatter_relay(2)
    scatter_next(5, 0)
    scatter_relay(3)
    scatter_last(4)
    scatter_last(5)
    for source in range(2 * depth):
        wait_bytes(sum_rx.at[source], sem["sum_r"].at[source])
    for index in range(len(column_peers)):
        wait_bytes(gsum, sem["sum_s"].at[index])
    total = sum_rx[0]
    for source in range(1, 2 * depth):
        total = total + sum_rx[source]
    gsum[...] = total
    for index, pp in enumerate(plane_peers):
        remote(
            gsum, all_rx.at[p], sem["all_s"].at[index], sem["all_r"].at[p], device(pp, c, z)
        ).start()
    pltpu.make_async_copy(gsum, all_rx.at[p], sem["all_r"].at[p]).start()
    scatter_relay(4)
    scatter_relay(5)
    scatter_finish(0)
    scatter_finish(1)
    for source in range(columns):
        wait_bytes(all_rx.at[source], sem["all_r"].at[source])
    for index in range(len(plane_peers)):
        wait_bytes(gsum, sem["all_s"].at[index])
    total = all_rx[0]
    for source in range(1, columns):
        total = total + all_rx[source]
    place_of = (2 * D // (2 * columns * depth)) * (dp * depth + z)
    wanted = jnp.where(place_of < D, total[0:1, :], total[1:2, :])
    turn = (D - place_of % D) % D
    gm_out[...] = pltpu.roll(jnp.broadcast_to(wanted, (8, D)), turn, 1)[:, 0:128]
    for u in (2, 3, 4, 5):
        scatter_finish(u)

    back_landed(1, dx_out)
    back_sent(1)
    rows_sent(0, tok)
    rows_sent(1, cot)
    pair_sent(0, ab)
    pair_sent(1, bnb)
    pair_sent(3, dyb)
    part_sent(2)
    part_sent(3)
    for u in range(len(SCATTER)):
        scatter_sent(u)


def whole_layer(mesh, tok, cot, first, up, down, gains, padding, lengths):
    depth = mesh.shape["tensor"]
    bit_count = (mesh.shape["dp"] // 2).bit_length() - 1
    columns = 1 << bit_count
    shard = up.shape[0]
    half = depth // 2
    rows = padding.shape[1]
    own = rows // 2
    vmem = pl.BlockSpec(memory_space=pltpu.VMEM)
    hbm = pl.BlockSpec(memory_space=pl.ANY)
    sem = pltpu.SemaphoreType.DMA
    blocks = 1 << (bit_count - 1)
    scratch = [
        ((half, TILE, D), BF16),
        ((rows, D), BF16),
        ((rows, D), BF16),
        ((rows, D), BF16),
        ((KINDS, half, D, D), BF16),
        ((D, 2 * D), BF16),
        ((rows, 1152), BF16),
        ((6, 128, rows), BF16),
        ((384, rows), BF16),
        ((384, rows), BF16),
        ((6, rows, rows), BF16),
        ((rows, rows), F32),
        ((384, rows), BF16),
        ((rows, 384), BF16),
        ((rows, 384), BF16),
        ((own, D), F32),
        ((half, rows, D), BF16),
        ((half, rows, D), BF16),
        ((2, own, D), BF16),
        ((2, own, D), BF16),
        ((half, TILE, D), BF16),
        ((KINDS, 2, columns - 1, half, shard, D), BF16),
        ((KINDS, depth, shard, D), BF16),
        ((KINDS, 2, half, shard, D), BF16),
        ((2 * columns, 8, 128), F32),
        ((8, D), F32),
        ((2, 8, rows), F32),
        ((8, D), F32),
        ((2 * depth, 8, D), F32),
        ((columns, 8, D), F32),
        ((6, 1, rows), F32),
        ((6, 1, rows), F32),
    ]
    sems = {
        "tok_s": (2, 2),
        "tok_r": (2, half),
        "gain_s": (2 * columns,),
        "gain_r": (2 * columns,),
        "code_s": (),
        "code_r": (),
        "z_s": (len(GATHER), depth),
        "z_r": (len(GATHER), 2, half),
        "rel_s": (len(GATHER), 2, half),
        "x_s": (len(GATHER), 2, bit_count, blocks),
        "x_r": (len(GATHER), 2, bit_count, blocks),
        "rs_s": (len(SCATTER), 2, bit_count, blocks),
        "rs_r": (len(SCATTER), 2, bit_count, blocks),
        "rz_s": (len(SCATTER), 2, half),
        "rz_r": (len(SCATTER), depth),
        "far_r": (len(SCATTER), 2, half),
        "out_s": (2, half),
        "out_r": (2, 2),
        "pa_s": (4,),
        "pa_r": (4,),
        "pr_s": (4,),
        "pr_r": (4,),
        "sum_s": (2 * depth - 1,),
        "sum_r": (2 * depth,),
        "all_s": (columns - 1,),
        "all_r": (columns,),
    }
    return pl.pallas_call(
        functools.partial(layer_kernel, depth, bit_count, shard, rows),
        out_shape=(
            jax.ShapeDtypeStruct((2,) + tok.shape, BF16),
            jax.ShapeDtypeStruct((KINDS,) + up.shape, F32),
            jax.ShapeDtypeStruct((8, 128), F32),
        ),
        in_specs=[hbm] * 5 + [vmem, vmem, pl.BlockSpec(memory_space=pltpu.SMEM)],
        out_specs=(hbm, vmem, vmem),
        scratch_shapes=[pltpu.VMEM(shape, dtype) for shape, dtype in scratch]
        + [sem(sems[name]) for name in SEMS],
        compiler_params=pltpu.CompilerParams(
            collective_id=0, has_side_effects=True, vmem_limit_bytes=67043328
        ),
        name="whole_layer",
    )(tok, cot, first, up, down, gains, padding, lengths)


def block_body(mesh, tokens, cotangent, lengths, padding, ln_gain, w_qkv, w_out, w_up, w_down):
    depth = mesh.shape["tensor"]
    shard = w_up.shape[1]
    pair = 2 * HD

    qkv = w_qkv[0]
    out_t = w_out[0].T
    packed = jnp.concatenate(
        [
            qkv[:, 0, :pair],
            qkv[:, 1, :pair],
            qkv[:, 2, :pair],
            qkv[:, 0, pair:],
            qkv[:, 1, pair:],
            qkv[:, 2, pair:],
            out_t[:, pair:],
            out_t[:, :pair],
        ],
        axis=1,
    )
    rows_back, summed, gain_sum = whole_layer(
        mesh,
        tokens,
        cotangent,
        packed,
        w_up[0],
        w_down[0].T,
        ln_gain[0],
        padding,
        lengths[:, 0],
    )
    gain_result = gain_sum[0, : 2 * D // (mesh.shape["dp"] * depth)]
    first = summed[0]
    qkv_grad = jnp.stack(
        [
            jnp.concatenate(
                [
                    first[:, pair * i : pair * i + pair],
                    first[:, 3 * pair + HD * i : 3 * pair + HD * i + HD],
                ],
                axis=1,
            )
            for i in range(3)
        ],
        axis=1,
    )[None]
    out_grad = jnp.concatenate([first[:, 5 * pair :], first[:, 4 * pair + HD : 5 * pair]], axis=1)
    return (
        rows_back[0].astype(F32),
        rows_back[1].astype(F32),
        gain_result,
        qkv_grad,
        out_grad.T[None],
        summed[1][None],
        summed[2].T[None],
    )


def visible(lengths_row, padding_row):
    places = lax.iota(jnp.int32, padding_row.shape[0])
    bounds = jnp.cumsum(lengths_row)
    picture = jnp.sum((places[:, None] >= bounds[None, :]).astype(jnp.int32), axis=1)
    same_image = picture[:, None] == picture[None, :]
    return same_image & ((padding_row[None, :] == 1) | (places[:, None] == places[None, :]))


def gelu_exact(pre_values):
    return jax.nn.gelu(pre_values, approximate=False)


def masked_scores(queries, key_rows, allowed):
    scaling = queries.shape[-1] ** (-0.5)
    scores = (
        jnp.einsum("qhd,khd->hqk", queries, key_rows, preferred_element_type=jnp.float32) * scaling
    )
    return (jnp.where(allowed[None], scores, NEGATIVE), scaling)


def attend(stacked, allowed):
    scores, scaling = masked_scores(stacked[:, 0], stacked[:, 1], allowed)
    highest = jnp.max(scores, axis=-1, keepdims=True)
    exponent = jnp.exp(scores - highest)
    totals = jnp.sum(exponent, axis=-1, keepdims=True)
    rounded = (exponent / totals).astype(jnp.bfloat16)
    mixture = jnp.einsum("hqk,khd->qhd", rounded, stacked[:, 2], preferred_element_type=jnp.float32)
    return (mixture, highest, totals)


def attend_back(stacked, allowed, highest, totals, grad_mix):
    queries, key_rows, value_rows = (stacked[:, 0], stacked[:, 1], stacked[:, 2])
    scores, scaling = masked_scores(queries, key_rows, allowed)
    probability = jnp.exp(scores - highest) / totals
    rounded = probability.astype(jnp.bfloat16)
    grad_prob = jnp.einsum("qhd,khd->hqk", grad_mix, value_rows, preferred_element_type=jnp.float32)
    grad_values = jnp.einsum("hqk,qhd->khd", rounded, grad_mix, preferred_element_type=jnp.float32)
    inner_sum = jnp.sum(probability * grad_prob, axis=-1, keepdims=True)
    grad_scores = (probability * (grad_prob - inner_sum)).astype(jnp.bfloat16)
    grad_queries = (
        jnp.einsum("hqk,khd->qhd", grad_scores, key_rows, preferred_element_type=jnp.float32)
        * scaling
    )
    grad_keys = (
        jnp.einsum("hqk,qhd->khd", grad_scores, queries, preferred_element_type=jnp.float32)
        * scaling
    )
    return jnp.stack([grad_queries, grad_keys, grad_values], axis=1).astype(jnp.bfloat16)


def collect_weights(ln_gain, w_qkv, w_out, w_up, w_down, layer_index):
    return (
        lax.all_gather(ln_gain[layer_index], "dp", axis=1, tiled=True),
        lax.all_gather(w_qkv[layer_index], "dp", axis=0, tiled=True),
        lax.all_gather(w_out[layer_index], "dp", axis=1, tiled=True),
        lax.all_gather(w_up[layer_index], "dp", axis=0, tiled=True),
        lax.all_gather(w_down[layer_index], "dp", axis=1, tiled=True),
    )


def spread(block_rows):
    return lax.all_gather(block_rows, "tensor", axis=0, tiled=True)


def spread_grad(block_rows):
    return lax.all_gather(block_rows, "tensor", axis=0, tiled=True)


def collect_rows(operand, weight):
    return lax.psum_scatter(
        jnp.dot(operand, weight, preferred_element_type=jnp.float32),
        "tensor",
        scatter_dimension=0,
        tiled=True,
    )


def return_rows(operand, weight):
    return lax.psum_scatter(
        lax.dot_general(
            operand, weight, (((1,), (1,)), ((), ())), preferred_element_type=jnp.float32
        ),
        "tensor",
        scatter_dimension=0,
        tiled=True,
    )


def reduce_grads(pieces):
    return (
        lax.psum_scatter(pieces[0], "dp", scatter_dimension=0, tiled=True),
        lax.psum_scatter(pieces[1], "dp", scatter_dimension=1, tiled=True),
        lax.psum_scatter(pieces[2], "dp", scatter_dimension=0, tiled=True),
        lax.psum_scatter(pieces[3], "dp", scatter_dimension=1, tiled=True),
    )


def body(tokens, cotangent, lengths, padding, ln_gain, w_qkv, w_out, w_up, w_down):
    layer_count = w_qkv.shape[0]
    micro_count = tokens.shape[0]
    residual = [tokens[batch_index].astype(jnp.float32) for batch_index in range(micro_count)]
    visibility = [
        visible(lengths[batch_index, 0], padding[batch_index]) for batch_index in range(micro_count)
    ]
    saved = []
    stored_weights = []
    layer_index = 0
    stored_weights.append(None)
    for batch_index in range(micro_count):
        weights = collect_weights(ln_gain, w_qkv, w_out, w_up, w_down, layer_index)
        gain_pair, qkv_weight, out_weight, up_weight, down_weight = weights
        gain_first = gain_pair[0].astype(jnp.float32)
        gain_second = gain_pair[1].astype(jnp.float32)
        entering = residual[batch_index]
        normed, inverse = normalize(entering)
        first_input = spread((normed * gain_first).astype(jnp.bfloat16))
        triple = jnp.einsum(
            "rd,dcn->rcn", first_input, qkv_weight, preferred_element_type=jnp.float32
        ).astype(jnp.bfloat16)
        stacked = triple.reshape(triple.shape[0], 3, -1, HD)
        mixture, highest, totals = attend(stacked, visibility[batch_index])
        mix_rounded = mixture.reshape(mixture.shape[0], -1).astype(jnp.bfloat16)
        middle = entering + collect_rows(mix_rounded, out_weight)
        normed_two, inverse_two = normalize(middle)
        second_input = spread((normed_two * gain_second).astype(jnp.bfloat16))
        hidden_pre = jnp.dot(second_input, up_weight, preferred_element_type=jnp.float32)
        activated = gelu_exact(hidden_pre).astype(jnp.bfloat16)
        residual[batch_index] = middle + collect_rows(activated, down_weight)
        saved.append(
            (
                entering,
                first_input,
                stacked,
                highest,
                totals,
                mix_rounded,
                middle,
                second_input,
                hidden_pre,
                activated,
            )
        )
    gradients = [cotangent[batch_index].astype(jnp.float32) for batch_index in range(micro_count)]
    gain_parts = [jnp.zeros((2, D), jnp.float32)]
    weight_results = [None]
    for layer_index in reversed(range(layer_count)):
        summed = None
        for batch_index in range(micro_count):
            weights = collect_weights(ln_gain, w_qkv, w_out, w_up, w_down, layer_index)
            gain_pair, qkv_weight, out_weight, up_weight, down_weight = weights
            gain_first = gain_pair[0].astype(jnp.float32)
            gain_second = gain_pair[1].astype(jnp.float32)
            (
                entering,
                first_input,
                stacked,
                highest,
                totals,
                mix_rounded,
                middle,
                second_input,
                hidden_pre,
                activated,
            ) = saved[layer_index * micro_count + batch_index]
            incoming = gradients[batch_index]
            grad_down = spread_grad(incoming.astype(jnp.bfloat16))
            down_part = jnp.einsum(
                "rf,rd->fd", activated, grad_down, preferred_element_type=jnp.float32
            )
            grad_act = lax.dot_general(
                grad_down, down_weight, (((1,), (1,)), ((), ())), preferred_element_type=jnp.float32
            )
            pulled = jax.vjp(gelu_exact, hidden_pre)
            grad_pre = pulled[1](grad_act)[0].astype(jnp.bfloat16)
            up_part = jnp.einsum(
                "rd,rf->df", second_input, grad_pre, preferred_element_type=jnp.float32
            )
            grad_norm_two = return_rows(grad_pre, up_weight)
            normed_two, inverse_two = normalize(middle)
            gain_two_part = jnp.sum(grad_norm_two * normed_two, axis=0)
            incoming = incoming + norm_back(grad_norm_two, gain_second, normed_two, inverse_two)
            grad_branch = spread_grad(incoming.astype(jnp.bfloat16))
            out_part = jnp.einsum(
                "rk,rd->kd", mix_rounded, grad_branch, preferred_element_type=jnp.float32
            )
            grad_mix = lax.dot_general(
                grad_branch,
                out_weight,
                (((1,), (1,)), ((), ())),
                preferred_element_type=jnp.float32,
            )
            grad_mix = grad_mix.astype(jnp.bfloat16).reshape(grad_mix.shape[0], -1, HD)
            grad_triple = attend_back(stacked, visibility[batch_index], highest, totals, grad_mix)
            flat_triple = grad_triple.reshape(grad_triple.shape[0], 3, -1)
            qkv_part = jnp.einsum(
                "rd,rcn->dcn", first_input, flat_triple, preferred_element_type=jnp.float32
            )
            grad_norm_one = return_rows(
                flat_triple.reshape(flat_triple.shape[0], -1),
                qkv_weight.reshape(qkv_weight.shape[0], -1),
            )
            normed, inverse = normalize(entering)
            gain_one_part = jnp.sum(grad_norm_one * normed, axis=0)
            incoming = incoming + norm_back(grad_norm_one, gain_first, normed, inverse)
            gradients[batch_index] = incoming
            gain_parts[layer_index] = gain_parts[layer_index] + jnp.stack(
                [gain_one_part, gain_two_part]
            )
            pieces = (qkv_part, out_part, up_part, down_part)
            if summed is None:
                summed = pieces
            else:
                summed = tuple((older + newer for older, newer in zip(summed, pieces)))
        summed = reduce_grads(summed)
        weight_results[layer_index] = summed
    gain_flat = jnp.stack(gain_parts).reshape(-1)
    gain_result = lax.psum_scatter(gain_flat, ("dp", "tensor"), scatter_dimension=0, tiled=True)
    layer_out = jnp.stack(residual)
    input_grad = jnp.stack(gradients)
    qkv_grad = jnp.stack([weight_results[0][0]])
    out_grad = jnp.stack([weight_results[0][1]])
    up_grad = jnp.stack([weight_results[0][2]])
    down_grad = jnp.stack([weight_results[0][3]])
    return (layer_out, input_grad, gain_result, qkv_grad, out_grad, up_grad, down_grad)


def fits(mesh, tokens, w_qkv):
    dp_size, depth = mesh.shape["dp"], mesh.shape["tensor"]
    columns = dp_size // 2
    return (
        depth == 4
        and dp_size >= 4
        and columns & (columns - 1) == 0
        and D == dp_size * 2 * HALF
        and tokens.shape[0] == 2
        and tokens.shape[1] == dp_size * depth * TILE
        and w_qkv.shape[0] == 1
    )


def solution(mesh):
    def run(tokens, cotangent, lengths, padding, ln_gain, w_qkv, *rest):
        one_block = fits(mesh, tokens, w_qkv)
        program = functools.partial(block_body, mesh) if one_block else body
        return jax.shard_map(
            program,
            mesh=mesh,
            in_specs=(
                P(None, ("dp", "tensor"), None),
                P(None, ("dp", "tensor"), None),
                P(None, "dp", None),
                P(None, "dp"),
                P(None, None, "dp"),
                P(None, "dp", None, "tensor"),
                P(None, "tensor", "dp"),
                P(None, "dp", "tensor"),
                P(None, "tensor", "dp"),
            ),
            out_specs=(
                P(None, ("dp", "tensor"), None),
                P(None, ("dp", "tensor"), None),
                P(("dp", "tensor")),
                P(None, "dp", None, "tensor"),
                P(None, "tensor", "dp"),
                P(None, "dp", "tensor"),
                P(None, "tensor", "dp"),
            ),
            check_vma=False,
        )(tokens, cotangent, lengths, padding, ln_gain, w_qkv, *rest)

    return run
```
